32 devices in a mesh: shard: 2 (over x), ctx: 4 (over z), tp: 4 (over y, core).
Axes of the slice: x: 2, y: 2, z: 4, core: 2. Of those that a mesh axis runs over, the one named last changes fastest.
Arguments:
- hidden_in: bfloat16 [8, 1024, 768], P('shard', 'ctx'), may hold values from -6 to 6
- token_type: int32 [8, 1024], P('shard', 'ctx'), may hold values 0 or 1
- segment: int32 [8, 1024], P('shard', 'ctx'), may hold values from 0 to 17, as said below
- query_weight: bfloat16 [4, 768, 768], P(None, 'shard', 'tp'), may hold values from -0.21875 to 0.21875
- key_value_weight: bfloat16 [2, 768, 768], P(None, 'shard', 'tp'), may hold values from -0.21875 to 0.21875
- query_bias: float32 [4, 768], P(None, 'tp'), may hold values from -1.75 to 1.75
- value_bias: float32 [768], P('tp'), may hold values from -1.75 to 1.75
- out_weight: bfloat16 [768, 768], P('tp', 'shard'), may hold values from -1.75 to 1.75
- out_bias: float32 [768], replicated, may hold values from -1.75 to 1.75
- norm1_gain: float32 [768], replicated, may hold values from 0.5 to 1.5
- norm1_bias: float32 [768], replicated, may hold values from -1.75 to 1.75
- up_weight: bfloat16 [768, 3072], P('shard', 'tp'), may hold values from -0.21875 to 0.21875
- up_bias: float32 [3072], P('tp'), may hold values from -1.75 to 1.75
- down_weight: bfloat16 [3072, 768], P('tp', 'shard'), may hold values from -0.109375 to 0.109375
- down_bias: float32 [768], replicated, may hold values from -1.75 to 1.75
- norm2_gain: float32 [768], replicated, may hold values from 0.5 to 1.5
- norm2_bias: float32 [768], replicated, may hold values from -1.75 to 1.75
- out_grad: bfloat16 [8, 1024, 768], P('shard', 'ctx'), may hold values from -6 to 6
Outputs:
- hidden_out: bfloat16 [8, 1024, 768], P('shard', 'ctx')
- in_grad: float32 [8, 1024, 768], P('shard', 'ctx')
- query_weight_grad: float32 [4, 768, 768], P(None, 'shard', 'tp')
- key_value_weight_grad: float32 [2, 768, 768], P(None, 'shard', 'tp')
- query_bias_grad: float32 [4, 768], P(None, 'tp')
- value_bias_grad: float32 [768], P('tp')
- out_weight_grad: float32 [768, 768], P('tp', 'shard')
- out_bias_grad: float32 [768], replicated
- norm1_gain_grad: float32 [768], replicated
- norm1_bias_grad: float32 [768], replicated
- up_weight_grad: float32 [768, 3072], P('shard', 'tp')
- up_bias_grad: float32 [3072], P('tp')
- down_weight_grad: float32 [3072, 768], P('tp', 'shard')
- down_bias_grad: float32 [768], replicated
- norm2_gain_grad: float32 [768], replicated
- norm2_bias_grad: float32 [768], replicated
The draws below stay inside these ranges and needn't reach their ends.
Inputs may be any that keep to these rules, and one draw needn't show every extreme that they name: `token_type`: 0 marks a word, 1 an entity. `segment`: within each sequence the documents are numbered 1, 2, 3 in order, each holds 60 to 800 consecutive positions, and the positions after the last document are 0.
All inputs are finite; a program needn't handle non-finite values. No bound on the sum of `token_type` on one device may be relied on, other than what follows from the above.
Results may differ from the reference program's by a relative error of at most 0.02.
Values may be sent and summed in bfloat16 or wider, within the bound.
A program may use at most 128 MiB of HBM per device.

```python
import jax
import jax.numpy as jnp
from jax import lax

D = 768
HEADS = 12
HEAD = 64
FF = 3072
LEN = 1024
DOC_MIN = 60
DOC_MAX = 800
SEQS = 8


def draw_segment(key, part):
    doc_lengths = jax.random.randint(jax.random.fold_in(key, 11), (SEQS, LEN // DOC_MIN + 1), DOC_MIN, DOC_MAX + 1)
    densest = jax.random.randint(jax.random.fold_in(key, 23), (), 0, SEQS)
    rows = jnp.arange(SEQS)[:, None]
    doc_lengths = jnp.where(rows == densest, DOC_MIN, doc_lengths)
    doc_ends = jnp.cumsum(doc_lengths, axis=1)
    position = jnp.arange(LEN)
    passed = jnp.sum((doc_ends[:, None, :] <= position[None, :, None]).astype(jnp.int32), axis=2)
    filled = jnp.max(jnp.where(doc_ends <= LEN, doc_ends, 0), axis=1)
    return jnp.where(position[None, :] < filled[:, None], passed + 1, 0).astype(jnp.int32)


def set_ends(result, rng, smallest, largest):
    extent = result.shape
    place = [jax.random.randint(jax.random.fold_in(rng, axis), (), 0, extent[axis]) for axis in range(len(extent))]
    result = result.at[tuple(place)].set(smallest)
    longest = extent.index(max(extent))
    place[longest] = (place[longest] + 1) % extent[longest]
    return result.at[tuple(place)].set(largest)


def block_scale(key, extent, cuts, least, largest):
    factor_of, own = 1.0, jax.random.fold_in(key, 6)
    for dim, parts in cuts:
        steps = jnp.exp(jax.random.uniform(jax.random.fold_in(own, dim), (parts,), jnp.float32, least / len(cuts), largest / len(cuts)))
        factor_of = factor_of * jnp.repeat(steps, extent[dim] // parts).reshape([-1 if axis == dim else 1 for axis in range(len(extent))])
    return factor_of


def normal_values(own_key, dims, scale, reach, shards=(), held_as=jnp.bfloat16):
    gain = block_scale(own_key, dims, shards, -0.22, 0.18) if shards else 1.0
    result = jax.random.normal(own_key, dims, jnp.float32) * scale * gain
    return jnp.minimum(jnp.maximum(result, -reach), reach).astype(held_as)


def setup_inputs(seed: int = 0) -> dict:
    keys = jax.random.split(jax.random.key(seed), 19)
    hidden_in = normal_values(keys[0], (SEQS, LEN, D), 1.0, 6.0, ((0, 2), (1, 4)))
    token_type = set_ends((jax.random.randint(keys[1], (SEQS, LEN), 0, 4) < 1).astype(jnp.int32), jax.random.fold_in(keys[1], 1), 0, 1)
    segment = draw_segment(jax.random.fold_in(keys[18], 71), 0)
    query_weight = normal_values(keys[3], (4, D, D), D ** -0.5, 0.21875, ((1, 2), (2, 4)))
    key_value_weight = normal_values(keys[4], (2, D, D), D ** -0.5, 0.21875, ((1, 2), (2, 4)))
    query_bias = normal_values(keys[5], (4, D), 0.3, 1.75, ((1, 4),), jnp.float32)
    value_bias = normal_values(keys[6], (D,), 0.3, 1.75, ((0, 4),), jnp.float32)
    out_weight = normal_values(keys[7], (D, D), (max(D // 64, 1)) ** -0.5, 1.75, ((0, 4), (1, 2)))
    out_bias = normal_values(keys[8], (D,), 0.3, 1.75, (), jnp.float32)
    norm1_gain = jnp.clip(1.0 + 0.1 * jax.random.normal(keys[9], (D,), jnp.float32), 0.5, 1.5)
    norm1_bias = normal_values(keys[10], (D,), 0.3, 1.75, (), jnp.float32)
    up_weight = normal_values(keys[11], (D, FF), D ** -0.5, 0.21875, ((0, 2), (1, 4)))
    up_bias = normal_values(keys[12], (FF,), 0.3, 1.75, ((0, 4),), jnp.float32)
    down_weight = normal_values(keys[13], (FF, D), FF ** -0.5, 0.109375, ((0, 4), (1, 2)))
    down_bias = normal_values(keys[14], (D,), 0.3, 1.75, (), jnp.float32)
    norm2_gain = jnp.clip(1.0 + 0.1 * jax.random.normal(keys[15], (D,), jnp.float32), 0.5, 1.5)
    norm2_bias = normal_values(keys[16], (D,), 0.3, 1.75, (), jnp.float32)
    out_grad = normal_values(keys[17], (SEQS, LEN, D), 1.0, 6.0, ((0, 2), (1, 4)))
    return dict(hidden_in=hidden_in, token_type=token_type, segment=segment, query_weight=query_weight, key_value_weight=key_value_weight, query_bias=query_bias, value_bias=value_bias, out_weight=out_weight, out_bias=out_bias, norm1_gain=norm1_gain, norm1_bias=norm1_bias, up_weight=up_weight, up_bias=up_bias, down_weight=down_weight, down_bias=down_bias, norm2_gain=norm2_gain, norm2_bias=norm2_bias, out_grad=out_grad)


@jax.custom_vjp
def low(v):
    return lax.optimization_barrier(v.astype(jnp.bfloat16)).astype(jnp.float32)

@jax.custom_vjp
def low_back(v):
    return v

def low_keep(v):
    return (low(v), None)

def low_pass(kept, grad):
    return (grad,)

def back_keep(v):
    return (v, None)

def back_low(kept, grad):
    return (low(grad),)
low.defvjp(low_keep, low_pass)
low_back.defvjp(back_keep, back_low)
eps_norm = 1e-05
big_neg = -1e+30
highest = lax.Precision.HIGHEST

def product(left, right):
    return jnp.dot(left, right, precision=highest)

def layer_norm(values, gain_vec, bias_vec):
    average = lax.optimization_barrier(jnp.mean(values, axis=-1, keepdims=True))
    centred = values - average
    variance = lax.optimization_barrier(jnp.mean(centred * centred, axis=-1, keepdims=True))
    return centred * lax.rsqrt(variance + eps_norm) * gain_vec + bias_vec

def layer_block(params, inputs, token_kinds, labels):
    w_query, b_query, w_keyval, b_value, w_out, b_out, gain_one, shift_one, w_up, b_up, w_down, b_down, gain_two, shift_two = params
    group_size = inputs.shape[0]
    row_data = inputs.reshape(-1, D)
    is_word = (token_kinds.reshape(-1) == 0)[:, None]
    query_four = jnp.einsum('rd,kde->kre', row_data, w_query, precision=highest) + b_query[:, None, :]
    chosen = jnp.stack([jnp.where(is_word, query_four[0], query_four[2]), jnp.where(is_word, query_four[1], query_four[3])])
    chosen = low_back(low(chosen))
    key_values = jnp.einsum('rd,kde->kre', row_data, w_keyval, precision=highest)
    key_values = key_values + jnp.stack([jnp.zeros_like(b_value), b_value])[:, None, :]
    key_values = low_back(low(key_values))

    def split_heads(values):
        return values.reshape(group_size, LEN, HEADS, HEAD)
    key_heads = split_heads(key_values[0])
    toward_word = jnp.einsum('gqhc,gkhc->ghqk', split_heads(chosen[0]), key_heads, precision=highest)
    toward_entity = jnp.einsum('gqhc,gkhc->ghqk', split_heads(chosen[1]), key_heads, precision=highest)
    key_word = (token_kinds == 0)[:, None, None, :]
    scores = low_back(jnp.where(key_word, toward_word, toward_entity) * HEAD ** (-0.5))
    allowed = (labels[:, None, :, None] == labels[:, None, None, :]) & (labels[:, None, None, :] > 0)
    row_max = lax.optimization_barrier(jnp.max(jnp.where(allowed, scores, big_neg), axis=-1, keepdims=True))
    exponent = jnp.exp(jnp.where(allowed, scores - row_max, big_neg))
    denominator = jnp.maximum(lax.optimization_barrier(jnp.sum(exponent, axis=-1, keepdims=True)), 1.0)
    probability = low(exponent / denominator)
    context = jnp.einsum('ghqk,gkhc->gqhc', probability, split_heads(key_values[1]), precision=highest)
    context = low_back(low(context.reshape(-1, D)))
    attention = low_back(product(context, w_out) + b_out)
    first_out = layer_norm(row_data + attention, gain_one, shift_one)
    up_value = low_back(product(low(first_out), w_up) + b_up)
    active = low_back(low(jax.nn.gelu(up_value, approximate=False)))
    feed_out = low_back(product(active, w_down) + b_down)
    return layer_norm(first_out + feed_out, gain_two, shift_two).reshape(inputs.shape)

def widen(values):
    return values.astype(jnp.float32)

def reference(hidden_in, token_type, segment, query_weight, key_value_weight, query_bias, value_bias, out_weight, out_bias, norm1_gain, norm1_bias, up_weight, up_bias, down_weight, down_bias, norm2_gain, norm2_bias, out_grad):
    params = (widen(query_weight), query_bias, widen(key_value_weight), value_bias, widen(out_weight), out_bias, norm1_gain, norm1_bias, widen(up_weight), up_bias, widen(down_weight), down_bias, norm2_gain, norm2_bias)
    groups = SEQS // 2
    inputs = widen(hidden_in).reshape(groups, 2, LEN, D)
    token_kinds = token_type.reshape(groups, 2, LEN)
    labels = segment.reshape(groups, 2, LEN)

    def forward(weights, batch_data):

        def one_group(pieces):
            return jax.checkpoint(layer_block)(weights, pieces[0], pieces[1], pieces[2])
        return lax.map(one_group, (batch_data, token_kinds, labels))
    outputs, pull_back = jax.vjp(forward, params, inputs)
    weight_grads, input_grad = pull_back(widen(out_grad).reshape(groups, 2, LEN, D))
    return (outputs.reshape(SEQS, LEN, D).astype(jnp.bfloat16), input_grad.reshape(SEQS, LEN, D), weight_grads[0], weight_grads[2], weight_grads[1], weight_grads[3], weight_grads[4], weight_grads[5], weight_grads[6], weight_grads[7], weight_grads[8], weight_grads[9], weight_grads[10], weight_grads[11], weight_grads[12], weight_grads[13])
```

```python
import functools

import jax
import jax.numpy as jnp
from jax import lax
from jax.experimental import pallas as pl
from jax.experimental.pallas import tpu as pltpu
from jax.sharding import PartitionSpec as P

BF = jnp.bfloat16
F32 = jnp.float32
HEAD = 64
EPS = 1e-05
MASKED = -1e30
ROOT_HALF = 0.7071067811865476
INV_ROOT_TWO_PI = 0.3989422804014327
VMEM_LIMIT = 66 * 1024 * 1000
MESH = pl.DeviceIdType.MESH
DMA = pltpu.SemaphoreType.DMA


def nn(left, right):
    return lax.dot_general(left, right, (((1,), (0,)), ((), ())), preferred_element_type=F32)


def nt(left, right):
    return lax.dot_general(left, right, (((1,), (1,)), ((), ())), preferred_element_type=F32)


def tn(left, right):
    return lax.dot_general(left, right, (((0,), (0,)), ((), ())), preferred_element_type=F32)


def remote(src, dst, send_sem, recv_sem, peer):
    return pltpu.make_async_remote_copy(
        src_ref=src,
        dst_ref=dst,
        send_sem=send_sem,
        recv_sem=recv_sem,
        device_id=peer,
        device_id_type=MESH,
    )


def greet(peers):
    barrier = pltpu.get_barrier_semaphore()
    for peer in peers:
        pl.semaphore_signal(barrier, inc=1, device_id=peer, device_id_type=MESH)
    pl.semaphore_wait(barrier, len(peers))


class Place:
    def __init__(self, ns, nc):
        self.s = lax.axis_index("shard")
        self.c = lax.axis_index("ctx")
        self.t = lax.axis_index("tp")
        self.core = lax.rem(self.t, 2)
        self.y = self.t // 2
        self.mate_t = self.t + 1 - 2 * self.core
        self.ymate_t = lax.rem(self.t + 2, 4)
        self.mate = {"tp": self.mate_t}
        self.ymate = {"tp": self.ymate_t}
        self.zpeers = [{"ctx": lax.rem(self.c + k, nc)} for k in range(1, nc)]
        self.xpeers = [{"shard": lax.rem(self.s + r, ns)} for r in range(1, ns)]


class TpGather:
    def __init__(self, place, buf, sems):
        self.p, self.buf = place, buf
        self.ys, self.yr, self.ks, self.kr, self.fs, self.fr = sems

    def _y(self, b, i, src):
        p = self.p
        return remote(src, self.buf.at[b, p.t], self.ys.at[i], self.yr.at[i], p.ymate)

    def _k(self, b, i, src):
        p = self.p
        return remote(src, self.buf.at[b, p.t], self.ks.at[i], self.kr.at[i], p.mate)

    def _f(self, b, i):
        p = self.p
        piece = self.buf.at[b, p.ymate_t]
        return remote(piece, piece, self.fs.at[i], self.fr.at[i], p.mate)

    def send(self, b, i, src=None):
        src = self.buf.at[b, self.p.t] if src is None else src
        self._y(b, i, src).start()
        self._k(b, i, src).start()

    def forward(self, b, i):
        p = self.p
        piece = self.buf.at[b, p.ymate_t]
        remote(piece, piece, self.ys.at[i], self.yr.at[i], p.ymate).wait_recv()
        self._f(b, i).start()

    def arrive(self, b, i):
        p = self.p
        piece = self.buf.at[b, p.mate_t]
        remote(piece, piece, self.ks.at[i], self.kr.at[i], p.mate).wait_recv()
        piece = self.buf.at[b, lax.rem(p.mate_t + 2, 4)]
        remote(piece, piece, self.fs.at[i], self.fr.at[i], p.mate).wait_recv()

    def drain(self, b, i, src=None):
        src = self.buf.at[b, self.p.t] if src is None else src
        self._y(b, i, src).wait_send()
        self._k(b, i, src).wait_send()
        self._f(b, i).wait_send()


class TpReduce:
    def __init__(self, place, terms, from_mate, staged, from_y, sems):
        self.p, self.terms, self.from_mate, self.staged, self.from_y = (
            place,
            terms,
            from_mate,
            staged,
            from_y,
        )
        self.ks, self.kr, self.ys, self.yr = sems

    def _k(self, b):
        p = self.p
        return remote(
            self.terms.at[b, :, 1 - p.core],
            self.from_mate.at[b],
            self.ks.at[b],
            self.kr.at[b],
            p.mate,
        )

    def _y(self, b):
        return remote(
            self.staged.at[b], self.from_y.at[b], self.ys.at[b], self.yr.at[b], self.p.ymate
        )

    def send(self, b):
        self._k(b).start()

    def across(self, b):
        p = self.p
        self._k(b).wait_recv()
        other = 1 - p.y
        self.staged[b] = (
            self.terms[b, other, p.core].astype(F32) + self.from_mate[b, other].astype(F32)
        ).astype(BF)
        self._y(b).start()

    def result(self, b):
        p = self.p
        self._y(b).wait_recv()
        return (
            self.terms[b, p.y, p.core].astype(F32)
            + self.from_mate[b, p.y].astype(F32)
            + self.from_y[b].astype(F32)
        )

    def drain(self, b):
        self._k(b).wait_send()
        self._y(b).wait_send()


def column(row, width=128):
    return jnp.broadcast_to(row, (width, row.shape[-1])).T


def project_kernel(
    ns, nc, x_ref, code_ref, w_ref, bias_ref,
    xf_ref, q_ref, kv_ref, codef_ref, wf_ref,
    local, zs, zr, ds, dr, ws, wr, *tp_sems,
):
    p = Place(ns, nc)
    piece = x_ref.shape[1] // 4
    greet([p.mate, p.ymate] + p.zpeers + p.xpeers)
    heads = w_ref.shape[0] - 1

    def weight(h, r):
        return remote(
            w_ref.at[h], wf_ref.at[h, p.s], ws.at[h, r], wr.at[h, r], p.xpeers[r]
        )

    for h in range(heads + 1):
        for r in range(ns - 1):
            weight(h, r).start()
    mine = pl.ds(p.t * piece, piece)

    def x_send(k):
        peer = p.zpeers[k]
        return remote(
            x_ref.at[peer["ctx"], mine], xf_ref.at[p.c, p.t], zs.at[k], zr.at[k], peer
        )

    def code_send(k):
        peer = p.zpeers[k]
        return remote(code_ref.at[peer["ctx"]], codef_ref.at[p.c], ds.at[k], dr.at[k], peer)

    for k in range(nc - 1):
        x_send(k).start()
    for k in range(nc - 1):
        code_send(k).start()
    own = x_ref.at[p.c, mine]
    copies = [
        pltpu.make_async_copy(own, xf_ref.at[p.c, p.t], local.at[0]),
        pltpu.make_async_copy(code_ref.at[p.c], codef_ref.at[p.c], local.at[1]),
        pltpu.make_async_copy(w_ref, wf_ref.at[:, p.s], local.at[2]),
    ]
    for copy in copies:
        copy.start()
    gather = TpGather(p, xf_ref, tp_sems)
    gather.send(p.c, 0, own)
    blocks = [lax.rem(p.c + nc - k, nc) for k in range(nc)]
    for k in range(1, nc):
        landed = xf_ref.at[blocks[k], p.t]
        remote(landed, landed, zs.at[k - 1], zr.at[k - 1], p.zpeers[k - 1]).wait_recv()
        gather.send(blocks[k], k)
        gather.forward(blocks[k - 1], k - 1)
    gather.forward(blocks[nc - 1], nc - 1)
    for k in range(nc):
        gather.arrive(blocks[k], k)
    for k in range(nc - 1):
        landed = codef_ref.at[blocks[k + 1]]
        remote(landed, landed, ds.at[k], dr.at[k], p.zpeers[k]).wait_recv()
    for copy in copies:
        copy.wait()
    width = xf_ref.shape[-1]
    rows = 4 * piece
    for h in range(heads):
        for r in range(ns - 1):
            landed = wf_ref.at[h, lax.rem(p.s + ns - 1 - r, ns)]
            remote(landed, landed, ws.at[h, r], wr.at[h, r], p.xpeers[r]).wait_recv()

        def project(b, carry):
            x = xf_ref[b].reshape(rows, width)
            out = nn(x, wf_ref[h].reshape(width, 384)) + bias_ref[h]
            entity = column(codef_ref[b]) < 0.0
            at = pl.ds(pl.multiple_of(b * rows, rows), rows)
            chosen = jnp.where(entity, out[:, 128:256], out[:, 0:128])
            q_ref[h, at] = (chosen * HEAD ** (-0.5)).astype(BF)
            kv_ref[h, at] = out[:, 256:384].astype(BF)
            return carry

        lax.fori_loop(0, nc, project, 0)
    for r in range(ns - 1):
        landed = wf_ref.at[heads, lax.rem(p.s + ns - 1 - r, ns)]
        remote(landed, landed, ws.at[heads, r], wr.at[heads, r], p.xpeers[r]).wait_recv()
    for h in range(heads + 1):
        for r in range(ns - 1):
            weight(h, r).wait_send()
    for k in range(nc - 1):
        x_send(k).wait_send()
        code_send(k).wait_send()
    gather.drain(p.c, 0, own)
    for k in range(1, nc):
        gather.drain(blocks[k], k)


def attend_kernel(q_ref, kv_ref, code_ref, e_ref, ctx_ref, inv_ref, kcat, vt, segcol):
    h, b = pl.program_id(0), pl.program_id(1)
    length = kv_ref.shape[1]
    nblk, rows = code_ref.shape[0], code_ref.shape[2]

    @pl.when((h == 0) & (b == 0))
    def _():
        for j in range(nblk):
            col = jnp.abs(column(code_ref[j]))
            segcol[j * rows : (j + 1) * rows] = jnp.where(col == 0.0, -1.0, col)

    @pl.when(b == 0)
    def _():
        low_half = lax.broadcasted_iota(jnp.int32, (rows, 128), 1) < HEAD
        for j in range(nblk):
            at = slice(j * rows, (j + 1) * rows)
            entity = column(code_ref[j]) < 0.0
            kv = kv_ref[0, at].astype(F32)
            turned = pltpu.roll(kv, HEAD, 1)
            keep = jnp.where(low_half, kv, turned)
            kcat[at] = jnp.where(low_half == entity, 0.0, keep).astype(BF)
            vt[:, at] = jnp.where(low_half, 0.0, kv).T.astype(BF)

    scores = nt(kcat[...], q_ref[0])
    segment = jnp.abs(code_ref[b])
    col = segcol[...]
    allowed = jnp.concatenate([col] * (rows // 128), axis=1) == segment
    scores = jnp.where(allowed, scores, MASKED)
    top = jnp.max(scores, axis=0, keepdims=True)
    top = jnp.where(top == MASKED, 0.0, top)
    exponent = jnp.exp(scores - top)
    inverse = 1.0 / jnp.maximum(jnp.sum(exponent, axis=0, keepdims=True), 1.0)
    exponent = exponent.astype(BF)
    e_ref[0] = exponent
    inv_ref[0, 0] = inverse
    ctx_ref[...] = (nn(vt[...], exponent) * inverse).T.astype(BF)


def spread(values):
    average = jnp.mean(values, axis=-1, keepdims=True)
    centred = values - average
    inverse = lax.rsqrt(jnp.mean(centred * centred, axis=-1, keepdims=True) + EPS)
    return centred * inverse, inverse


def unspread(upstream, normed, inverse, gain):
    scaled = upstream * gain
    first = jnp.mean(scaled, axis=-1, keepdims=True)
    second = jnp.mean(scaled * normed, axis=-1, keepdims=True)
    return inverse * (scaled - first - normed * second)


def total(values):
    return jnp.sum(values, axis=0, keepdims=True)


SKEWS_C = (0, 1, 3, 4, 5, 6, 8, 9, 10, 11, 13, 14, 15)


def feed_kernel(
    ns, nc, ctx_ref, wo_ref, xf_ref, og_ref, wu_ref, wd_ref, vec_ref,
    ga_ref, hid_ref, gfi_ref, dff_ref, small_ref,
    wuf, wdf, ogo, hsend,
    t0, m0, s0, y0, t1, m1, s1, y1, t2, m2, s2, y2,
    low, gf, active, slope, gup, fo, fh, fi, gs, dst, xr,
    local, ws, wr, os, orr, hs, hr, xs, xrs, *tp_sems,
):
    p = Place(ns, nc)
    piece, width = xf_ref.shape[2:]
    rows = 4 * piece
    greet([p.mate, p.ymate] + p.zpeers + p.xpeers)
    weights = ((wu_ref, wuf), (wd_ref, wdf))

    def weight(a, r):
        src, dst = weights[a]
        return remote(src, dst.at[p.s], ws.at[a, r], wr.at[a, r], p.xpeers[r])

    for a in range(2):
        for r in range(ns - 1):
            weight(a, r).start()
    mine = pl.ds(p.t * piece, piece)

    def og_send(k):
        peer = p.zpeers[k]
        return remote(og_ref.at[peer["ctx"], mine], ogo.at[p.c], os.at[k], orr.at[k], peer)

    for k in range(nc - 1):
        og_send(k).start()
    copies = [
        pltpu.make_async_copy(og_ref.at[p.c, mine], ogo.at[p.c], local.at[0]),
        pltpu.make_async_copy(wu_ref, wuf.at[p.s], local.at[1]),
        pltpu.make_async_copy(wd_ref, wdf.at[p.s], local.at[2]),
    ]
    for copy in copies:
        copy.start()
    small_ref[...] = jnp.zeros_like(small_ref)

    sums = [
        TpReduce(p, *bufs, [tp_sems[j].at[i] for j in range(4)])
        for i, bufs in enumerate(((t0, m0, s0, y0), (t1, m1, s1, y1), (t2, m2, s2, y2)))
    ]
    shares = [
        TpGather(p, buf, [tp_sems[4 + j].at[i] for j in range(6)])
        for i, buf in enumerate((low, gf, ga_ref))
    ]
    out_bias, gain1, bias1, up_bias, down_bias, gain2, bias2 = (
        vec_ref[i : i + 1] for i in range(7)
    )

    def put(terms, b, values):
        terms[b] = values.astype(BF).reshape(2, 2, piece, width)

    def add_small(row, values):
        small_ref[row : row + 1] += total(values)

    def out_project(b):
        put(t0, b, nt(ctx_ref[b], wo_ref[...]))
        sums[0].send(b)

    def norm_one(b):
        h = xf_ref[b, p.t].astype(F32) + (sums[0].result(b) + out_bias)
        normed, inverse = spread(h)
        first = normed * gain1 + bias1
        fo[b] = first
        fh[b] = normed
        fi[b] = inverse
        low[b, p.t] = first.astype(BF)
        shares[0].send(b, b)

    def feed_forward(b):
        @pl.when(b == 0)
        def _():
            for a in range(2):
                for r in range(ns - 1):
                    landed = weights[a][1].at[lax.rem(p.s + ns - 1 - r, ns)]
                    remote(landed, landed, ws.at[a, r], wr.at[a, r], p.xpeers[r]).wait_recv()
            for copy in copies[1:]:
                copy.wait()

        shares[0].arrive(b, b)
        up = nn(low[b].reshape(rows, width), wuf[...].reshape(width, -1)) + up_bias
        cdf = 0.5 * (1.0 + lax.erf(up * ROOT_HALF))
        act = (up * cdf).astype(BF)
        active[b] = act
        slope[b] = cdf + up * (jnp.exp(-0.5 * up * up) * INV_ROOT_TWO_PI)
        put(t1, b, nt(act, wdf[...].reshape(width, -1)))
        sums[1].send(b)

    def hid_send(b):
        return remote(hsend.at[b], hid_ref.at[p.c], hs.at[b], hr.at[p.c], {"ctx": b})

    def norm_two(b):
        @pl.when(b == 0)
        def _():
            for k in range(nc - 1):
                landed = ogo.at[lax.rem(p.c + nc - 1 - k, nc)]
                remote(landed, landed, os.at[k], orr.at[k], p.zpeers[k]).wait_recv()
            copies[0].wait()

        normed, inverse = spread(fo[b] + (sums[1].result(b) + down_bias))
        hsend[b] = (normed * gain2 + bias2).astype(BF)

        upstream = ogo[b].astype(F32)
        add_small(2, upstream * normed)
        add_small(3, upstream)
        grad = unspread(upstream, normed, inverse, gain2)
        gs[b] = grad
        grad = grad.astype(BF)
        gf[b, p.t] = grad
        add_small(5, grad.astype(F32))
        shares[1].send(b, b)

        @pl.when(b != p.c)
        def _():
            hid_send(b).start()

        @pl.when(b == p.c)
        def _():
            pltpu.make_async_copy(hsend.at[b], hid_ref.at[p.c], local.at[3]).start()

    def feed_back(b):
        shares[1].arrive(b, b)
        grad = nn(gf[b].reshape(rows, width), wdf[...].reshape(width, -1))
        grad = (grad.astype(BF).astype(F32) * slope[b]).astype(BF)
        gup[b] = grad
        add_small(6, grad.astype(F32))
        put(t2, b, nt(grad, wuf[...].reshape(width, -1)))
        sums[2].send(b)

    def norm_back(b):
        grad = gs[b] + sums[2].result(b)
        add_small(0, grad * fh[b])
        add_small(1, grad)
        grad = unspread(grad, fh[b], fi[b], gain1)
        gfi_ref[b] = grad
        grad = grad.astype(BF)
        ga_ref[b, p.t] = grad
        add_small(4, grad.astype(F32))
        shares[2].send(b, b)

    stages = (
        out_project,
        sums[0].across,
        norm_one,
        lambda b: shares[0].forward(b, b),
        feed_forward,
        sums[1].across,
        norm_two,
        lambda b: shares[1].forward(b, b),
        feed_back,
        sums[2].across,
        norm_back,
        lambda b: shares[2].forward(b, b),
        lambda b: shares[2].arrive(b, b),
    )

    def grad_send(a, r):
        return remote(
            dst.at[a, p.xpeers[r]["shard"]], xr.at[a, r], xs.at[a, r], xrs.at[a, r], p.xpeers[r]
        )

    def weight_grad(a):
        left = (low, gf)[a][...].reshape(nc * rows, width)
        right = (gup, active)[a][...].reshape(nc * rows, -1)
        dst[a] = tn(left, right).astype(BF).reshape(dst.shape[1:])
        for r in range(ns - 1):
            grad_send(a, r).start()

    def slot(step, carry):
        for skew, stage in zip(SKEWS_C, stages):
            b = step - skew

            @pl.when((b >= 0) & (b < nc))
            def _(stage=stage, b=b):
                stage(b)

        for a in range(2):

            @pl.when(step == SKEWS_C[8] + nc - 1 + a)
            def _(a=a):
                weight_grad(1 - a)

        return carry

    lax.fori_loop(0, SKEWS_C[-1] + nc, slot, 0)
    half = width // 2
    for a in (1, 0):
        grad = dst[a, p.s].astype(F32)
        for r in range(ns - 1):
            grad_send(a, r).wait_recv()
            grad = grad + xr[a, r].astype(F32)
        grad = grad.astype(BF)
        dff_ref[2 * a] = grad[:, :half]
        dff_ref[2 * a + 1] = grad[:, half:]
    for k in range(1, nc):
        src = lax.rem(p.c + k, nc)
        landed = hid_ref.at[src]
        remote(landed, landed, hs.at[src], hr.at[src], p.zpeers[k - 1]).wait_recv()
        hid_send(src).wait_send()
    pltpu.make_async_copy(hsend.at[p.c], hid_ref.at[p.c], local.at[3]).wait()
    for a in range(2):
        for r in range(ns - 1):
            weight(a, r).wait_send()
            grad_send(a, r).wait_send()
    for k in range(nc - 1):
        og_send(k).wait_send()
    for i in range(3):
        for b in range(nc):
            sums[i].drain(b)
            shares[i].drain(b, b)


def attend_back_kernel(
    ga_ref, wf_ref, ctxf_ref, xf_ref, code_ref, e_ref, inv_ref, ctx_ref, q_ref, kv_ref,
    dw_ref, back_ref, qb_ref,
    dctx, kcat, dkey, dval, dqkv, back,
):
    h, b = pl.program_id(0), pl.program_id(1)
    heads = pl.num_programs(0)
    nblk, rows = code_ref.shape[0], code_ref.shape[2]
    width = xf_ref.shape[1]

    @pl.when((h == 0) & (b == 0))
    def _():
        out = wf_ref[3].reshape(width, 384)
        for i in range(3):
            dctx[i] = nn(ga_ref[...], out[:, i * 128 : (i + 1) * 128]).astype(BF)
        dw_ref[3] = tn(ga_ref[...], ctxf_ref[...]).astype(BF)
        back[...] = jnp.zeros_like(back)

    low_half = lax.broadcasted_iota(jnp.int32, (rows, 128), 1) < HEAD

    @pl.when(b == 0)
    def _():
        for j in range(nblk):
            at = slice(j * rows, (j + 1) * rows)
            entity = column(code_ref[j]) < 0.0
            kv = kv_ref[0, at].astype(F32)
            keep = jnp.where(low_half, kv, pltpu.roll(kv, HEAD, 1))
            kcat[at] = jnp.where(low_half == entity, 0.0, keep).astype(BF)
        dkey[...] = jnp.zeros_like(dkey)
        dval[...] = jnp.zeros_like(dval)

    at = pl.ds(pl.multiple_of(b * rows, rows), rows)
    grad_ctx = dctx[h, at].astype(F32).T * inv_ref[0, 0]
    row_dot = jnp.sum(grad_ctx * ctx_ref[...].astype(F32).T, axis=0, keepdims=True)
    grad_ctx = grad_ctx.astype(BF)
    weight = e_ref[0]
    grad = nn(kv_ref[0], grad_ctx)
    grad = (weight.astype(F32) * (grad - row_dot)).astype(BF)
    dval[...] += nt(weight, grad_ctx)
    dkey[...] += nn(grad, q_ref[0])
    grad_q = tn(kcat[...], grad).T * HEAD ** (-0.5)
    entity = column(code_ref[b]) < 0.0
    dqkv[at, 0:128] = jnp.where(entity, 0.0, grad_q).astype(BF)
    dqkv[at, 128:256] = jnp.where(entity, grad_q, 0.0).astype(BF)

    @pl.when(b == nblk - 1)
    def _():
        for j in range(nblk):
            part = slice(j * rows, (j + 1) * rows)
            entity = column(code_ref[j]) < 0.0
            grad_k = dkey[part]
            grad_k = jnp.where(entity, pltpu.roll(grad_k, HEAD, 1), grad_k)
            dqkv[part, 256:384] = jnp.where(low_half, grad_k, dval[part]).astype(BF)
        grads = dqkv[...]
        qb_ref[h] = total(grads.astype(F32))
        dw_ref[h] = tn(xf_ref[...], grads).astype(BF)
        back[...] += nt(grads, wf_ref[h].reshape(width, 384))

        @pl.when(h == heads - 1)
        def _():
            back_ref[...] = back[...].astype(BF)


def finish_kernel(
    ns, nc, back_ref, gfi_ref, hid_ref, dff_ref, dqo_ref, smc_ref, qb_ref,
    ing_ref, hidf_ref, dw_ref, sm_ref,
    m0, s0, y0, ig, zo, zr, zq, zsum, xr, smt, smz, smx,
    local, xs, xrs, z1s, z1r, z2s, z2r, z3s, z3r, z4s, z4r, gs, gr, hl, ss, sr, szs, szr, sxs, sxr,
    *tp_sems,
):
    p = Place(ns, nc)
    piece, width = gfi_ref.shape[1:]
    chunks = dw_ref.shape[0]
    first = dff_ref.shape[0]
    greet([p.mate, p.ymate] + p.zpeers + p.xpeers)

    def x_send(k, r):
        peer = p.xpeers[r]
        return remote(dqo_ref.at[k, peer["shard"]], xr.at[k, r], xs.at[k, r], xrs.at[k, r], peer)

    back_sum = TpReduce(p, back_ref, m0, s0, y0, [tp_sems[j] for j in range(4)])
    for b in range(nc):
        back_sum.send(b)
    for k in range(chunks - first):
        for r in range(ns - 1):
            x_send(k, r).start()
    copies = [
        pltpu.make_async_copy(dff_ref, zo.at[pl.ds(0, first)], local.at[0]),
        pltpu.make_async_copy(hid_ref, hidf_ref.at[:, p.t], local.at[1]),
    ]
    for copy in copies:
        copy.start()
    share_h = TpGather(p, hidf_ref, [tp_sems[4 + j].at[0] for j in range(6)])
    share_g = TpGather(p, ing_ref, [tp_sems[4 + j].at[1] for j in range(6)])

    outer = (p.c == 0) | (p.c == nc - 1)
    inner = (p.c > 0) & (p.c < nc - 1)
    inward = {"ctx": 1 + p.c // 3}
    outward = {"ctx": lax.rem(3 * (p.c + nc - 1), 6)}
    across = {"ctx": lax.rem(2 * nc - 1 - p.c, nc)}

    def to_inner(k):
        return remote(zo.at[k], zr.at[k], z1s.at[k], z1r.at[k], inward)

    def to_owner(k):
        return remote(zsum.at[k], zq.at[k], z2s.at[k], z2r.at[k], across)

    def to_other(k):
        return remote(dw_ref.at[k], dw_ref.at[k], z3s.at[k], z3r.at[k], across)

    def to_outer(k):
        return remote(dw_ref.at[k], dw_ref.at[k], z4s.at[k], z4r.at[k], outward)

    def owns(k):
        return lax.rem(k + p.c, 2) == 1

    def line_start(k):
        @pl.when(k == 0)
        def _():
            copies[0].wait()

        @pl.when(k >= first)
        def _():
            j = k - first
            grad = dqo_ref[j, p.s].astype(F32)
            for r in range(ns - 1):
                x_send(j, r).wait_recv()
                grad = grad + xr[j, r].astype(F32)
            zo[k] = grad.astype(BF)

        @pl.when(outer)
        def _():
            to_inner(k).start()

    def line_in(k):
        @pl.when(inner)
        def _():
            to_inner(k).wait_recv()

            @pl.when(jnp.logical_not(owns(k)))
            def _():
                zsum[k] = (zo[k].astype(F32) + zr[k].astype(F32)).astype(BF)
                to_owner(k).start()

    def line_out(k):
        @pl.when(inner)
        def _():
            @pl.when(owns(k))
            def _():
                to_owner(k).wait_recv()
                dw_ref[k] = (zo[k].astype(F32) + zr[k].astype(F32) + zq[k].astype(F32)).astype(BF)
                to_other(k).start()

            @pl.when(jnp.logical_not(owns(k)))
            def _():
                to_other(k).wait_recv()

            to_outer(k).start()

    at = p.c

    def small_tp(i, peer):
        return remote(smt.at[2 * i], smt.at[2 * i + 1], ss.at[i], sr.at[i], peer)

    shared = lax.broadcasted_iota(jnp.int32, smt.shape[1:], 0) < 6

    def small_fold(i):
        return smt[2 * i] + jnp.where(shared, smt[2 * i + 1], 0.0)

    def small_z(k):
        return remote(smz.at[at], smz.at[at], szs.at[k], szr.at[k], p.zpeers[k])

    def small_x(r):
        return remote(smx.at[p.s], smx.at[p.s], sxs.at[r], sxr.at[r], p.xpeers[r])

    def small_zero():
        smt[0] = jnp.zeros_like(smt[0])
        smt[0, :, 0:width] = smc_ref[...]
        for h in range(qb_ref.shape[0]):
            smt[0, 7:8, h * 384 : (h + 1) * 384] = qb_ref[h]
        small_tp(0, p.mate).start()

    def small_one():
        small_tp(0, p.mate).wait_recv()
        smt[2] = small_fold(0)
        small_tp(1, p.ymate).start()

    def small_two():
        small_tp(1, p.ymate).wait_recv()
        smz[at] = small_fold(1)
        for k in range(nc - 1):
            small_z(k).start()

    def small_three():
        for k in range(nc - 1):
            landed = smz.at[lax.rem(p.c + nc - 1 - k, nc)]
            remote(landed, landed, szs.at[k], szr.at[k], p.zpeers[k]).wait_recv()
        value = smz[0]
        for k in range(1, nc):
            value = value + smz[k]
        smx[p.s] = value
        for r in range(ns - 1):
            small_x(r).start()

    def small_four():
        for r in range(ns - 1):
            landed = smx.at[lax.rem(p.s + ns - 1 - r, ns)]
            remote(landed, landed, sxs.at[r], sxr.at[r], p.xpeers[r]).wait_recv()
        value = smx[0]
        for r in range(1, ns):
            value = value + smx[r]
        sm_ref[...] = value

    def grad_send(b):
        return remote(ig.at[b], ing_ref.at[p.c, p.t], gs.at[b], gr.at[p.c], {"ctx": b})

    def grad_own(b):
        ig[b] = (gfi_ref[b] + back_sum.result(b)).astype(BF)

        @pl.when(b != p.c)
        def _():
            grad_send(b).start()

        @pl.when(b == p.c)
        def _():
            pltpu.make_async_copy(ig.at[b], ing_ref.at[p.c, p.t], hl.at[0]).start()

    order = [lax.rem(p.c + k, nc) for k in range(nc)]

    def grad_share(k):
        q = lax.rem(p.c + k, nc)

        @pl.when(k > 0)
        def _():
            landed = ing_ref.at[q, p.t]
            remote(landed, landed, gs.at[q], gr.at[q], {"ctx": q}).wait_recv()
            share_g.send(q, k)

        @pl.when(k == 0)
        def _():
            pltpu.make_async_copy(ig.at[p.c], ing_ref.at[p.c, p.t], hl.at[0]).wait()
            share_g.send(q, k)

    for b in range(nc):
        share_h.send(b, b, hid_ref.at[b])
    small_zero()
    for k in range(first):
        line_start(k)
    for b in range(nc):
        back_sum.across(b)
    small_one()
    for b in range(nc):
        grad_own(b)
    small_two()
    for k in range(first):
        line_in(k)
    for b in range(nc):
        share_h.forward(b, b)
    for k in range(nc):
        grad_share(k)
    small_three()
    for k in range(first):
        line_out(k)
        line_start(k + first)
    for k in range(nc):
        share_g.forward(order[k], k)
    small_four()
    for k in range(first, chunks):
        line_in(k)
    for k in range(first, chunks):
        line_out(k)
    for b in range(nc):
        share_h.arrive(b, b)
        share_g.arrive(order[b], b)

    def line_end(k, carry):
        @pl.when(outer)
        def _():
            to_outer(k).wait_recv()
            to_inner(k).wait_send()

        @pl.when(inner)
        def _():
            @pl.when(owns(k))
            def _():
                to_other(k).wait_send()

            @pl.when(jnp.logical_not(owns(k)))
            def _():
                to_owner(k).wait_send()

            to_outer(k).wait_send()

        return carry

    lax.fori_loop(0, chunks, line_end, 0)
    copies[1].wait()
    for k in range(chunks - first):
        for r in range(ns - 1):
            x_send(k, r).wait_send()
    for b in range(nc):
        back_sum.drain(b)
        share_h.drain(b, b, hid_ref.at[b])
        share_g.drain(order[b], b)

        @pl.when(b != p.c)
        def _():
            grad_send(b).wait_send()

    small_tp(0, p.mate).wait_send()
    small_tp(1, p.ymate).wait_send()
    for k in range(nc - 1):
        small_z(k).wait_send()
    for r in range(ns - 1):
        small_x(r).wait_send()


def vmem(count):
    return [pl.BlockSpec(memory_space=pltpu.VMEM)] * count


def struct(shape, dtype):
    return jax.ShapeDtypeStruct(shape, dtype)


def params(collective_id=None):
    if collective_id is None:
        return pltpu.CompilerParams(
            vmem_limit_bytes=VMEM_LIMIT, dimension_semantics=("arbitrary", "arbitrary")
        )
    return pltpu.CompilerParams(
        vmem_limit_bytes=VMEM_LIMIT, collective_id=collective_id, has_side_effects=True
    )


TP_GATHER = 6
TP_REDUCE = 4


def per_device(
    hidden_in,
    token_type,
    segment,
    query_weight,
    key_value_weight,
    query_bias,
    value_bias,
    out_weight,
    out_bias,
    norm1_gain,
    norm1_bias,
    up_weight,
    up_bias,
    down_weight,
    down_bias,
    norm2_gain,
    norm2_bias,
    out_grad,
):
    ns, nc = lax.axis_size("shard"), lax.axis_size("ctx")
    seqs, local_len, width = hidden_in.shape
    part = query_weight.shape[2]
    heads = part // HEAD
    shard_rows = query_weight.shape[1]
    ff = up_weight.shape[1]
    piece = local_len // 4
    length = nc * local_len
    assert seqs == nc == 4 and heads == 3 and ff == width
    wide = ns - 1

    code = jnp.where(token_type == 0, segment, -segment).astype(F32).reshape(nc, 1, local_len)
    stacked = jnp.concatenate([query_weight, key_value_weight], axis=0)
    stacked = stacked.reshape(6, shard_rows, heads, HEAD).transpose(2, 1, 0, 3)
    stacked = stacked.reshape(heads, shard_rows, 6 * HEAD)
    out_t = out_weight.T.reshape(shard_rows, heads, 1, HEAD)
    out_t = jnp.pad(out_t, ((0, 0), (0, 0), (1, 0), (0, 0))).reshape(1, shard_rows, 2 * part)
    stacked = jnp.concatenate([stacked, out_t], axis=0)
    bias = jnp.concatenate([query_bias, jnp.zeros((1, part), F32), value_bias[None]], axis=0)
    bias = bias.reshape(6, heads, HEAD).transpose(1, 0, 2).reshape(heads, 1, 6 * HEAD)
    vectors = jnp.stack(
        [out_bias, norm1_gain, norm1_bias, up_bias, down_bias, norm2_gain, norm2_bias, norm2_bias]
    )
    down_t = down_weight.T

    xf, q, kv, code, wf = pl.pallas_call(
        functools.partial(project_kernel, ns, nc),
        out_shape=(
            struct((nc, 4, piece, width), BF),
            struct((heads, length, 128), BF),
            struct((heads, length, 128), BF),
            struct((nc, 1, local_len), F32),
            struct((heads + 1, ns, shard_rows, 384), BF),
        ),
        in_specs=vmem(4),
        out_specs=vmem(5),
        scratch_shapes=[DMA((3,))]
        + [DMA((nc - 1,))] * 4
        + [DMA((heads + 1, wide))] * 2
        + [DMA((nc,))] * TP_GATHER,
        compiler_params=params(0),
        name="project",
    )(hidden_in, code, stacked, bias)

    grid = (heads, nc)
    e_spec = pl.BlockSpec((1, length, local_len), lambda h, b: (h, 0, b))
    inv_spec = pl.BlockSpec((1, 1, 1, local_len), lambda h, b: (h, b, 0, 0))
    ctx_spec = pl.BlockSpec((local_len, 128), lambda h, b: (b, h))
    q_spec = pl.BlockSpec((1, local_len, 128), lambda h, b: (h, b, 0))
    kv_spec = pl.BlockSpec((1, length, 128), lambda h, b: (h, 0, 0))

    def whole(shape):
        return pl.BlockSpec(shape, lambda h, b: (0,) * len(shape))

    e, ctx, inv = pl.pallas_call(
        attend_kernel,
        grid=grid,
        out_shape=(
            struct((heads, length, length), BF),
            struct((length, heads * 128), BF),
            struct((heads, nc, 1, local_len), F32),
        ),
        in_specs=[q_spec, kv_spec, whole((nc, 1, local_len))],
        out_specs=(e_spec, ctx_spec, inv_spec),
        scratch_shapes=[
            pltpu.VMEM((length, 128), BF),
            pltpu.VMEM((128, length), BF),
            pltpu.VMEM((length, 128), F32),
        ],
        compiler_params=params(),
        name="attend",
    )(q, kv, code)

    full = pltpu.VMEM((nc, 4, piece, width), BF)
    own = pltpu.VMEM((nc, piece, width), BF)
    own32 = pltpu.VMEM((nc, piece, width), F32)
    reduce_bufs = [
        pltpu.VMEM((nc, 2, 2, piece, width), BF),
        pltpu.VMEM((nc, 2, piece, width), BF),
        own,
        own,
    ]
    rows_ff = pltpu.VMEM((nc, local_len, ff), BF)
    ga, hid, gfi, dff, small = pl.pallas_call(
        functools.partial(feed_kernel, ns, nc),
        out_shape=(
            struct((nc, 4, piece, width), BF),
            struct((nc, piece, width), BF),
            struct((nc, piece, width), F32),
            struct((4, shard_rows, width // 2), BF),
            struct((8, width), F32),
        ),
        in_specs=vmem(7),
        out_specs=vmem(5),
        scratch_shapes=[
            pltpu.VMEM((ns, shard_rows, ff), BF),
            pltpu.VMEM((ns, shard_rows, ff), BF),
            own,
            own,
        ]
        + reduce_bufs * 3
        + [
            full,
            full,
            rows_ff,
            pltpu.VMEM((nc, local_len, ff), F32),
            rows_ff,
            own32,
            own32,
            pltpu.VMEM((nc, piece, 1), F32),
            own32,
            pltpu.VMEM((2, ns, shard_rows, ff), BF),
            pltpu.VMEM((2, wide, shard_rows, ff), BF),
        ]
        + [DMA((4,))]
        + [DMA((2, wide))] * 2
        + [DMA((nc - 1,))] * 2
        + [DMA((nc,))] * 2
        + [DMA((2, wide))] * 2
        + [DMA((3, nc))] * (TP_REDUCE + TP_GATHER),
        compiler_params=params(1),
        name="feed",
    )(
        ctx.reshape(nc, local_len, heads * 128),
        wf[heads].reshape(width, 384),
        xf,
        out_grad,
        up_weight,
        down_t,
        vectors,
    )

    dqo, back, qb = pl.pallas_call(
        attend_back_kernel,
        grid=grid,
        out_shape=(
            struct((heads + 1, width, 384), BF),
            struct((length, width), BF),
            struct((heads, 1, 384), F32),
        ),
        in_specs=[
            whole((length, width)),
            whole((heads + 1, ns, shard_rows, 384)),
            whole((length, heads * 128)),
            whole((length, width)),
            whole((nc, 1, local_len)),
            e_spec,
            inv_spec,
            ctx_spec,
            q_spec,
            kv_spec,
        ],
        out_specs=(
            whole((heads + 1, width, 384)),
            whole((length, width)),
            whole((heads, 1, 384)),
        ),
        scratch_shapes=[
            pltpu.VMEM((heads, length, 128), BF),
            pltpu.VMEM((length, 128), BF),
            pltpu.VMEM((length, 128), F32),
            pltpu.VMEM((length, 128), F32),
            pltpu.VMEM((length, 384), BF),
            pltpu.VMEM((length, width), F32),
        ],
        compiler_params=params(),
        name="attend_back",
    )(
        ga.reshape(length, width),
        wf,
        ctx,
        xf.reshape(length, width),
        code,
        e,
        inv,
        ctx,
        q,
        kv,
    )

    chunks = 4 + heads + 1
    line = pltpu.VMEM((chunks, shard_rows, 384), BF)
    wide_small = 3 * 384
    ing, hid, dw, small = pl.pallas_call(
        functools.partial(finish_kernel, ns, nc),
        out_shape=(
            struct((nc, 4, piece, width), BF),
            struct((nc, 4, piece, width), BF),
            struct((chunks, shard_rows, 384), BF),
            struct((8, wide_small), F32),
        ),
        in_specs=vmem(7),
        out_specs=vmem(4),
        scratch_shapes=[
            pltpu.VMEM((nc, 2, piece, width), BF),
            own,
            own,
            own,
            line,
            line,
            line,
            line,
            pltpu.VMEM((heads + 1, wide, shard_rows, 384), BF),
            pltpu.VMEM((4, 8, wide_small), F32),
            pltpu.VMEM((nc, 8, wide_small), F32),
            pltpu.VMEM((ns, 8, wide_small), F32),
        ]
        + [DMA((2,))]
        + [DMA((heads + 1, wide))] * 2
        + [DMA((chunks,))] * 8
        + [DMA((nc,))] * 2
        + [DMA((1,))]
        + [DMA((2,))] * 2
        + [DMA((nc - 1,))] * 2
        + [DMA((wide,))] * 2
        + [DMA((nc,))] * TP_REDUCE
        + [DMA((2, nc))] * TP_GATHER,
        compiler_params=params(2),
        name="finish",
    )(
        back.reshape(nc, 2, 2, piece, width),
        gfi,
        hid,
        dff,
        dqo.reshape(heads + 1, ns, shard_rows, 384),
        small,
        qb,
    )

    hidden_out = hid.reshape(nc, local_len, width)
    in_grad = ing.reshape(nc, local_len, width).astype(F32)
    grads = dw.astype(F32)
    up_grad = jnp.concatenate([grads[0], grads[1]], axis=1)
    down_grad = jnp.concatenate([grads[2], grads[3]], axis=1).T
    split = grads[4:7].reshape(heads, shard_rows, 6, HEAD).transpose(2, 1, 0, 3)
    split = split.reshape(6, shard_rows, part)
    out_w = grads[7].reshape(shard_rows, heads, 2, HEAD)[:, :, 1].reshape(shard_rows, part).T
    vec = small[7].reshape(heads, 6, HEAD).transpose(1, 0, 2).reshape(6, part)
    return (
        hidden_out,
        in_grad,
        split[:4],
        split[4:],
        vec[:4],
        vec[5],
        out_w,
        small[4, :width],
        small[0, :width],
        small[1, :width],
        up_grad,
        small[6, :width],
        down_grad,
        small[5, :width],
        small[2, :width],
        small[3, :width],
    )


def solution(mesh):
    in_specs = (
        P("shard", "ctx", None),
        P("shard", "ctx"),
        P("shard", "ctx"),
        P(None, "shard", "tp"),
        P(None, "shard", "tp"),
        P(None, "tp"),
        P("tp"),
        P("tp", "shard"),
        P(),
        P(),
        P(),
        P("shard", "tp"),
        P("tp"),
        P("tp", "shard"),
        P(),
        P(),
        P(),
        P("shard", "ctx", None),
    )
    out_specs = (
        P("shard", "ctx", None),
        P("shard", "ctx", None),
        P(None, "shard", "tp"),
        P(None, "shard", "tp"),
        P(None, "tp"),
        P("tp"),
        P("tp", "shard"),
        P(),
        P(),
        P(),
        P("shard", "tp"),
        P("tp"),
        P("tp", "shard"),
        P(),
        P(),
        P(),
    )
    return jax.shard_map(
        per_device, mesh=mesh, in_specs=in_specs, out_specs=out_specs, check_vma=False
    )
```

```python
import functools

import jax
import jax.numpy as jnp
from jax import lax
from jax.experimental import pallas as pl
from jax.experimental.pallas import tpu as pltpu
from jax.sharding import PartitionSpec as P

BF = jnp.bfloat16
F32 = jnp.float32
HEAD = 64
EPS = 1e-05
MASKED = -1e30
ROOT_HALF = 0.7071067811865476
INV_ROOT_TWO_PI = 0.3989422804014327
VMEM_LIMIT = 66 * 1024 * 1000
MESH = pl.DeviceIdType.MESH
DMA = pltpu.SemaphoreType.DMA


def nn(left, right):
    return lax.dot_general(left, right, (((1,), (0,)), ((), ())), preferred_element_type=F32)


def nt(left, right):
    return lax.dot_general(left, right, (((1,), (1,)), ((), ())), preferred_element_type=F32)


def tn(left, right):
    return lax.dot_general(left, right, (((0,), (0,)), ((), ())), preferred_element_type=F32)


def remote(src, dst, send_sem, recv_sem, peer):
    return pltpu.make_async_remote_copy(
        src_ref=src,
        dst_ref=dst,
        send_sem=send_sem,
        recv_sem=recv_sem,
        device_id=peer,
        device_id_type=MESH,
    )


def greet(peers):
    barrier = pltpu.get_barrier_semaphore()
    for peer in peers:
        pl.semaphore_signal(barrier, inc=1, device_id=peer, device_id_type=MESH)
    pl.semaphore_wait(barrier, len(peers))


class Place:
    def __init__(self, ns, nc):
        self.s = lax.axis_index("shard")
        self.c = lax.axis_index("ctx")
        self.t = lax.axis_index("tp")
        self.core = lax.rem(self.t, 2)
        self.y = self.t // 2
        self.mate_t = self.t + 1 - 2 * self.core
        self.ymate_t = lax.rem(self.t + 2, 4)
        self.mate = {"tp": self.mate_t}
        self.ymate = {"tp": self.ymate_t}
        self.zpeers = [{"ctx": lax.rem(self.c + k, nc)} for k in range(1, nc)]
        self.xpeers = [{"shard": lax.rem(self.s + r, ns)} for r in range(1, ns)]


class TpGather:
    def __init__(self, place, buf, sems):
        self.p, self.buf = place, buf
        self.ys, self.yr, self.ks, self.kr, self.fs, self.fr = sems

    def _y(self, b, i, src):
        p = self.p
        return remote(src, self.buf.at[b, p.t], self.ys.at[i], self.yr.at[i], p.ymate)

    def _k(self, b, i, src):
        p = self.p
        return remote(src, self.buf.at[b, p.t], self.ks.at[i], self.kr.at[i], p.mate)

    def _f(self, b, i):
        p = self.p
        piece = self.buf.at[b, p.ymate_t]
        return remote(piece, piece, self.fs.at[i], self.fr.at[i], p.mate)

    def send(self, b, i, src=None):
        src = self.buf.at[b, self.p.t] if src is None else src
        self._y(b, i, src).start()
        self._k(b, i, src).start()

    def forward(self, b, i):
        p = self.p
        piece = self.buf.at[b, p.ymate_t]
        remote(piece, piece, self.ys.at[i], self.yr.at[i], p.ymate).wait_recv()
        self._f(b, i).start()

    def arrive(self, b, i):
        p = self.p
        piece = self.buf.at[b, p.mate_t]
        remote(piece, piece, self.ks.at[i], self.kr.at[i], p.mate).wait_recv()
        piece = self.buf.at[b, lax.rem(p.mate_t + 2, 4)]
        remote(piece, piece, self.fs.at[i], self.fr.at[i], p.mate).wait_recv()

    def drain(self, b, i, src=None):
        src = self.buf.at[b, self.p.t] if src is None else src
        self._y(b, i, src).wait_send()
        self._k(b, i, src).wait_send()
        self._f(b, i).wait_send()


class TpReduce:
    def __init__(self, place, terms, from_mate, staged, from_y, sems):
        self.p, self.terms, self.from_mate, self.staged, self.from_y = (
            place,
            terms,
            from_mate,
            staged,
            from_y,
        )
        self.ks, self.kr, self.ys, self.yr = sems

    def _k(self, b):
        p = self.p
        return remote(
            self.terms.at[b, :, 1 - p.core],
            self.from_mate.at[b],
            self.ks.at[b],
            self.kr.at[b],
            p.mate,
        )

    def _y(self, b):
        return remote(
            self.staged.at[b], self.from_y.at[b], self.ys.at[b], self.yr.at[b], self.p.ymate
        )

    def send(self, b):
        self._k(b).start()

    def across(self, b):
        p = self.p
        self._k(b).wait_recv()
        other = 1 - p.y
        self.staged[b] = (
            self.terms[b, other, p.core].astype(F32) + self.from_mate[b, other].astype(F32)
        ).astype(BF)
        self._y(b).start()

    def result(self, b):
        p = self.p
        self._y(b).wait_recv()
        return (
            self.terms[b, p.y, p.core].astype(F32)
            + self.from_mate[b, p.y].astype(F32)
            + self.from_y[b].astype(F32)
        )

    def drain(self, b):
        self._k(b).wait_send()
        self._y(b).wait_send()


def column(row, width=128):
    return jnp.broadcast_to(row, (width, row.shape[-1])).T


def project_kernel(
    ns, nc, x_ref, type_ref, seg_ref, qw_ref, kvw_ref, ow_ref, dn_ref, qb_ref, vb_ref,
    xf_ref, q_ref, kv_ref, codef_ref, wf_ref, wo_ref, dnt_ref,
    wst, code, bias, local, zs, zr, ds, dr, ws, wr, *tp_sems,
):
    p = Place(ns, nc)
    piece = x_ref.shape[1] // 4
    heads = wst.shape[0] - 1
    for j in range(nc):
        label = seg_ref[j : j + 1]
        code[j] = jnp.where(type_ref[j : j + 1] == 0, label, -label).astype(F32)
    greet([p.mate, p.ymate] + p.zpeers + p.xpeers)
    mine = pl.ds(p.t * piece, piece)

    def x_send(k):
        peer = p.zpeers[k]
        return remote(
            x_ref.at[peer["ctx"], mine], xf_ref.at[p.c, p.t], zs.at[k], zr.at[k], peer
        )

    def code_send(k):
        peer = p.zpeers[k]
        return remote(code.at[peer["ctx"]], codef_ref.at[p.c], ds.at[k], dr.at[k], peer)

    def gathered(h, src):
        return wf_ref.at[h, src] if h < heads else wo_ref.at[src]

    def weight(h, r):
        return remote(wst.at[h], gathered(h, p.s), ws.at[h, r], wr.at[h, r], p.xpeers[r])

    def weight_landed(h):
        for r in range(ns - 1):
            landed = gathered(h, lax.rem(p.s + ns - 1 - r, ns))
            remote(landed, landed, ws.at[h, r], wr.at[h, r], p.xpeers[r]).wait_recv()

    for k in range(nc - 1):
        x_send(k).start()
    own = x_ref.at[p.c, mine]
    gather = TpGather(p, xf_ref, tp_sems)
    gather.send(p.c, 0, own)
    for h in range(heads):
        cols = slice(h * HEAD, (h + 1) * HEAD)
        parts = [qw_ref[k, cols] for k in range(4)] + [kvw_ref[k, cols] for k in range(2)]
        wst[h] = jnp.concatenate(parts, axis=0).T
        for r in range(ns - 1):
            weight(h, r).start()
    turned = ow_ref[...].T
    blank = jnp.zeros((turned.shape[0], HEAD), BF)
    parts = []
    for h in range(heads):
        parts += [blank, turned[:, h * HEAD : (h + 1) * HEAD]]
    wst[heads] = jnp.concatenate(parts, axis=1)
    for r in range(ns - 1):
        weight(heads, r).start()
    for k in range(nc - 1):
        code_send(k).start()
    copies = [
        pltpu.make_async_copy(own, xf_ref.at[p.c, p.t], local.at[0]),
        pltpu.make_async_copy(code.at[p.c], codef_ref.at[p.c], local.at[1]),
        pltpu.make_async_copy(wst.at[pl.ds(0, heads)], wf_ref.at[:, p.s], local.at[2]),
        pltpu.make_async_copy(wst.at[heads], wo_ref.at[p.s], local.at[3]),
    ]
    for copy in copies:
        copy.start()
    vb = vb_ref[...].reshape(1, -1)
    for h in range(heads):
        cols = slice(h * HEAD, (h + 1) * HEAD)
        parts = [qb_ref[k : k + 1, cols] for k in range(4)]
        bias[h] = jnp.concatenate(parts + [jnp.zeros((1, HEAD), F32), vb[:, cols]], axis=1)
    dnt_ref[...] = dn_ref[...].T
    blocks = [lax.rem(p.c + nc - k, nc) for k in range(nc)]
    for k in range(1, nc):
        landed = xf_ref.at[blocks[k], p.t]
        remote(landed, landed, zs.at[k - 1], zr.at[k - 1], p.zpeers[k - 1]).wait_recv()
        gather.send(blocks[k], k)
        gather.forward(blocks[k - 1], k - 1)
    gather.forward(blocks[nc - 1], nc - 1)
    for k in range(nc):
        gather.arrive(blocks[k], k)
    for k in range(nc - 1):
        landed = codef_ref.at[blocks[k + 1]]
        remote(landed, landed, ds.at[k], dr.at[k], p.zpeers[k]).wait_recv()
    for copy in copies:
        copy.wait()
    width = xf_ref.shape[-1]
    rows = 4 * piece
    for h in range(heads):
        weight_landed(h)

        def project(b, carry):
            x = xf_ref[b].reshape(rows, width)
            out = nn(x, wf_ref[h].reshape(width, 384)) + bias[h]
            entity = column(codef_ref[b]) < 0.0
            at = pl.ds(pl.multiple_of(b * rows, rows), rows)
            chosen = jnp.where(entity, out[:, 128:256], out[:, 0:128])
            q_ref[h, at] = (chosen * HEAD ** (-0.5)).astype(BF)
            kv_ref[h, at] = out[:, 256:384].astype(BF)
            return carry

        lax.fori_loop(0, nc, project, 0)
    weight_landed(heads)
    for h in range(heads + 1):
        for r in range(ns - 1):
            weight(h, r).wait_send()
    for k in range(nc - 1):
        x_send(k).wait_send()
        code_send(k).wait_send()
    gather.drain(p.c, 0, own)
    for k in range(1, nc):
        gather.drain(blocks[k], k)


def attend_kernel(q_ref, kv_ref, code_ref, e_ref, ctx_ref, inv_ref, kcat, vt, segcol):
    h, b = pl.program_id(0), pl.program_id(1)
    length = kv_ref.shape[1]
    nblk, rows = code_ref.shape[0], code_ref.shape[2]

    @pl.when((h == 0) & (b == 0))
    def _():
        for j in range(nblk):
            col = jnp.abs(column(code_ref[j]))
            segcol[j * rows : (j + 1) * rows] = jnp.where(col == 0.0, -1.0, col)

    @pl.when(b == 0)
    def _():
        low_half = lax.broadcasted_iota(jnp.int32, (rows, 128), 1) < HEAD
        for j in range(nblk):
            at = slice(j * rows, (j + 1) * rows)
            entity = column(code_ref[j]) < 0.0
            kv = kv_ref[0, at].astype(F32)
            turned = pltpu.roll(kv, HEAD, 1)
            keep = jnp.where(low_half, kv, turned)
            kcat[at] = jnp.where(low_half == entity, 0.0, keep).astype(BF)
            vt[:, at] = jnp.where(low_half, 0.0, kv).T.astype(BF)

    scores = nt(kcat[...], q_ref[0])
    segment = jnp.abs(code_ref[b])
    col = segcol[...]
    allowed = jnp.concatenate([col] * (rows // 128), axis=1) == segment
    scores = jnp.where(allowed, scores, MASKED)
    top = jnp.max(scores, axis=0, keepdims=True)
    top = jnp.where(top == MASKED, 0.0, top)
    exponent = jnp.exp(scores - top)
    inverse = 1.0 / jnp.maximum(jnp.sum(exponent, axis=0, keepdims=True), 1.0)
    exponent = exponent.astype(BF)
    e_ref[0] = exponent
    inv_ref[0] = inverse
    ctx_ref[...] = (nn(vt[...], exponent) * inverse).T.astype(BF)


def spread(values):
    average = jnp.mean(values, axis=-1, keepdims=True)
    centred = values - average
    inverse = lax.rsqrt(jnp.mean(centred * centred, axis=-1, keepdims=True) + EPS)
    return centred * inverse, inverse


def unspread(upstream, normed, inverse, gain):
    scaled = upstream * gain
    first = jnp.mean(scaled, axis=-1, keepdims=True)
    second = jnp.mean(scaled * normed, axis=-1, keepdims=True)
    return inverse * (scaled - first - normed * second)


def total(values):
    return jnp.sum(values, axis=0, keepdims=True)


SKEWS_C = (0, 1, 3, 4, 5, 6, 8, 9, 10, 11, 13, 14, 15)


def feed_kernel(
    ns, nc, ctx_ref, wo_ref, xf_ref, og_ref, wu_ref, wd_ref, *rest,
):
    vecs, rest = rest[:7], rest[7:]
    (
        ga_ref, hid_ref, gfi_ref, dff_ref, small_ref,
        wuf, wdf, ogo, hsend,
        t0, m0, s0, y0, t1, m1, s1, y1, t2, m2, s2, y2,
        low, gf, active, slope, gup, fo, fh, fi, gs, dst, xr,
        local, ws, wr, os, orr, hs, hr, xs, xrs, *tp_sems,
    ) = rest
    p = Place(ns, nc)
    piece, width = xf_ref.shape[2:]
    rows = 4 * piece
    greet([p.mate, p.ymate] + p.zpeers + p.xpeers)
    weights = ((wu_ref, wuf), (wd_ref, wdf))

    def weight(a, r):
        src, dst = weights[a]
        return remote(src, dst.at[p.s], ws.at[a, r], wr.at[a, r], p.xpeers[r])

    for a in range(2):
        for r in range(ns - 1):
            weight(a, r).start()
    mine = pl.ds(p.t * piece, piece)

    def og_send(k):
        peer = p.zpeers[k]
        return remote(og_ref.at[peer["ctx"], mine], ogo.at[p.c], os.at[k], orr.at[k], peer)

    for k in range(nc - 1):
        og_send(k).start()
    copies = [
        pltpu.make_async_copy(og_ref.at[p.c, mine], ogo.at[p.c], local.at[0]),
        pltpu.make_async_copy(wu_ref, wuf.at[p.s], local.at[1]),
        pltpu.make_async_copy(wd_ref, wdf.at[p.s], local.at[2]),
    ]
    for copy in copies:
        copy.start()
    small_ref[...] = jnp.zeros_like(small_ref)

    sums = [
        TpReduce(p, *bufs, [tp_sems[j].at[i] for j in range(4)])
        for i, bufs in enumerate(((t0, m0, s0, y0), (t1, m1, s1, y1), (t2, m2, s2, y2)))
    ]
    shares = [
        TpGather(p, buf, [tp_sems[4 + j].at[i] for j in range(6)])
        for i, buf in enumerate((low, gf, ga_ref))
    ]
    out_bias, gain1, bias1, up_bias, down_bias, gain2, bias2 = (
        ref[...].reshape(1, -1) for ref in vecs
    )

    def put(terms, b, values):
        terms[b] = values.astype(BF).reshape(2, 2, piece, width)

    def add_small(row, values):
        small_ref[row : row + 1] += total(values)

    def out_project(b):
        put(t0, b, nt(ctx_ref[b], wo_ref[...].reshape(width, -1)))
        sums[0].send(b)

    def norm_one(b):
        h = xf_ref[b, p.t].astype(F32) + (sums[0].result(b) + out_bias)
        normed, inverse = spread(h)
        first = normed * gain1 + bias1
        fo[b] = first
        fh[b] = normed
        fi[b] = inverse
        low[b, p.t] = first.astype(BF)
        shares[0].send(b, b)

    def feed_forward(b):
        @pl.when(b == 0)
        def _():
            for a in range(2):
                for r in range(ns - 1):
                    landed = weights[a][1].at[lax.rem(p.s + ns - 1 - r, ns)]
                    remote(landed, landed, ws.at[a, r], wr.at[a, r], p.xpeers[r]).wait_recv()
            for copy in copies[1:]:
                copy.wait()

        shares[0].arrive(b, b)
        up = nn(low[b].reshape(rows, width), wuf[...].reshape(width, -1)) + up_bias
        cdf = 0.5 * (1.0 + lax.erf(up * ROOT_HALF))
        act = (up * cdf).astype(BF)
        active[b] = act
        slope[b] = cdf + up * (jnp.exp(-0.5 * up * up) * INV_ROOT_TWO_PI)
        put(t1, b, nt(act, wdf[...].reshape(width, -1)))
        sums[1].send(b)

    def hid_send(b):
        return remote(hsend.at[b], hid_ref.at[p.c], hs.at[b], hr.at[p.c], {"ctx": b})

    def norm_two(b):
        @pl.when(b == 0)
        def _():
            for k in range(nc - 1):
                landed = ogo.at[lax.rem(p.c + nc - 1 - k, nc)]
                remote(landed, landed, os.at[k], orr.at[k], p.zpeers[k]).wait_recv()
            copies[0].wait()

        normed, inverse = spread(fo[b] + (sums[1].result(b) + down_bias))
        hsend[b] = (normed * gain2 + bias2).astype(BF)

        upstream = ogo[b].astype(F32)
        add_small(2, upstream * normed)
        add_small(3, upstream)
        grad = unspread(upstream, normed, inverse, gain2)
        gs[b] = grad
        grad = grad.astype(BF)
        gf[b, p.t] = grad
        add_small(5, grad.astype(F32))
        shares[1].send(b, b)

        @pl.when(b != p.c)
        def _():
            hid_send(b).start()

        @pl.when(b == p.c)
        def _():
            pltpu.make_async_copy(hsend.at[b], hid_ref.at[p.c], local.at[3]).start()

    def feed_back(b):
        shares[1].arrive(b, b)
        grad = nn(gf[b].reshape(rows, width), wdf[...].reshape(width, -1))
        grad = (grad.astype(BF).astype(F32) * slope[b]).astype(BF)
        gup[b] = grad
        add_small(6, grad.astype(F32))
        put(t2, b, nt(grad, wuf[...].reshape(width, -1)))
        sums[2].send(b)

    def norm_back(b):
        grad = gs[b] + sums[2].result(b)
        add_small(0, grad * fh[b])
        add_small(1, grad)
        grad = unspread(grad, fh[b], fi[b], gain1)
        gfi_ref[b] = grad
        grad = grad.astype(BF)
        ga_ref[b, p.t] = grad
        add_small(4, grad.astype(F32))
        shares[2].send(b, b)

    stages = (
        out_project,
        sums[0].across,
        norm_one,
        lambda b: shares[0].forward(b, b),
        feed_forward,
        sums[1].across,
        norm_two,
        lambda b: shares[1].forward(b, b),
        feed_back,
        sums[2].across,
        norm_back,
        lambda b: shares[2].forward(b, b),
        lambda b: shares[2].arrive(b, b),
    )

    def grad_send(a, r):
        return remote(
            dst.at[a, p.xpeers[r]["shard"]], xr.at[a, r], xs.at[a, r], xrs.at[a, r], p.xpeers[r]
        )

    def weight_grad(a):
        left = (low, gf)[a][...].reshape(nc * rows, width)
        right = (gup, active)[a][...].reshape(nc * rows, -1)
        dst[a] = tn(left, right).astype(BF).reshape(dst.shape[1:])
        for r in range(ns - 1):
            grad_send(a, r).start()

    def slot(step, carry):
        for skew, stage in zip(SKEWS_C, stages):
            b = step - skew

            @pl.when((b >= 0) & (b < nc))
            def _(stage=stage, b=b):
                stage(b)

        for a in range(2):

            @pl.when(step == SKEWS_C[8] + nc - 1 + a)
            def _(a=a):
                weight_grad(1 - a)

        return carry

    lax.fori_loop(0, SKEWS_C[-1] + nc, slot, 0)
    lanes = width // 128
    for a in (1, 0):
        grad = dst[a, p.s].astype(F32)
        for r in range(ns - 1):
            grad_send(a, r).wait_recv()
            grad = grad + xr[a, r].astype(F32)
        grad = grad.astype(BF)
        for j in range(lanes):
            dff_ref[lanes * a + j] = grad[:, j * 128 : (j + 1) * 128]
    for k in range(1, nc):
        src = lax.rem(p.c + k, nc)
        landed = hid_ref.at[src]
        remote(landed, landed, hs.at[src], hr.at[src], p.zpeers[k - 1]).wait_recv()
        hid_send(src).wait_send()
    pltpu.make_async_copy(hsend.at[p.c], hid_ref.at[p.c], local.at[3]).wait()
    for a in range(2):
        for r in range(ns - 1):
            weight(a, r).wait_send()
            grad_send(a, r).wait_send()
    for k in range(nc - 1):
        og_send(k).wait_send()
    for i in range(3):
        for b in range(nc):
            sums[i].drain(b)
            shares[i].drain(b, b)


FF_CHUNKS = 12
OUT_CHUNKS = 2
HEAD_CHUNKS = 3
OWN_LAG, PASS_LAG = 3, 6


def back_kernel(
    ns, nc, ga_ref, wf_ref, wo_ref, ctx_ref, xf_ref, code_ref, inv_ref, q_ref, kv_ref, gfi_ref, hid_ref,
    dff_ref, smc_ref, e_ref,
    ing_ref, hidf_ref, dw_ref, sm_ref,
    dctx, kcat, dkey, dval, dqkv, back, qb, ebuf, dqo, terms,
    m0, s0, y0, ig, zo, zr, zq, zsum, xr, smt, smz, smx,
    local, es, xs, xrs, z1s, z1r, z2s, z2r, z3s, z3r, z4s, z4r, gs, gr, hl,
    ss, sr, szs, szr, sxs, sxr, *tp_sems,
):
    p = Place(ns, nc)
    piece, width = gfi_ref.shape[1:]
    rows = 4 * piece
    length = nc * rows
    heads = q_ref.shape[0]
    steps = heads * nc
    chunks = dw_ref.shape[0]

    def fetch(i):
        return pltpu.make_async_copy(e_ref.at[i], ebuf.at[lax.rem(i, 2)], es.at[lax.rem(i, 2)])

    fetch(0).start()
    greet([p.mate, p.ymate] + p.zpeers + p.xpeers)


    def x_send(lo, n, r):
        peer = p.xpeers[r]
        return remote(
            dqo.at[pl.ds(lo, n), peer["shard"]],
            xr.at[r, pl.ds(lo, n)],
            xs.at[lo, r],
            xrs.at[lo, r],
            peer,
        )

    back_sum = TpReduce(p, terms, m0, s0, y0, [tp_sems[j] for j in range(4)])
    share_h = TpGather(p, hidf_ref, [tp_sems[4 + j].at[0] for j in range(6)])
    share_g = TpGather(p, ing_ref, [tp_sems[4 + j].at[1] for j in range(6)])

    outer = (p.c == 0) | (p.c == nc - 1)
    inner = (p.c > 0) & (p.c < nc - 1)
    inward = {"ctx": 1 + p.c // 3}
    outward = {"ctx": lax.rem(3 * (p.c + nc - 1), 6)}
    across = {"ctx": lax.rem(2 * nc - 1 - p.c, nc)}

    def to_inner(k):
        return remote(zo.at[k], zr.at[k], z1s.at[k], z1r.at[k], inward)

    def to_owner(k):
        return remote(zsum.at[k], zq.at[k], z2s.at[k], z2r.at[k], across)

    def to_other(k):
        return remote(dw_ref.at[k], dw_ref.at[k], z3s.at[k], z3r.at[k], across)

    def to_outer(k):
        return remote(dw_ref.at[k], dw_ref.at[k], z4s.at[k], z4r.at[k], outward)

    def owns(k):
        return lax.rem(k + p.c, 2) == 1

    def line_start(lo, n):
        for k in range(lo, lo + n):
            if k >= FF_CHUNKS:
                j = k - FF_CHUNKS
                grad = dqo[j, p.s].astype(F32)
                for r in range(ns - 1):
                    if k == lo:
                        x_send(j, n, r).wait_recv()
                    grad = grad + xr[r, j].astype(F32)
                zo[k] = grad.astype(BF)

            @pl.when(outer)
            def _(k=k):
                to_inner(k).start()

    def line_in(k):
        to_inner(k).wait_recv()

        @pl.when(jnp.logical_not(owns(k)))
        def _():
            zsum[k] = (zo[k].astype(F32) + zr[k].astype(F32)).astype(BF)
            to_owner(k).start()

    def line_own(k):
        @pl.when(owns(k))
        def _():
            to_owner(k).wait_recv()
            dw_ref[k] = (zo[k].astype(F32) + zr[k].astype(F32) + zq[k].astype(F32)).astype(BF)
            to_other(k).start()
            to_outer(k).start()

    def line_pass(k):
        @pl.when(jnp.logical_not(owns(k)))
        def _():
            to_other(k).wait_recv()
            to_outer(k).start()

    def line_to(lo, hi):
        @pl.when(inner)
        def _():
            for k in range(lo, hi):
                if k < chunks:
                    line_in(k)
                if 0 <= k - OWN_LAG < chunks:
                    line_own(k - OWN_LAG)
                if 0 <= k - PASS_LAG < chunks:
                    line_pass(k - PASS_LAG)

    def line_end(k):
        @pl.when(outer)
        def _():
            to_outer(k).wait_recv()
            to_inner(k).wait_send()

        @pl.when(inner)
        def _():
            @pl.when(owns(k))
            def _():
                to_other(k).wait_send()

            @pl.when(jnp.logical_not(owns(k)))
            def _():
                to_owner(k).wait_send()

            to_outer(k).wait_send()


    def small_tp(i, peer):
        return remote(smt.at[2 * i], smt.at[2 * i + 1], ss.at[i], sr.at[i], peer)

    shared = lax.broadcasted_iota(jnp.int32, smt.shape[1:], 0) < 6

    def small_fold(i):
        return smt[2 * i] + jnp.where(shared, smt[2 * i + 1], 0.0)

    def small_z(k):
        return remote(smz.at[p.c], smz.at[p.c], szs.at[k], szr.at[k], p.zpeers[k])

    def small_x(r):
        return remote(smx.at[p.s], smx.at[p.s], sxs.at[r], sxr.at[r], p.xpeers[r])

    def small_zero():
        smt[0] = jnp.zeros_like(smt[0])
        smt[0, :, 0:width] = smc_ref[...]
        for h in range(heads):
            smt[0, 7:8, h * 384 : (h + 1) * 384] = qb[h]
        small_tp(0, p.mate).start()

    def small_one():
        small_tp(0, p.mate).wait_recv()
        smt[2] = small_fold(0)
        small_tp(1, p.ymate).start()

    def small_two():
        small_tp(1, p.ymate).wait_recv()
        smz[p.c] = small_fold(1)
        for k in range(nc - 1):
            small_z(k).start()

    def small_three():
        for k in range(nc - 1):
            landed = smz.at[lax.rem(p.c + nc - 1 - k, nc)]
            remote(landed, landed, szs.at[k], szr.at[k], p.zpeers[k]).wait_recv()
        value = smz[0]
        for k in range(1, nc):
            value = value + smz[k]
        smx[p.s] = value
        for r in range(ns - 1):
            small_x(r).start()

    def small_four():
        for r in range(ns - 1):
            landed = smx.at[lax.rem(p.s + ns - 1 - r, ns)]
            remote(landed, landed, sxs.at[r], sxr.at[r], p.xpeers[r]).wait_recv()
        value = smx[0]
        for r in range(1, ns):
            value = value + smx[r]
        sm_ref[...] = value


    def grad_send(b):
        return remote(ig.at[b], ing_ref.at[p.c, p.t], gs.at[b], gr.at[p.c], {"ctx": b})

    def grad_own(b):
        ig[b] = (gfi_ref[b] + back_sum.result(b)).astype(BF)

        @pl.when(b != p.c)
        def _():
            grad_send(b).start()

        @pl.when(b == p.c)
        def _():
            pltpu.make_async_copy(ig.at[b], ing_ref.at[p.c, p.t], hl.at[0]).start()

    order = [lax.rem(p.c + k, nc) for k in range(nc)]

    def grad_share(k):
        q = order[k]
        if k > 0:
            landed = ing_ref.at[q, p.t]
            remote(landed, landed, gs.at[q], gr.at[q], {"ctx": q}).wait_recv()
        else:
            pltpu.make_async_copy(ig.at[p.c], ing_ref.at[p.c, p.t], hl.at[0]).wait()
        share_g.send(q, k)


    for b in range(nc):
        share_h.send(b, b, hid_ref.at[b])
    keep = pltpu.make_async_copy(hid_ref, hidf_ref.at[:, p.t], local.at[0])
    keep.start()
    zo[0:FF_CHUNKS] = dff_ref[...]
    line_start(0, FF_CHUNKS)
    grad_attn = ga_ref[...].reshape(length, width)
    out = wo_ref[...].reshape(width, heads * 128)
    for i in range(heads):
        dctx[i] = nn(grad_attn, out[:, i * 128 : (i + 1) * 128]).astype(BF)

    def put_grad(lo, n, value):
        for j in range(n):
            dqo[lo + j] = value[:, j * 128 : (j + 1) * 128].reshape(dqo.shape[1:])
        for r in range(ns - 1):
            x_send(lo, n, r).start()

    value = tn(grad_attn, ctx_ref[...]).astype(BF)
    value = [value[:, i * 128 + HEAD : (i + 1) * 128] for i in range(heads)]
    put_grad(0, OUT_CHUNKS, jnp.concatenate(value + [jnp.zeros_like(value[0])], axis=1))
    back[...] = jnp.zeros_like(back)
    low_half = lax.broadcasted_iota(jnp.int32, (rows, 128), 1) < HEAD

    def attend_step(i):
        h, b = i // nc, lax.rem(i, nc)
        fetch(i).wait()

        @pl.when(i + 1 < steps)
        def _():
            fetch(i + 1).start()

        @pl.when(b == 0)
        def _():
            for j in range(nc):
                at = slice(j * rows, (j + 1) * rows)
                entity = column(code_ref[j]) < 0.0
                kv = kv_ref[h, at].astype(F32)
                kept = jnp.where(low_half, kv, pltpu.roll(kv, HEAD, 1))
                kcat[at] = jnp.where(low_half == entity, 0.0, kept).astype(BF)
            dkey[...] = jnp.zeros_like(dkey)
            dval[...] = jnp.zeros_like(dval)

        at = pl.ds(pl.multiple_of(b * rows, rows), rows)
        lanes = pl.ds(pl.multiple_of(h * 128, 128), 128)
        grad_ctx = dctx[h, at].astype(F32).T * inv_ref[i]
        row_dot = jnp.sum(grad_ctx * ctx_ref[at, lanes].astype(F32).T, axis=0, keepdims=True)
        grad_ctx = grad_ctx.astype(BF)
        weight = ebuf[lax.rem(i, 2)]
        grad = nn(kv_ref[h], grad_ctx)
        grad = (weight.astype(F32) * (grad - row_dot)).astype(BF)
        dval[...] += nt(weight, grad_ctx)
        dkey[...] += nn(grad, q_ref[h, at])
        grad_q = tn(kcat[...], grad).T * HEAD ** (-0.5)
        entity = column(code_ref[b]) < 0.0
        dqkv[at, 0:128] = jnp.where(entity, 0.0, grad_q).astype(BF)
        dqkv[at, 128:256] = jnp.where(entity, grad_q, 0.0).astype(BF)

        @pl.when(b == nc - 1)
        def _():
            for j in range(nc):
                part = slice(j * rows, (j + 1) * rows)
                entity = column(code_ref[j]) < 0.0
                grad_k = dkey[part]
                grad_k = jnp.where(entity, pltpu.roll(grad_k, HEAD, 1), grad_k)
                dqkv[part, 256:384] = jnp.where(low_half, grad_k, dval[part]).astype(BF)
            w = wf_ref[h].reshape(width, 384)

            @pl.when(h < heads - 1)
            def _():
                back[...] += nt(dqkv[...], w)

            @pl.when(h == heads - 1)
            def _():
                for j in range(nc):
                    part = slice(j * rows, (j + 1) * rows)
                    value = back[part] + nt(dqkv[part], w)
                    terms[j] = value.astype(BF).reshape(2, 2, piece, width)
                    back_sum.send(j)

            grads = dqkv[...]
            value = tn(xf_ref[...].reshape(length, width), grads).astype(BF)
            put_grad(OUT_CHUNKS + HEAD_CHUNKS * h, HEAD_CHUNKS, value)
            qb[h] = total(grads.astype(F32))

    groups = [(FF_CHUNKS, OUT_CHUNKS)]
    groups += [
        (FF_CHUNKS + OUT_CHUNKS + HEAD_CHUNKS * h, HEAD_CHUNKS) for h in range(heads)
    ]
    reached = [0]

    def line(upto):
        line_to(reached[0], upto)
        reached[0] = upto

    def forward_hidden():
        for b in range(nc):
            share_h.forward(b, b)

    def hand(k):
        share_g.forward(order[k], k)

    events = {
        0: lambda: line(1),
        2: lambda: line(2),
        3: lambda: line(3),
        5: lambda: (line(4), forward_hidden(), line_start(*groups[0])),
        7: lambda: line(5),
        8: lambda: line(6),
        9: lambda: line_start(*groups[1]),
        10: lambda: line(7),
        11: lambda: line(8),
    }

    def slot(i, carry):
        attend_step(i)
        for when, action in events.items():

            @pl.when(i == when)
            def _(action=action):
                action()

        return carry

    lax.fori_loop(0, steps, slot, 0)
    for b in range(nc):
        back_sum.across(b)
    small_zero()
    line_start(*groups[2])
    line(9)
    grad_own(0)
    line(10)
    grad_own(1)
    line(11)
    grad_own(2)
    small_one()
    line(12)
    grad_own(3)
    line_start(*groups[3])
    line(13)
    small_two()
    line(14)
    grad_share(0)
    grad_share(1)
    line(15)
    grad_share(2)
    hand(0)
    grad_share(3)
    hand(1)
    small_three()
    line(16)
    hand(2)
    hand(3)
    small_four()
    line(chunks + PASS_LAG)
    for b in range(nc):
        share_h.arrive(b, b)
        share_g.arrive(order[b], b)
    for k in range(chunks):
        line_end(k)
    keep.wait()
    for lo, n in groups:
        for r in range(ns - 1):
            x_send(lo - FF_CHUNKS, n, r).wait_send()
    for b in range(nc):
        back_sum.drain(b)
        share_h.drain(b, b, hid_ref.at[b])
        share_g.drain(order[b], b)

        @pl.when(b != p.c)
        def _(b=b):
            grad_send(b).wait_send()

    small_tp(0, p.mate).wait_send()
    small_tp(1, p.ymate).wait_send()
    for k in range(nc - 1):
        small_z(k).wait_send()
    for r in range(ns - 1):
        small_x(r).wait_send()


def deliver_kernel(
    ing_ref, hid_ref, dw_ref, sm_ref,
    hidden_ref, grad_ref, qw_ref, kvw_ref, qb_ref, vb_ref, ow_ref, uw_ref, dn_ref, *vec_refs,
):
    hidden_ref[...] = hid_ref[...]
    grad_ref[...] = ing_ref[...].astype(F32)

    @pl.when(pl.program_id(0) == 0)
    def _():
        def wide(lo, n):
            return jnp.concatenate([dw_ref[lo + j].astype(F32) for j in range(n)], axis=1)

        uw_ref[...] = wide(0, 6)
        dn_ref[...] = wide(6, 6).T
        heads = qb_ref.shape[1] // HEAD
        ow_ref[...] = wide(FF_CHUNKS, OUT_CHUNKS)[:, : heads * HEAD].T
        first = FF_CHUNKS + OUT_CHUNKS
        grads = [wide(first + HEAD_CHUNKS * h, HEAD_CHUNKS).T for h in range(heads)]
        small = sm_ref[...]
        for k in range(6):
            cols = slice(k * HEAD, (k + 1) * HEAD)
            part = jnp.concatenate([grad[cols] for grad in grads], axis=0)
            vec = jnp.concatenate(
                [
                    small[7:8, h * 384 + k * HEAD : h * 384 + (k + 1) * HEAD]
                    for h in range(heads)
                ],
                axis=1,
            )
            if k < 4:
                qw_ref[k] = part
                qb_ref[k : k + 1] = vec
            else:
                kvw_ref[k - 4] = part
            if k == 5:
                vb_ref[...] = vec.reshape(-1)
        width = uw_ref.shape[1]
        for i, ref in enumerate(vec_refs):
            ref[...] = small[i : i + 1, :width].reshape(-1)


def vmem(count):
    return [pl.BlockSpec(memory_space=pltpu.VMEM)] * count


def struct(shape, dtype):
    return jax.ShapeDtypeStruct(shape, dtype)


def params(collective_id=None):
    if collective_id is None:
        return pltpu.CompilerParams(
            vmem_limit_bytes=VMEM_LIMIT, dimension_semantics=("arbitrary", "arbitrary")
        )
    return pltpu.CompilerParams(
        vmem_limit_bytes=VMEM_LIMIT, collective_id=collective_id, has_side_effects=True
    )


TP_GATHER = 6
TP_REDUCE = 4


def per_device(
    hidden_in,
    token_type,
    segment,
    query_weight,
    key_value_weight,
    query_bias,
    value_bias,
    out_weight,
    out_bias,
    norm1_gain,
    norm1_bias,
    up_weight,
    up_bias,
    down_weight,
    down_bias,
    norm2_gain,
    norm2_bias,
    out_grad,
):
    ns, nc = lax.axis_size("shard"), lax.axis_size("ctx")
    seqs, local_len, width = hidden_in.shape
    part = query_weight.shape[2]
    heads = part // HEAD
    shard_rows = query_weight.shape[1]
    ff = up_weight.shape[1]
    piece = local_len // 4
    length = nc * local_len
    assert seqs == nc == 4 and heads == 3 and ff == width
    wide = ns - 1

    mixed = OUT_CHUNKS + HEAD_CHUNKS * heads
    line = (FF_CHUNKS + mixed, shard_rows, 128)
    xf, q, kv, code, wf, wo, down_t = pl.pallas_call(
        functools.partial(project_kernel, ns, nc),
        out_shape=(
            struct((nc, 4, piece, width), BF),
            struct((heads, length, 128), BF),
            struct((heads, length, 128), BF),
            struct((nc, 1, local_len), F32),
            struct((heads, ns, shard_rows, 384), BF),
            struct((ns, shard_rows, 384), BF),
            struct((shard_rows, ff), BF),
        ),
        in_specs=vmem(9),
        out_specs=vmem(7),
        scratch_shapes=[
            pltpu.VMEM((heads + 1, shard_rows, 384), BF),
            pltpu.VMEM((nc, 1, local_len), F32),
            pltpu.VMEM((heads, 1, 384), F32),
            DMA((4,)),
        ]
        + [DMA((nc - 1,))] * 4
        + [DMA((heads + 1, wide))] * 2
        + [DMA((nc,))] * TP_GATHER,
        compiler_params=params(0),
        name="project",
    )(
        hidden_in,
        token_type,
        segment,
        query_weight.swapaxes(1, 2),
        key_value_weight.swapaxes(1, 2),
        out_weight,
        down_weight,
        query_bias,
        value_bias,
    )

    grid = (heads, nc)
    e_spec = pl.BlockSpec((1, length, local_len), lambda h, b: (h * nc + b, 0, 0))
    inv_spec = pl.BlockSpec((1, 1, local_len), lambda h, b: (h * nc + b, 0, 0))
    ctx_spec = pl.BlockSpec((local_len, 128), lambda h, b: (b, h))
    q_spec = pl.BlockSpec((1, local_len, 128), lambda h, b: (h, b, 0))
    kv_spec = pl.BlockSpec((1, length, 128), lambda h, b: (h, 0, 0))

    def whole(shape):
        return pl.BlockSpec(shape, lambda h, b: (0,) * len(shape))

    e, ctx, inv = pl.pallas_call(
        attend_kernel,
        grid=grid,
        out_shape=(
            struct((heads * nc, length, local_len), BF),
            struct((length, heads * 128), BF),
            struct((heads * nc, 1, local_len), F32),
        ),
        in_specs=[q_spec, kv_spec, whole((nc, 1, local_len))],
        out_specs=(e_spec, ctx_spec, inv_spec),
        scratch_shapes=[
            pltpu.VMEM((length, 128), BF),
            pltpu.VMEM((128, length), BF),
            pltpu.VMEM((length, 128), F32),
        ],
        compiler_params=params(),
        name="attend",
    )(q, kv, code)

    full = pltpu.VMEM((nc, 4, piece, width), BF)
    own = pltpu.VMEM((nc, piece, width), BF)
    own32 = pltpu.VMEM((nc, piece, width), F32)
    reduce_bufs = [
        pltpu.VMEM((nc, 2, 2, piece, width), BF),
        pltpu.VMEM((nc, 2, piece, width), BF),
        own,
        own,
    ]
    rows_ff = pltpu.VMEM((nc, local_len, ff), BF)
    ga, hid, gfi, dff, small = pl.pallas_call(
        functools.partial(feed_kernel, ns, nc),
        out_shape=(
            struct((nc, 4, piece, width), BF),
            struct((nc, piece, width), BF),
            struct((nc, piece, width), F32),
            struct((FF_CHUNKS, shard_rows, 128), BF),
            struct((8, width), F32),
        ),
        in_specs=vmem(13),
        out_specs=vmem(5),
        scratch_shapes=[
            pltpu.VMEM((ns, shard_rows, ff), BF),
            pltpu.VMEM((ns, shard_rows, ff), BF),
            own,
            own,
        ]
        + reduce_bufs * 3
        + [
            full,
            full,
            rows_ff,
            pltpu.VMEM((nc, local_len, ff), F32),
            rows_ff,
            own32,
            own32,
            pltpu.VMEM((nc, piece, 1), F32),
            own32,
            pltpu.VMEM((2, ns, shard_rows, ff), BF),
            pltpu.VMEM((2, wide, shard_rows, ff), BF),
        ]
        + [DMA((4,))]
        + [DMA((2, wide))] * 2
        + [DMA((nc - 1,))] * 2
        + [DMA((nc,))] * 2
        + [DMA((2, wide))] * 2
        + [DMA((3, nc))] * (TP_REDUCE + TP_GATHER),
        compiler_params=params(1),
        name="feed",
    )(
        ctx.reshape(nc, local_len, heads * 128),
        wo,
        xf,
        out_grad,
        up_weight,
        down_t,
        out_bias,
        norm1_gain,
        norm1_bias,
        up_bias,
        down_bias,
        norm2_gain,
        norm2_bias,
    )

    chunks = pltpu.VMEM(line, BF)
    wide_small = heads * 384
    ing, hid, dw, small = pl.pallas_call(
        functools.partial(back_kernel, ns, nc),
        out_shape=(
            struct((nc, 4, piece, width), BF),
            struct((nc, 4, piece, width), BF),
            struct(line, BF),
            struct((8, wide_small), F32),
        ),
        in_specs=vmem(13) + [pl.BlockSpec(memory_space=pl.ANY)],
        out_specs=vmem(4),
        scratch_shapes=[
            pltpu.VMEM((heads, length, 128), BF),
            pltpu.VMEM((length, 128), BF),
            pltpu.VMEM((length, 128), F32),
            pltpu.VMEM((length, 128), F32),
            pltpu.VMEM((length, 384), BF),
            pltpu.VMEM((length, width), F32),
            pltpu.VMEM((heads, 1, 384), F32),
            pltpu.VMEM((2, length, local_len), BF),
            pltpu.VMEM((mixed, ns, shard_rows, 128), BF),
        ]
        + reduce_bufs
        + [own]
        + [chunks] * 4
        + [
            pltpu.VMEM((wide, mixed, shard_rows, 128), BF),
            pltpu.VMEM((4, 8, wide_small), F32),
            pltpu.VMEM((nc, 8, wide_small), F32),
            pltpu.VMEM((ns, 8, wide_small), F32),
            DMA((1,)),
            DMA((2,)),
        ]
        + [DMA((mixed, wide))] * 2
        + [DMA((FF_CHUNKS + mixed,))] * 8
        + [DMA((nc,))] * 2
        + [DMA((1,))]
        + [DMA((2,))] * 2
        + [DMA((nc - 1,))] * 2
        + [DMA((wide,))] * 2
        + [DMA((nc,))] * TP_REDUCE
        + [DMA((2, nc))] * TP_GATHER,
        compiler_params=params(2),
        name="back",
    )(ga, wf, wo, ctx, xf, code, inv, q, kv, gfi, hid, dff, small, e)

    def block(*shape):
        return pl.BlockSpec(shape, lambda i: (i,) + (0,) * (len(shape) - 1))

    def fixed(*shape):
        return pl.BlockSpec(shape, lambda i: (0,) * len(shape))

    def vector(size):
        return pl.BlockSpec((size,), lambda i: (0,))

    (
        hidden_out,
        in_grad,
        qw,
        kvw,
        qb,
        vb,
        ow,
        uw,
        dn,
        gain1,
        bias1,
        gain2,
        bias2,
        ob,
        db,
        ub,
    ) = pl.pallas_call(
        deliver_kernel,
        grid=(nc,),
        out_shape=(
            struct((nc, local_len, width), BF),
            struct((nc, local_len, width), F32),
            struct((4, part, shard_rows), F32),
            struct((2, part, shard_rows), F32),
            struct((4, part), F32),
            struct((part,), F32),
            struct((part, shard_rows), F32),
            struct((shard_rows, ff), F32),
            struct((ff, shard_rows), F32),
        )
        + (struct((width,), F32),) * 7,
        in_specs=[
            block(1, local_len, width),
            block(1, local_len, width),
            fixed(*line),
            fixed(8, wide_small),
        ],
        out_specs=[
            block(1, local_len, width),
            block(1, local_len, width),
            fixed(4, part, shard_rows),
            fixed(2, part, shard_rows),
            fixed(4, part),
            vector(part),
            fixed(part, shard_rows),
            fixed(shard_rows, ff),
            fixed(ff, shard_rows),
        ]
        + [vector(width)] * 7,
        compiler_params=pltpu.CompilerParams(
            vmem_limit_bytes=VMEM_LIMIT, dimension_semantics=("arbitrary",)
        ),
        name="deliver",
    )(ing.reshape(nc, local_len, width), hid.reshape(nc, local_len, width), dw, small)
    return (
        hidden_out,
        in_grad,
        qw.swapaxes(1, 2),
        kvw.swapaxes(1, 2),
        qb,
        vb,
        ow,
        ob,
        gain1,
        bias1,
        uw,
        ub,
        dn,
        db,
        gain2,
        bias2,
    )


def solution(mesh):
    in_specs = (
        P("shard", "ctx", None),
        P("shard", "ctx"),
        P("shard", "ctx"),
        P(None, "shard", "tp"),
        P(None, "shard", "tp"),
        P(None, "tp"),
        P("tp"),
        P("tp", "shard"),
        P(),
        P(),
        P(),
        P("shard", "tp"),
        P("tp"),
        P("tp", "shard"),
        P(),
        P(),
        P(),
        P("shard", "ctx", None),
    )
    out_specs = (
        P("shard", "ctx", None),
        P("shard", "ctx", None),
        P(None, "shard", "tp"),
        P(None, "shard", "tp"),
        P(None, "tp"),
        P("tp"),
        P("tp", "shard"),
        P(),
        P(),
        P(),
        P("shard", "tp"),
        P("tp"),
        P("tp", "shard"),
        P(),
        P(),
        P(),
    )
    return jax.shard_map(
        per_device, mesh=mesh, in_specs=in_specs, out_specs=out_specs, check_vma=False
    )
```

```python
import functools

import jax
import jax.numpy as jnp
from jax import lax
from jax.experimental import pallas as pl
from jax.experimental.pallas import tpu as pltpu
from jax.sharding import PartitionSpec as P

BF = jnp.bfloat16
F32 = jnp.float32
HEAD = 64
EPS = 1e-05
MASKED = -1e30
ROOT_HALF = 0.7071067811865476
INV_ROOT_TWO_PI = 0.3989422804014327
VMEM_LIMIT = 66 * 1024 * 1000
MESH = pl.DeviceIdType.MESH
DMA = pltpu.SemaphoreType.DMA


def nn(left, right):
    return lax.dot_general(left, right, (((1,), (0,)), ((), ())), preferred_element_type=F32)


def nt(left, right):
    return lax.dot_general(left, right, (((1,), (1,)), ((), ())), preferred_element_type=F32)


def tn(left, right):
    return lax.dot_general(left, right, (((0,), (0,)), ((), ())), preferred_element_type=F32)


def remote(src, dst, send_sem, recv_sem, peer):
    return pltpu.make_async_remote_copy(
        src_ref=src,
        dst_ref=dst,
        send_sem=send_sem,
        recv_sem=recv_sem,
        device_id=peer,
        device_id_type=MESH,
    )


def greet(peers):
    barrier = pltpu.get_barrier_semaphore()
    for peer in peers:
        pl.semaphore_signal(barrier, inc=1, device_id=peer, device_id_type=MESH)
    pl.semaphore_wait(barrier, len(peers))


class Place:
    def __init__(self, ns, nc):
        self.s = lax.axis_index("shard")
        self.c = lax.axis_index("ctx")
        self.t = lax.axis_index("tp")
        self.core = lax.rem(self.t, 2)
        self.y = self.t // 2
        self.mate_t = self.t + 1 - 2 * self.core
        self.ymate_t = lax.rem(self.t + 2, 4)
        self.mate = {"tp": self.mate_t}
        self.ymate = {"tp": self.ymate_t}
        self.zpeers = [{"ctx": lax.rem(self.c + k, nc)} for k in range(1, nc)]
        self.xpeers = [{"shard": lax.rem(self.s + r, ns)} for r in range(1, ns)]


class TpGather:
    def __init__(self, place, buf, sems):
        self.p, self.buf = place, buf
        self.ys, self.yr, self.ks, self.kr, self.fs, self.fr = sems

    def _y(self, b, i, src):
        p = self.p
        return remote(src, self.buf.at[b, p.t], self.ys.at[i], self.yr.at[i], p.ymate)

    def _k(self, b, i, src):
        p = self.p
        return remote(src, self.buf.at[b, p.t], self.ks.at[i], self.kr.at[i], p.mate)

    def _f(self, b, i):
        p = self.p
        piece = self.buf.at[b, p.ymate_t]
        return remote(piece, piece, self.fs.at[i], self.fr.at[i], p.mate)

    def send(self, b, i, src=None):
        src = self.buf.at[b, self.p.t] if src is None else src
        self._y(b, i, src).start()
        self._k(b, i, src).start()

    def forward(self, b, i):
        p = self.p
        piece = self.buf.at[b, p.ymate_t]
        remote(piece, piece, self.ys.at[i], self.yr.at[i], p.ymate).wait_recv()
        self._f(b, i).start()

    def arrive(self, b, i):
        p = self.p
        piece = self.buf.at[b, p.mate_t]
        remote(piece, piece, self.ks.at[i], self.kr.at[i], p.mate).wait_recv()
        piece = self.buf.at[b, lax.rem(p.mate_t + 2, 4)]
        remote(piece, piece, self.fs.at[i], self.fr.at[i], p.mate).wait_recv()

    def drain(self, b, i, src=None):
        src = self.buf.at[b, self.p.t] if src is None else src
        self._y(b, i, src).wait_send()
        self._k(b, i, src).wait_send()
        self._f(b, i).wait_send()


class TpReduce:
    def __init__(self, place, terms, from_mate, staged, from_y, sems):
        self.p, self.terms, self.from_mate, self.staged, self.from_y = (
            place,
            terms,
            from_mate,
            staged,
            from_y,
        )
        self.ks, self.kr, self.ys, self.yr = sems

    def _k(self, b):
        p = self.p
        return remote(
            self.terms.at[b, :, 1 - p.core],
            self.from_mate.at[b],
            self.ks.at[b],
            self.kr.at[b],
            p.mate,
        )

    def _y(self, b):
        return remote(
            self.staged.at[b], self.from_y.at[b], self.ys.at[b], self.yr.at[b], self.p.ymate
        )

    def send(self, b):
        self._k(b).start()

    def across(self, b):
        p = self.p
        self._k(b).wait_recv()
        other = 1 - p.y
        self.staged[b] = (
            self.terms[b, other, p.core].astype(F32) + self.from_mate[b, other].astype(F32)
        ).astype(BF)
        self._y(b).start()

    def result(self, b):
        p = self.p
        self._y(b).wait_recv()
        return (
            self.terms[b, p.y, p.core].astype(F32)
            + self.from_mate[b, p.y].astype(F32)
            + self.from_y[b].astype(F32)
        )

    def drain(self, b):
        self._k(b).wait_send()
        self._y(b).wait_send()


def column(row, width=128):
    return jnp.broadcast_to(row, (width, row.shape[-1])).T


def project_kernel(
    ns, nc, x_ref, type_ref, seg_ref, qw_ref, kvw_ref, ow_ref, dn_ref, qb_ref, vb_ref,
    xf_ref, q_ref, kv_ref, codef_ref, wf_ref, wo_ref, dnt_ref,
    wst, code, bias, local, zs, zr, ds, dr, ws, wr, *tp_sems,
):
    p = Place(ns, nc)
    piece = x_ref.shape[1] // 4
    heads = wst.shape[0] - 1
    for j in range(nc):
        label = seg_ref[j : j + 1]
        code[j] = jnp.where(type_ref[j : j + 1] == 0, label, -label).astype(F32)
    greet([p.mate, p.ymate] + p.zpeers + p.xpeers)
    mine = pl.ds(p.t * piece, piece)

    def x_send(k):
        peer = p.zpeers[k]
        return remote(
            x_ref.at[peer["ctx"], mine], xf_ref.at[p.c, p.t], zs.at[k], zr.at[k], peer
        )

    def code_send(k):
        peer = p.zpeers[k]
        return remote(code.at[peer["ctx"]], codef_ref.at[p.c], ds.at[k], dr.at[k], peer)

    def gathered(h, src):
        return wf_ref.at[h, src] if h < heads else wo_ref.at[src]

    def weight(h, r):
        return remote(wst.at[h], gathered(h, p.s), ws.at[h, r], wr.at[h, r], p.xpeers[r])

    def weight_landed(h):
        for r in range(ns - 1):
            landed = gathered(h, lax.rem(p.s + ns - 1 - r, ns))
            remote(landed, landed, ws.at[h, r], wr.at[h, r], p.xpeers[r]).wait_recv()

    for k in range(nc - 1):
        x_send(k).start()
    own = x_ref.at[p.c, mine]
    gather = TpGather(p, xf_ref, tp_sems)
    gather.send(p.c, 0, own)
    for h in range(heads):
        cols = slice(h * HEAD, (h + 1) * HEAD)
        parts = [qw_ref[k, cols] for k in range(4)] + [kvw_ref[k, cols] for k in range(2)]
        wst[h] = jnp.concatenate(parts, axis=0).T
        for r in range(ns - 1):
            weight(h, r).start()
    turned = ow_ref[...].T
    blank = jnp.zeros((turned.shape[0], HEAD), BF)
    parts = []
    for h in range(heads):
        parts += [blank, turned[:, h * HEAD : (h + 1) * HEAD]]
    wst[heads] = jnp.concatenate(parts, axis=1)
    for r in range(ns - 1):
        weight(heads, r).start()
    for k in range(nc - 1):
        code_send(k).start()
    copies = [
        pltpu.make_async_copy(own, xf_ref.at[p.c, p.t], local.at[0]),
        pltpu.make_async_copy(code.at[p.c], codef_ref.at[p.c], local.at[1]),
        pltpu.make_async_copy(wst.at[pl.ds(0, heads)], wf_ref.at[:, p.s], local.at[2]),
        pltpu.make_async_copy(wst.at[heads], wo_ref.at[p.s], local.at[3]),
    ]
    for copy in copies:
        copy.start()
    vb = vb_ref[...].reshape(1, -1)
    for h in range(heads):
        cols = slice(h * HEAD, (h + 1) * HEAD)
        parts = [qb_ref[k : k + 1, cols] for k in range(4)]
        bias[h] = jnp.concatenate(parts + [jnp.zeros((1, HEAD), F32), vb[:, cols]], axis=1)
    dnt_ref[...] = dn_ref[...].T
    blocks = [lax.rem(p.c + nc - k, nc) for k in range(nc)]
    for k in range(1, nc):
        landed = xf_ref.at[blocks[k], p.t]
        remote(landed, landed, zs.at[k - 1], zr.at[k - 1], p.zpeers[k - 1]).wait_recv()
        gather.send(blocks[k], k)
        gather.forward(blocks[k - 1], k - 1)
    gather.forward(blocks[nc - 1], nc - 1)
    for k in range(nc):
        gather.arrive(blocks[k], k)
    for k in range(nc - 1):
        landed = codef_ref.at[blocks[k + 1]]
        remote(landed, landed, ds.at[k], dr.at[k], p.zpeers[k]).wait_recv()
    for copy in copies:
        copy.wait()
    width = xf_ref.shape[-1]
    rows = 4 * piece
    for h in range(heads):
        weight_landed(h)

        def project(b, carry):
            x = xf_ref[b].reshape(rows, width)
            out = nn(x, wf_ref[h].reshape(width, 384)) + bias[h]
            entity = column(codef_ref[b]) < 0.0
            at = pl.ds(pl.multiple_of(b * rows, rows), rows)
            chosen = jnp.where(entity, out[:, 128:256], out[:, 0:128])
            q_ref[h, at] = (chosen * HEAD ** (-0.5)).astype(BF)
            kv_ref[h, at] = out[:, 256:384].astype(BF)
            return carry

        lax.fori_loop(0, nc, project, 0)
    weight_landed(heads)
    for h in range(heads + 1):
        for r in range(ns - 1):
            weight(h, r).wait_send()
    for k in range(nc - 1):
        x_send(k).wait_send()
        code_send(k).wait_send()
    gather.drain(p.c, 0, own)
    for k in range(1, nc):
        gather.drain(blocks[k], k)


def attend_kernel(q_ref, kv_ref, code_ref, e_ref, ctx_ref, inv_ref, kcat, vt, segcol):
    h, b = pl.program_id(0), pl.program_id(1)
    length = kv_ref.shape[1]
    nblk, rows = code_ref.shape[0], code_ref.shape[2]

    @pl.when((h == 0) & (b == 0))
    def _():
        for j in range(nblk):
            col = jnp.abs(column(code_ref[j]))
            segcol[j * rows : (j + 1) * rows] = jnp.where(col == 0.0, -1.0, col)

    @pl.when(b == 0)
    def _():
        low_half = lax.broadcasted_iota(jnp.int32, (rows, 128), 1) < HEAD
        for j in range(nblk):
            at = slice(j * rows, (j + 1) * rows)
            entity = column(code_ref[j]) < 0.0
            kv = kv_ref[0, at].astype(F32)
            turned = pltpu.roll(kv, HEAD, 1)
            keep = jnp.where(low_half, kv, turned)
            kcat[at] = jnp.where(low_half == entity, 0.0, keep).astype(BF)
            vt[:, at] = jnp.where(low_half, 0.0, kv).T.astype(BF)

    scores = nt(kcat[...], q_ref[0])
    segment = jnp.abs(code_ref[b])
    col = segcol[...]
    allowed = jnp.concatenate([col] * (rows // 128), axis=1) == segment
    scores = jnp.where(allowed, scores, MASKED)
    top = jnp.max(scores, axis=0, keepdims=True)
    top = jnp.where(top == MASKED, 0.0, top)
    exponent = jnp.exp(scores - top)
    inverse = 1.0 / jnp.maximum(jnp.sum(exponent, axis=0, keepdims=True), 1.0)
    exponent = exponent.astype(BF)
    e_ref[0] = exponent
    inv_ref[0] = inverse
    ctx_ref[...] = (nn(vt[...], exponent) * inverse).T.astype(BF)


def spread(values):
    average = jnp.mean(values, axis=-1, keepdims=True)
    centred = values - average
    inverse = lax.rsqrt(jnp.mean(centred * centred, axis=-1, keepdims=True) + EPS)
    return centred * inverse, inverse


def unspread(upstream, normed, inverse, gain):
    scaled = upstream * gain
    first = jnp.mean(scaled, axis=-1, keepdims=True)
    second = jnp.mean(scaled * normed, axis=-1, keepdims=True)
    return inverse * (scaled - first - normed * second)


def total(values):
    return jnp.sum(values, axis=0, keepdims=True)


SKEWS_C = (0, 1, 3, 4, 5, 6, 8, 9, 10, 11, 13, 14, 15)
FF_CHUNKS = 12
OUT_CHUNKS = 2
HEAD_CHUNKS = 3
OWN_LAG, PASS_LAG = 3, 6


def layer_kernel(
    ns, nc, ctx_ref, wo_ref, xf_ref, og_ref, wu_ref, wd_ref, *rest,
):
    vecs, rest = rest[:7], rest[7:]
    (
        wf_ref, code_ref, inv_ref, q_ref, kv_ref, e_ref,
        ing_ref, hidf_ref, dw_ref, sm_ref,
        ga, hid, gfi, small,
        wuf, wdf, ogo, hsend,
        t0, m0, s0, y0, t1, m1, s1, y1, t2, m2, s2, y2,
        low, gf, active, slope, gup, fo, fh, fi, gs,
        dctx, kcat, dkey, dval, dqkv, qb, ebuf, dqo,
        ig, zo, zr, zq, xr, smt, smz, smx,
        local, ws, wr, os, orr, hs, hr,
        es, xs, xrs, z1s, z1r, z2s, z2r, z3s, z3r, z4s, z4r, igs, igr,
        ss, sr, szs, szr, sxs, sxr, *tp_sems,
    ) = rest
    p = Place(ns, nc)
    piece, width = xf_ref.shape[2:]
    rows = 4 * piece
    length = nc * rows
    heads = q_ref.shape[0]
    steps = heads * nc
    chunks = dw_ref.shape[0]
    back = slope

    def fetch(i):
        return pltpu.make_async_copy(e_ref.at[i], ebuf.at[lax.rem(i, 2)], es.at[lax.rem(i, 2)])

    fetch(0).start()
    greet([p.mate, p.ymate] + p.zpeers + p.xpeers)
    weights = ((wu_ref, wuf), (wd_ref, wdf))

    def weight(a, r):
        src, dst = weights[a]
        return remote(src, dst.at[p.s], ws.at[a, r], wr.at[a, r], p.xpeers[r])

    for a in range(2):
        for r in range(ns - 1):
            weight(a, r).start()
    mine = pl.ds(p.t * piece, piece)

    def og_send(k):
        peer = p.zpeers[k]
        return remote(og_ref.at[peer["ctx"], mine], ogo.at[p.c], os.at[k], orr.at[k], peer)

    for k in range(nc - 1):
        og_send(k).start()
    copies = [
        pltpu.make_async_copy(og_ref.at[p.c, mine], ogo.at[p.c], local.at[0]),
        pltpu.make_async_copy(wu_ref, wuf.at[p.s], local.at[1]),
        pltpu.make_async_copy(wd_ref, wdf.at[p.s], local.at[2]),
    ]
    for copy in copies:
        copy.start()
    small[...] = jnp.zeros_like(small)

    sums = [
        TpReduce(p, *bufs, [tp_sems[j].at[i] for j in range(4)])
        for i, bufs in enumerate(
            ((t0, m0, s0, y0), (t1, m1, s1, y1), (t2, m2, s2, y2), (t0, m0, s0, y0))
        )
    ]
    shares = [
        TpGather(p, buf, [tp_sems[4 + j].at[i] for j in range(6)])
        for i, buf in enumerate((low, gf, ga, hidf_ref, ing_ref))
    ]
    back_sum, share_h, share_g = sums[3], shares[3], shares[4]
    out_bias, gain1, bias1, up_bias, down_bias, gain2, bias2 = (
        ref[...].reshape(1, -1) for ref in vecs
    )


    def x_send(lo, n, r):
        peer = p.xpeers[r]
        return remote(
            dqo.at[pl.ds(lo, n), peer["shard"]],
            xr.at[r, pl.ds(lo, n)],
            xs.at[lo, r],
            xrs.at[lo, r],
            peer,
        )

    outer = (p.c == 0) | (p.c == nc - 1)
    inner = (p.c > 0) & (p.c < nc - 1)
    inward = {"ctx": 1 + p.c // 3}
    outward = {"ctx": lax.rem(3 * (p.c + nc - 1), 6)}
    across = {"ctx": lax.rem(2 * nc - 1 - p.c, nc)}

    def to_inner(k):
        return remote(zo.at[k], zr.at[k], z1s.at[k], z1r.at[k], inward)

    def to_owner(k):
        return remote(zq.at[k], zq.at[k], z2s.at[k], z2r.at[k], across)

    def to_other(k):
        return remote(dw_ref.at[k], dw_ref.at[k], z3s.at[k], z3r.at[k], across)

    def to_outer(k):
        return remote(dw_ref.at[k], dw_ref.at[k], z4s.at[k], z4r.at[k], outward)

    def owns(k):
        return lax.rem(k + p.c, 2) == 1

    def line_start(lo, n):
        for r in range(ns - 1):
            x_send(lo, n, r).wait_recv()
        for k in range(lo, lo + n):
            grad = dqo[k, p.s].astype(F32)
            for r in range(ns - 1):
                grad = grad + xr[r, k].astype(F32)
            zo[k] = grad.astype(BF)

            @pl.when(outer)
            def _(k=k):
                to_inner(k).start()

    def line_in(k):
        to_inner(k).wait_recv()

        @pl.when(jnp.logical_not(owns(k)))
        def _():
            zq[k] = (zo[k].astype(F32) + zr[k].astype(F32)).astype(BF)
            to_owner(k).start()

    def line_own(k):
        @pl.when(owns(k))
        def _():
            to_owner(k).wait_recv()
            dw_ref[k] = (zo[k].astype(F32) + zr[k].astype(F32) + zq[k].astype(F32)).astype(BF)
            to_other(k).start()
            to_outer(k).start()

    def line_pass(k):
        @pl.when(jnp.logical_not(owns(k)))
        def _():
            to_other(k).wait_recv()
            to_outer(k).start()

    reached = [0]

    def line(upto):
        lo = reached[0]
        reached[0] = upto

        @pl.when(inner)
        def _():
            for k in range(lo, upto):
                if k < chunks:
                    line_in(k)
                if 0 <= k - OWN_LAG < chunks:
                    line_own(k - OWN_LAG)
                if 0 <= k - PASS_LAG < chunks:
                    line_pass(k - PASS_LAG)

    def line_end(k):
        @pl.when(outer)
        def _():
            to_outer(k).wait_recv()
            to_inner(k).wait_send()

        @pl.when(inner)
        def _():
            @pl.when(owns(k))
            def _():
                to_other(k).wait_send()

            @pl.when(jnp.logical_not(owns(k)))
            def _():
                to_owner(k).wait_send()

            to_outer(k).wait_send()

    sizes = [HEAD_CHUNKS] * 4 + [OUT_CHUNKS] + [HEAD_CHUNKS] * heads
    groups = [(sum(sizes[:g]), n) for g, n in enumerate(sizes)]

    def start(g):
        line_start(*groups[g])

    def put_grad(lo, n, value):
        for j in range(n):
            dqo[lo + j] = value[:, j * 128 : (j + 1) * 128].reshape(dqo.shape[1:])
        for r in range(ns - 1):
            x_send(lo, n, r).start()


    def put(terms, b, values):
        terms[b] = values.astype(BF).reshape(2, 2, piece, width)

    def add_small(row, values):
        small[row : row + 1] += total(values)

    def block_rows(b):
        return pl.ds(pl.multiple_of(b * rows, rows), rows)

    def out_project(b):
        put(t0, b, nt(ctx_ref[block_rows(b)], wo_ref[...].reshape(width, -1)))
        sums[0].send(b)

    def norm_one(b):
        h = xf_ref[b, p.t].astype(F32) + (sums[0].result(b) + out_bias)
        normed, inverse = spread(h)
        first = normed * gain1 + bias1
        fo[b] = first
        fh[b] = normed
        fi[b] = inverse
        low[b, p.t] = first.astype(BF)
        shares[0].send(b, b)

    def feed_forward(b):
        @pl.when(b == 0)
        def _():
            for a in range(2):
                for r in range(ns - 1):
                    landed = weights[a][1].at[lax.rem(p.s + ns - 1 - r, ns)]
                    remote(landed, landed, ws.at[a, r], wr.at[a, r], p.xpeers[r]).wait_recv()
            for copy in copies[1:]:
                copy.wait()

        shares[0].arrive(b, b)
        up = nn(low[b].reshape(rows, width), wuf[...].reshape(width, -1)) + up_bias
        cdf = 0.5 * (1.0 + lax.erf(up * ROOT_HALF))
        act = (up * cdf).astype(BF)
        active[b] = act
        slope[b] = cdf + up * (jnp.exp(-0.5 * up * up) * INV_ROOT_TWO_PI)
        put(t1, b, nt(act, wdf[...].reshape(width, -1)))
        sums[1].send(b)

    def hid_send(b):
        return remote(hsend.at[b], hid.at[p.c], hs.at[b], hr.at[p.c], {"ctx": b})

    def norm_two(b):
        @pl.when(b == 0)
        def _():
            for k in range(nc - 1):
                landed = ogo.at[lax.rem(p.c + nc - 1 - k, nc)]
                remote(landed, landed, os.at[k], orr.at[k], p.zpeers[k]).wait_recv()
            copies[0].wait()

        normed, inverse = spread(fo[b] + (sums[1].result(b) + down_bias))
        hsend[b] = (normed * gain2 + bias2).astype(BF)

        upstream = ogo[b].astype(F32)
        add_small(2, upstream * normed)
        add_small(3, upstream)
        grad = unspread(upstream, normed, inverse, gain2)
        gs[b] = grad
        grad = grad.astype(BF)
        gf[b, p.t] = grad
        add_small(5, grad.astype(F32))
        shares[1].send(b, b)

        @pl.when(b != p.c)
        def _():
            hid_send(b).start()

        @pl.when(b == p.c)
        def _():
            pltpu.make_async_copy(hsend.at[b], hid.at[p.c], local.at[3]).start()

    def feed_back(b):
        shares[1].arrive(b, b)
        grad = nn(gf[b].reshape(rows, width), wdf[...].reshape(width, -1))
        grad = (grad.astype(BF).astype(F32) * slope[b]).astype(BF)
        gup[b] = grad
        add_small(6, grad.astype(F32))
        put(t2, b, nt(grad, wuf[...].reshape(width, -1)))
        sums[2].send(b)

    def norm_back(b):
        grad = gs[b] + sums[2].result(b)
        add_small(0, grad * fh[b])
        add_small(1, grad)
        grad = unspread(grad, fh[b], fi[b], gain1)
        gfi[b] = grad
        grad = grad.astype(BF)
        ga[b, p.t] = grad
        add_small(4, grad.astype(F32))
        shares[2].send(b, b)

    stages = (
        out_project,
        sums[0].across,
        norm_one,
        lambda b: shares[0].forward(b, b),
        feed_forward,
        sums[1].across,
        norm_two,
        lambda b: shares[1].forward(b, b),
        feed_back,
        sums[2].across,
        norm_back,
        lambda b: shares[2].forward(b, b),
        lambda b: shares[2].arrive(b, b),
    )

    half = HEAD_CHUNKS * 128

    def weight_grad(g):
        left = (gf, low)[g // 2][...].reshape(length, width)
        right = (active, gup)[g // 2][:, :, half * (g % 2) : half * (g % 2 + 1)]
        put_grad(*groups[g], tn(left, right.reshape(length, half)).astype(BF))

    def run_at(step, events):
        for when, action in events.items():

            @pl.when(step == when)
            def _(action=action):
                action()

    full = SKEWS_C[8] + nc - 1
    feed_events = {
        full: lambda: (weight_grad(0), weight_grad(1)),
        full + 1: lambda: (weight_grad(2), weight_grad(3)),
        full + 2: lambda: start(0),
        full + 3: lambda: line(1),
        full + 4: lambda: (start(1), line(3)),
        full + 5: lambda: line(4),
    }

    def feed_slot(step, carry):
        for skew, stage in zip(SKEWS_C, stages):
            b = step - skew

            @pl.when((b >= 0) & (b < nc))
            def _(stage=stage, b=b):
                stage(b)

        run_at(step, feed_events)
        return carry

    lax.fori_loop(0, SKEWS_C[-1] + nc, feed_slot, 0)


    def small_tp(i, peer):
        return remote(smt.at[2 * i], smt.at[2 * i + 1], ss.at[i], sr.at[i], peer)

    shared = lax.broadcasted_iota(jnp.int32, smt.shape[1:], 0) < 6

    def small_fold(i):
        return smt[2 * i] + jnp.where(shared, smt[2 * i + 1], 0.0)

    def small_z(k):
        return remote(smz.at[p.c], smz.at[p.c], szs.at[k], szr.at[k], p.zpeers[k])

    def small_x(r):
        return remote(smx.at[p.s], smx.at[p.s], sxs.at[r], sxr.at[r], p.xpeers[r])

    def small_zero():
        smt[0] = jnp.zeros_like(smt[0])
        smt[0, :, 0:width] = small[...]
        for h in range(heads):
            smt[0, 7:8, h * 384 : (h + 1) * 384] = qb[h]
        small_tp(0, p.mate).start()

    def small_one():
        small_tp(0, p.mate).wait_recv()
        smt[2] = small_fold(0)
        small_tp(1, p.ymate).start()

    def small_two():
        small_tp(1, p.ymate).wait_recv()
        smz[p.c] = small_fold(1)
        for k in range(nc - 1):
            small_z(k).start()

    def small_three():
        for k in range(nc - 1):
            landed = smz.at[lax.rem(p.c + nc - 1 - k, nc)]
            remote(landed, landed, szs.at[k], szr.at[k], p.zpeers[k]).wait_recv()
        value = smz[0]
        for k in range(1, nc):
            value = value + smz[k]
        smx[p.s] = value
        for r in range(ns - 1):
            small_x(r).start()

    def small_four():
        for r in range(ns - 1):
            landed = smx.at[lax.rem(p.s + ns - 1 - r, ns)]
            remote(landed, landed, sxs.at[r], sxr.at[r], p.xpeers[r]).wait_recv()
        value = smx[0]
        for r in range(1, ns):
            value = value + smx[r]
        sm_ref[...] = value


    def grad_send(b):
        return remote(ig.at[b], ing_ref.at[p.c, p.t], igs.at[b], igr.at[p.c], {"ctx": b})

    def grad_own(b):
        ig[b] = (gfi[b] + back_sum.result(b)).astype(BF)

        @pl.when(b != p.c)
        def _():
            grad_send(b).start()

        @pl.when(b == p.c)
        def _():
            pltpu.make_async_copy(ig.at[b], ing_ref.at[p.c, p.t], local.at[4]).start()

    order = [lax.rem(p.c + k, nc) for k in range(nc)]

    def grad_share(k):
        q = order[k]
        if k > 0:
            landed = ing_ref.at[q, p.t]
            remote(landed, landed, igs.at[q], igr.at[q], {"ctx": q}).wait_recv()
        else:
            pltpu.make_async_copy(ig.at[p.c], ing_ref.at[p.c, p.t], local.at[4]).wait()
        share_g.send(q, k)


    for k in range(1, nc):
        src = lax.rem(p.c + k, nc)
        landed = hid.at[src]
        remote(landed, landed, hs.at[src], hr.at[src], p.zpeers[k - 1]).wait_recv()
        hid_send(src).wait_send()
    pltpu.make_async_copy(hsend.at[p.c], hid.at[p.c], local.at[3]).wait()
    for b in range(nc):
        share_h.send(b, b, hid.at[b])
    keep = pltpu.make_async_copy(hid, hidf_ref.at[:, p.t], local.at[5])
    keep.start()
    for b in range(nc):
        sums[0].drain(b)
    grad_attn = ga[...].reshape(length, width)
    out = wo_ref[...].reshape(width, heads * 128)
    for i in range(heads):
        dctx[i] = nn(grad_attn, out[:, i * 128 : (i + 1) * 128]).astype(BF)
    value = tn(grad_attn, ctx_ref[...]).astype(BF)
    value = [value[:, i * 128 + HEAD : (i + 1) * 128] for i in range(heads)]
    put_grad(*groups[4], jnp.concatenate(value + [jnp.zeros_like(value[0])], axis=1))
    back[...] = jnp.zeros_like(back)
    low_half = lax.broadcasted_iota(jnp.int32, (rows, 128), 1) < HEAD

    def attend_step(i):
        h, b = i // nc, lax.rem(i, nc)
        fetch(i).wait()

        @pl.when(i + 1 < steps)
        def _():
            fetch(i + 1).start()

        @pl.when(b == 0)
        def _():
            for j in range(nc):
                at = slice(j * rows, (j + 1) * rows)
                entity = column(code_ref[j]) < 0.0
                kv = kv_ref[h, at].astype(F32)
                kept = jnp.where(low_half, kv, pltpu.roll(kv, HEAD, 1))
                kcat[at] = jnp.where(low_half == entity, 0.0, kept).astype(BF)
            dkey[...] = jnp.zeros_like(dkey)
            dval[...] = jnp.zeros_like(dval)

        at = block_rows(b)
        lanes = pl.ds(pl.multiple_of(h * 128, 128), 128)
        grad_ctx = dctx[h, at].astype(F32).T * inv_ref[i]
        row_dot = jnp.sum(grad_ctx * ctx_ref[at, lanes].astype(F32).T, axis=0, keepdims=True)
        grad_ctx = grad_ctx.astype(BF)
        weight = ebuf[lax.rem(i, 2)]
        grad = nn(kv_ref[h], grad_ctx)
        grad = (weight.astype(F32) * (grad - row_dot)).astype(BF)
        dval[...] += nt(weight, grad_ctx)
        dkey[...] += nn(grad, q_ref[h, at])
        grad_q = tn(kcat[...], grad).T * HEAD ** (-0.5)
        entity = column(code_ref[b]) < 0.0
        dqkv[at, 0:128] = jnp.where(entity, 0.0, grad_q).astype(BF)
        dqkv[at, 128:256] = jnp.where(entity, grad_q, 0.0).astype(BF)

        @pl.when(b == nc - 1)
        def _():
            for j in range(nc):
                part = slice(j * rows, (j + 1) * rows)
                entity = column(code_ref[j]) < 0.0
                grad_k = dkey[part]
                grad_k = jnp.where(entity, pltpu.roll(grad_k, HEAD, 1), grad_k)
                dqkv[part, 256:384] = jnp.where(low_half, grad_k, dval[part]).astype(BF)
            w = wf_ref[h].reshape(width, 384)

            @pl.when(h < heads - 1)
            def _():
                for j in range(nc):
                    back[j] += nt(dqkv[j * rows : (j + 1) * rows], w)

            @pl.when(h == heads - 1)
            def _():
                for j in range(nc):
                    put(t0, j, back[j] + nt(dqkv[j * rows : (j + 1) * rows], w))
                    back_sum.send(j)

            grads = dqkv[...]
            value = tn(xf_ref[...].reshape(length, width), grads).astype(BF)
            put_grad(FF_CHUNKS + OUT_CHUNKS + HEAD_CHUNKS * h, HEAD_CHUNKS, value)
            qb[h] = total(grads.astype(F32))

    def forward_hidden():
        for b in range(nc):
            share_h.forward(b, b)

    def hand(k):
        share_g.forward(order[k], k)

    start(2)
    line(5)
    events = {
        0: lambda: line(6),
        1: lambda: line(7),
        3: lambda: (forward_hidden(), start(3), line(8)),
        5: lambda: line(9),
        6: lambda: line(10),
        7: lambda: line(11),
        8: lambda: line(12),
        9: lambda: start(4),
        10: lambda: line(13),
        11: lambda: line(14),
    }

    def slot(i, carry):
        attend_step(i)
        run_at(i, events)
        return carry

    lax.fori_loop(0, steps, slot, 0)
    for b in range(nc):
        back_sum.across(b)
    small_zero()
    start(5)
    line(15)
    grad_own(0)
    grad_own(1)
    line(16)
    grad_own(2)
    small_one()
    line(17)
    grad_own(3)
    start(6)
    line(18)
    small_two()
    grad_share(0)
    grad_share(1)
    line(19)
    start(7)
    grad_share(2)
    hand(0)
    line(20)
    grad_share(3)
    hand(1)
    small_three()
    line(21)
    hand(2)
    hand(3)
    small_four()
    line(chunks + PASS_LAG)
    for b in range(nc):
        share_h.arrive(b, b)
        share_g.arrive(order[b], b)
    for k in range(chunks):
        line_end(k)
    keep.wait()
    for lo, n in groups:
        for r in range(ns - 1):
            x_send(lo, n, r).wait_send()
    for b in range(nc):
        for i in range(1, 4):
            sums[i].drain(b)
        for i in range(3):
            shares[i].drain(b, b)
        share_h.drain(b, b, hid.at[b])
        share_g.drain(order[b], b)

        @pl.when(b != p.c)
        def _(b=b):
            grad_send(b).wait_send()

    for a in range(2):
        for r in range(ns - 1):
            weight(a, r).wait_send()
    for k in range(nc - 1):
        og_send(k).wait_send()
    small_tp(0, p.mate).wait_send()
    small_tp(1, p.ymate).wait_send()
    for k in range(nc - 1):
        small_z(k).wait_send()
    for r in range(ns - 1):
        small_x(r).wait_send()


def deliver_kernel(
    ing_ref, hid_ref, dw_ref, sm_ref,
    hidden_ref, grad_ref, qw_ref, kvw_ref, qb_ref, vb_ref, ow_ref, uw_ref, dn_ref, *vec_refs,
):
    hidden_ref[...] = hid_ref[...]
    grad_ref[...] = ing_ref[...].astype(F32)

    @pl.when(pl.program_id(0) == 0)
    def _():
        def wide(lo, n):
            return jnp.concatenate([dw_ref[lo + j].astype(F32) for j in range(n)], axis=1)

        uw_ref[...] = wide(6, 6)
        dn_ref[...] = wide(0, 6).T
        heads = qb_ref.shape[1] // HEAD
        ow_ref[...] = wide(FF_CHUNKS, OUT_CHUNKS)[:, : heads * HEAD].T
        first = FF_CHUNKS + OUT_CHUNKS
        grads = [wide(first + HEAD_CHUNKS * h, HEAD_CHUNKS).T for h in range(heads)]
        small = sm_ref[...]
        for k in range(6):
            cols = slice(k * HEAD, (k + 1) * HEAD)
            part = jnp.concatenate([grad[cols] for grad in grads], axis=0)
            vec = jnp.concatenate(
                [
                    small[7:8, h * 384 + k * HEAD : h * 384 + (k + 1) * HEAD]
                    for h in range(heads)
                ],
                axis=1,
            )
            if k < 4:
                qw_ref[k] = part
                qb_ref[k : k + 1] = vec
            else:
                kvw_ref[k - 4] = part
            if k == 5:
                vb_ref[...] = vec.reshape(-1)
        width = uw_ref.shape[1]
        for i, ref in enumerate(vec_refs):
            ref[...] = small[i : i + 1, :width].reshape(-1)


def vmem(count):
    return [pl.BlockSpec(memory_space=pltpu.VMEM)] * count


def struct(shape, dtype):
    return jax.ShapeDtypeStruct(shape, dtype)


def params(collective_id=None):
    if collective_id is None:
        return pltpu.CompilerParams(
            vmem_limit_bytes=VMEM_LIMIT, dimension_semantics=("arbitrary", "arbitrary")
        )
    return pltpu.CompilerParams(
        vmem_limit_bytes=VMEM_LIMIT, collective_id=collective_id, has_side_effects=True
    )


TP_GATHER = 6
TP_REDUCE = 4


def per_device(
    hidden_in,
    token_type,
    segment,
    query_weight,
    key_value_weight,
    query_bias,
    value_bias,
    out_weight,
    out_bias,
    norm1_gain,
    norm1_bias,
    up_weight,
    up_bias,
    down_weight,
    down_bias,
    norm2_gain,
    norm2_bias,
    out_grad,
):
    ns, nc = lax.axis_size("shard"), lax.axis_size("ctx")
    seqs, local_len, width = hidden_in.shape
    part = query_weight.shape[2]
    heads = part // HEAD
    shard_rows = query_weight.shape[1]
    ff = up_weight.shape[1]
    piece = local_len // 4
    length = nc * local_len
    assert seqs == nc == 4 and heads == 3 and ff == width
    wide = ns - 1

    mixed = OUT_CHUNKS + HEAD_CHUNKS * heads
    line = (FF_CHUNKS + mixed, shard_rows, 128)
    xf, q, kv, code, wf, wo, down_t = pl.pallas_call(
        functools.partial(project_kernel, ns, nc),
        out_shape=(
            struct((nc, 4, piece, width), BF),
            struct((heads, length, 128), BF),
            struct((heads, length, 128), BF),
            struct((nc, 1, local_len), F32),
            struct((heads, ns, shard_rows, 384), BF),
            struct((ns, shard_rows, 384), BF),
            struct((shard_rows, ff), BF),
        ),
        in_specs=vmem(9),
        out_specs=vmem(7),
        scratch_shapes=[
            pltpu.VMEM((heads + 1, shard_rows, 384), BF),
            pltpu.VMEM((nc, 1, local_len), F32),
            pltpu.VMEM((heads, 1, 384), F32),
            DMA((4,)),
        ]
        + [DMA((nc - 1,))] * 4
        + [DMA((heads + 1, wide))] * 2
        + [DMA((nc,))] * TP_GATHER,
        compiler_params=params(0),
        name="project",
    )(
        hidden_in,
        token_type,
        segment,
        query_weight.swapaxes(1, 2),
        key_value_weight.swapaxes(1, 2),
        out_weight,
        down_weight,
        query_bias,
        value_bias,
    )

    grid = (heads, nc)
    e_spec = pl.BlockSpec((1, length, local_len), lambda h, b: (h * nc + b, 0, 0))
    inv_spec = pl.BlockSpec((1, 1, local_len), lambda h, b: (h * nc + b, 0, 0))
    ctx_spec = pl.BlockSpec((local_len, 128), lambda h, b: (b, h))
    q_spec = pl.BlockSpec((1, local_len, 128), lambda h, b: (h, b, 0))
    kv_spec = pl.BlockSpec((1, length, 128), lambda h, b: (h, 0, 0))

    def whole(shape):
        return pl.BlockSpec(shape, lambda h, b: (0,) * len(shape))

    e, ctx, inv = pl.pallas_call(
        attend_kernel,
        grid=grid,
        out_shape=(
            struct((heads * nc, length, local_len), BF),
            struct((length, heads * 128), BF),
            struct((heads * nc, 1, local_len), F32),
        ),
        in_specs=[q_spec, kv_spec, whole((nc, 1, local_len))],
        out_specs=(e_spec, ctx_spec, inv_spec),
        scratch_shapes=[
            pltpu.VMEM((length, 128), BF),
            pltpu.VMEM((128, length), BF),
            pltpu.VMEM((length, 128), F32),
        ],
        compiler_params=params(),
        name="attend",
    )(q, kv, code)

    full = pltpu.VMEM((nc, 4, piece, width), BF)
    own = pltpu.VMEM((nc, piece, width), BF)
    own32 = pltpu.VMEM((nc, piece, width), F32)
    reduce_bufs = [
        pltpu.VMEM((nc, 2, 2, piece, width), BF),
        pltpu.VMEM((nc, 2, piece, width), BF),
        own,
        own,
    ]
    rows_ff = pltpu.VMEM((nc, local_len, ff), BF)
    total_chunks = line[0]
    chunks = pltpu.VMEM(line, BF)
    wide_small = heads * 384
    hbm = [pl.BlockSpec(memory_space=pl.ANY)]
    ing, hid, dw, small = pl.pallas_call(
        functools.partial(layer_kernel, ns, nc),
        out_shape=(
            struct((nc, 4, piece, width), BF),
            struct((nc, 4, piece, width), BF),
            struct(line, BF),
            struct((8, wide_small), F32),
        ),
        in_specs=vmem(3) + hbm * 3 + vmem(12) + hbm,
        out_specs=vmem(4),
        scratch_shapes=[
            full,
            own,
            own32,
            pltpu.VMEM((8, width), F32),
            pltpu.VMEM((ns, shard_rows, ff), BF),
            pltpu.VMEM((ns, shard_rows, ff), BF),
            own,
            own,
        ]
        + reduce_bufs * 3
        + [
            full,
            full,
            rows_ff,
            pltpu.VMEM((nc, local_len, ff), F32),
            rows_ff,
            own32,
            own32,
            pltpu.VMEM((nc, piece, 1), F32),
            own32,
            pltpu.VMEM((heads, length, 128), BF),
            pltpu.VMEM((length, 128), BF),
            pltpu.VMEM((length, 128), F32),
            pltpu.VMEM((length, 128), F32),
            pltpu.VMEM((length, 384), BF),
            pltpu.VMEM((heads, 1, 384), F32),
            pltpu.VMEM((2, length, local_len), BF),
            pltpu.VMEM((total_chunks, ns, shard_rows, 128), BF),
            own,
        ]
        + [chunks] * 3
        + [
            pltpu.VMEM((wide, total_chunks, shard_rows, 128), BF),
            pltpu.VMEM((4, 8, wide_small), F32),
            pltpu.VMEM((nc, 8, wide_small), F32),
            pltpu.VMEM((ns, 8, wide_small), F32),
            DMA((6,)),
        ]
        + [DMA((2, wide))] * 2
        + [DMA((nc - 1,))] * 2
        + [DMA((nc,))] * 2
        + [DMA((2,))]
        + [DMA((total_chunks, wide))] * 2
        + [DMA((total_chunks,))] * 8
        + [DMA((nc,))] * 2
        + [DMA((2,))] * 2
        + [DMA((nc - 1,))] * 2
        + [DMA((wide,))] * 2
        + [DMA((4, nc))] * TP_REDUCE
        + [DMA((5, nc))] * TP_GATHER,
        compiler_params=params(1),
        name="layer",
    )(
        ctx,
        wo,
        xf,
        out_grad,
        up_weight,
        down_t,
        out_bias,
        norm1_gain,
        norm1_bias,
        up_bias,
        down_bias,
        norm2_gain,
        norm2_bias,
        wf,
        code,
        inv,
        q,
        kv,
        e,
    )

    def block(*shape):
        return pl.BlockSpec(shape, lambda i: (i,) + (0,) * (len(shape) - 1))

    def fixed(*shape):
        return pl.BlockSpec(shape, lambda i: (0,) * len(shape))

    def vector(size):
        return pl.BlockSpec((size,), lambda i: (0,))

    (
        hidden_out,
        in_grad,
        qw,
        kvw,
        qb,
        vb,
        ow,
        uw,
        dn,
        gain1,
        bias1,
        gain2,
        bias2,
        ob,
        db,
        ub,
    ) = pl.pallas_call(
        deliver_kernel,
        grid=(nc,),
        out_shape=(
            struct((nc, local_len, width), BF),
            struct((nc, local_len, width), F32),
            struct((4, part, shard_rows), F32),
            struct((2, part, shard_rows), F32),
            struct((4, part), F32),
            struct((part,), F32),
            struct((part, shard_rows), F32),
            struct((shard_rows, ff), F32),
            struct((ff, shard_rows), F32),
        )
        + (struct((width,), F32),) * 7,
        in_specs=[
            block(1, local_len, width),
            block(1, local_len, width),
            fixed(*line),
            fixed(8, wide_small),
        ],
        out_specs=[
            block(1, local_len, width),
            block(1, local_len, width),
            fixed(4, part, shard_rows),
            fixed(2, part, shard_rows),
            fixed(4, part),
            vector(part),
            fixed(part, shard_rows),
            fixed(shard_rows, ff),
            fixed(ff, shard_rows),
        ]
        + [vector(width)] * 7,
        compiler_params=pltpu.CompilerParams(
            vmem_limit_bytes=VMEM_LIMIT, dimension_semantics=("arbitrary",)
        ),
        name="deliver",
    )(ing.reshape(nc, local_len, width), hid.reshape(nc, local_len, width), dw, small)
    return (
        hidden_out,
        in_grad,
        qw.swapaxes(1, 2),
        kvw.swapaxes(1, 2),
        qb,
        vb,
        ow,
        ob,
        gain1,
        bias1,
        uw,
        ub,
        dn,
        db,
        gain2,
        bias2,
    )


def solution(mesh):
    in_specs = (
        P("shard", "ctx", None),
        P("shard", "ctx"),
        P("shard", "ctx"),
        P(None, "shard", "tp"),
        P(None, "shard", "tp"),
        P(None, "tp"),
        P("tp"),
        P("tp", "shard"),
        P(),
        P(),
        P(),
        P("shard", "tp"),
        P("tp"),
        P("tp", "shard"),
        P(),
        P(),
        P(),
        P("shard", "ctx", None),
    )
    out_specs = (
        P("shard", "ctx", None),
        P("shard", "ctx", None),
        P(None, "shard", "tp"),
        P(None, "shard", "tp"),
        P(None, "tp"),
        P("tp"),
        P("tp", "shard"),
        P(),
        P(),
        P(),
        P("shard", "tp"),
        P("tp"),
        P("tp", "shard"),
        P(),
        P(),
        P(),
    )
    return jax.shard_map(
        per_device, mesh=mesh, in_specs=in_specs, out_specs=out_specs, check_vma=False
    )
```

```python
import functools

import jax
import jax.numpy as jnp
from jax import lax
from jax.experimental import pallas as pl
from jax.experimental.pallas import tpu as pltpu
from jax.sharding import PartitionSpec as P

BF = jnp.bfloat16
F32 = jnp.float32
HEAD = 64
EPS = 1e-05
MASKED = -1e30
ROOT_HALF = 0.7071067811865476
INV_ROOT_TWO_PI = 0.3989422804014327
VMEM_LIMIT = 66 * 1024 * 1000
MESH = pl.DeviceIdType.MESH
DMA = pltpu.SemaphoreType.DMA


def nn(left, right):
    return lax.dot_general(left, right, (((1,), (0,)), ((), ())), preferred_element_type=F32)


def nt(left, right):
    return lax.dot_general(left, right, (((1,), (1,)), ((), ())), preferred_element_type=F32)


def tn(left, right):
    return lax.dot_general(left, right, (((0,), (0,)), ((), ())), preferred_element_type=F32)


def remote(src, dst, send_sem, recv_sem, peer):
    return pltpu.make_async_remote_copy(
        src_ref=src,
        dst_ref=dst,
        send_sem=send_sem,
        recv_sem=recv_sem,
        device_id=peer,
        device_id_type=MESH,
    )


def greet(peers):
    barrier = pltpu.get_barrier_semaphore()
    for peer in peers:
        pl.semaphore_signal(barrier, inc=1, device_id=peer, device_id_type=MESH)
    pl.semaphore_wait(barrier, len(peers))


class Place:
    def __init__(self, ns, nc):
        self.s = lax.axis_index("shard")
        self.c = lax.axis_index("ctx")
        self.t = lax.axis_index("tp")
        self.core = lax.rem(self.t, 2)
        self.y = self.t // 2
        self.mate_t = self.t + 1 - 2 * self.core
        self.ymate_t = lax.rem(self.t + 2, 4)
        self.mate = {"tp": self.mate_t}
        self.ymate = {"tp": self.ymate_t}
        self.zpeers = [{"ctx": lax.rem(self.c + k, nc)} for k in range(1, nc)]
        self.xpeers = [{"shard": lax.rem(self.s + r, ns)} for r in range(1, ns)]


class TpGather:
    def __init__(self, place, buf, sems):
        self.p, self.buf = place, buf
        self.ys, self.yr, self.ks, self.kr, self.fs, self.fr = sems

    def _y(self, b, i, src):
        p = self.p
        return remote(src, self.buf.at[b, p.t], self.ys.at[i], self.yr.at[i], p.ymate)

    def _k(self, b, i, src):
        p = self.p
        return remote(src, self.buf.at[b, p.t], self.ks.at[i], self.kr.at[i], p.mate)

    def _f(self, b, i):
        p = self.p
        piece = self.buf.at[b, p.ymate_t]
        return remote(piece, piece, self.fs.at[i], self.fr.at[i], p.mate)

    def send(self, b, i, src=None):
        src = self.buf.at[b, self.p.t] if src is None else src
        self._y(b, i, src).start()
        self._k(b, i, src).start()

    def forward(self, b, i):
        p = self.p
        piece = self.buf.at[b, p.ymate_t]
        remote(piece, piece, self.ys.at[i], self.yr.at[i], p.ymate).wait_recv()
        self._f(b, i).start()

    def arrive(self, b, i):
        p = self.p
        piece = self.buf.at[b, p.mate_t]
        remote(piece, piece, self.ks.at[i], self.kr.at[i], p.mate).wait_recv()
        piece = self.buf.at[b, lax.rem(p.mate_t + 2, 4)]
        remote(piece, piece, self.fs.at[i], self.fr.at[i], p.mate).wait_recv()

    def drain(self, b, i, src=None):
        src = self.buf.at[b, self.p.t] if src is None else src
        self._y(b, i, src).wait_send()
        self._k(b, i, src).wait_send()
        self._f(b, i).wait_send()


class TpReduce:
    def __init__(self, place, terms, from_mate, staged, from_y, sems):
        self.p, self.terms, self.from_mate, self.staged, self.from_y = (
            place,
            terms,
            from_mate,
            staged,
            from_y,
        )
        self.ks, self.kr, self.ys, self.yr = sems

    def _k(self, b):
        p = self.p
        return remote(
            self.terms.at[b, :, 1 - p.core],
            self.from_mate.at[b],
            self.ks.at[b],
            self.kr.at[b],
            p.mate,
        )

    def _y(self, b):
        return remote(
            self.staged.at[b], self.from_y.at[b], self.ys.at[b], self.yr.at[b], self.p.ymate
        )

    def send(self, b):
        self._k(b).start()

    def across(self, b):
        p = self.p
        self._k(b).wait_recv()
        other = 1 - p.y
        self.staged[b] = (
            self.terms[b, other, p.core].astype(F32) + self.from_mate[b, other].astype(F32)
        ).astype(BF)
        self._y(b).start()

    def result(self, b):
        p = self.p
        self._y(b).wait_recv()
        return (
            self.terms[b, p.y, p.core].astype(F32)
            + self.from_mate[b, p.y].astype(F32)
            + self.from_y[b].astype(F32)
        )

    def drain(self, b):
        self._k(b).wait_send()
        self._y(b).wait_send()


def column(row, width=128):
    return jnp.broadcast_to(row, (width, row.shape[-1])).T


def project_kernel(
    ns, nc, x_ref, type_ref, seg_ref, qw_ref, kvw_ref, ow_ref, dn_ref, qb_ref, vb_ref, wu_ref,
    xf_ref, q_ref, kv_ref, codef_ref, wf_ref, wo_ref, dnt_ref, wuf_ref, ctx_ref, inv_ref, e_ref,
    wst, code, bias, kcat, vt, segcol, ebuf,
    local, zs, zr, ds, dr, ws, wr, us, ur, es, *tp_sems,
):
    p = Place(ns, nc)
    piece = x_ref.shape[1] // 4
    heads = wst.shape[0] - 1
    for j in range(nc):
        label = seg_ref[j : j + 1]
        code[j] = jnp.where(type_ref[j : j + 1] == 0, label, -label).astype(F32)
    greet([p.mate, p.ymate] + p.zpeers + p.xpeers)
    mine = pl.ds(p.t * piece, piece)

    def x_send(k):
        peer = p.zpeers[k]
        return remote(
            x_ref.at[peer["ctx"], mine], xf_ref.at[p.c, p.t], zs.at[k], zr.at[k], peer
        )

    def code_send(k):
        peer = p.zpeers[k]
        return remote(code.at[peer["ctx"]], codef_ref.at[p.c], ds.at[k], dr.at[k], peer)

    def gathered(h, src):
        return wo_ref.at[src] if isinstance(h, int) and h == heads else wf_ref.at[h, src]

    def weight(h, r):
        return remote(wst.at[h], gathered(h, p.s), ws.at[h, r], wr.at[h, r], p.xpeers[r])

    def weight_landed(h):
        for r in range(ns - 1):
            landed = gathered(h, lax.rem(p.s + ns - 1 - r, ns))
            remote(landed, landed, ws.at[h, r], wr.at[h, r], p.xpeers[r]).wait_recv()

    for k in range(nc - 1):
        x_send(k).start()
    own = x_ref.at[p.c, mine]
    gather = TpGather(p, xf_ref, tp_sems)
    gather.send(p.c, 0, own)
    for h in range(heads):
        cols = slice(h * HEAD, (h + 1) * HEAD)
        parts = [qw_ref[k, cols] for k in range(4)] + [kvw_ref[k, cols] for k in range(2)]
        wst[h] = jnp.concatenate(parts, axis=0).T
        for r in range(ns - 1):
            weight(h, r).start()
    turned = ow_ref[...].T
    blank = jnp.zeros((turned.shape[0], HEAD), BF)
    parts = []
    for h in range(heads):
        parts += [blank, turned[:, h * HEAD : (h + 1) * HEAD]]
    wst[heads] = jnp.concatenate(parts, axis=1)
    for r in range(ns - 1):
        weight(heads, r).start()

    def up_send(r):
        return remote(wu_ref, wuf_ref.at[p.s], us.at[r], ur.at[r], p.xpeers[r])

    for r in range(ns - 1):
        up_send(r).start()
    for k in range(nc - 1):
        code_send(k).start()
    copies = [
        pltpu.make_async_copy(own, xf_ref.at[p.c, p.t], local.at[0]),
        pltpu.make_async_copy(code.at[p.c], codef_ref.at[p.c], local.at[1]),
        pltpu.make_async_copy(wst.at[pl.ds(0, heads)], wf_ref.at[:, p.s], local.at[2]),
        pltpu.make_async_copy(wst.at[heads], wo_ref.at[p.s], local.at[3]),
        pltpu.make_async_copy(wu_ref, wuf_ref.at[p.s], local.at[4]),
    ]
    for copy in copies:
        copy.start()
    vb = vb_ref[...].reshape(1, -1)
    for h in range(heads):
        cols = slice(h * HEAD, (h + 1) * HEAD)
        parts = [qb_ref[k : k + 1, cols] for k in range(4)]
        bias[h] = jnp.concatenate(parts + [jnp.zeros((1, HEAD), F32), vb[:, cols]], axis=1)
    dnt_ref[...] = dn_ref[...].T
    blocks = [lax.rem(p.c + nc - k, nc) for k in range(nc)]
    for k in range(1, nc):
        landed = xf_ref.at[blocks[k], p.t]
        remote(landed, landed, zs.at[k - 1], zr.at[k - 1], p.zpeers[k - 1]).wait_recv()
        gather.send(blocks[k], k)
        gather.forward(blocks[k - 1], k - 1)
    gather.forward(blocks[nc - 1], nc - 1)
    for k in range(nc):
        gather.arrive(blocks[k], k)
    for k in range(nc - 1):
        landed = codef_ref.at[blocks[k + 1]]
        remote(landed, landed, ds.at[k], dr.at[k], p.zpeers[k]).wait_recv()
    for copy in copies:
        copy.wait()
    width = xf_ref.shape[-1]
    rows = 4 * piece
    length = nc * rows
    for j in range(nc):
        col = jnp.abs(column(codef_ref[j]))
        segcol[j * rows : (j + 1) * rows] = jnp.where(col == 0.0, -1.0, col)
    low_half = lax.broadcasted_iota(jnp.int32, (rows, 128), 1) < HEAD

    def e_out(i):
        slot = lax.rem(i, 2)
        return pltpu.make_async_copy(ebuf.at[slot], e_ref.at[i], es.at[slot])

    def head_step(h, carry):
        weight_landed(h)

        def project(b, carry):
            x = xf_ref[b].reshape(rows, width)
            out = nn(x, wf_ref[h].reshape(width, 384)) + bias[h]
            entity = column(codef_ref[b]) < 0.0
            at = pl.ds(pl.multiple_of(b * rows, rows), rows)
            chosen = jnp.where(entity, out[:, 128:256], out[:, 0:128])
            q_ref[h, at] = (chosen * HEAD ** (-0.5)).astype(BF)
            kv = out[:, 256:384].astype(BF)
            kv_ref[h, at] = kv
            kv = kv.astype(F32)
            turned = pltpu.roll(kv, HEAD, 1)
            keep = jnp.where(low_half, kv, turned)
            kcat[at] = jnp.where(low_half == entity, 0.0, keep).astype(BF)
            vt[:, at] = jnp.where(low_half, 0.0, kv).T.astype(BF)
            return carry

        lax.fori_loop(0, nc, project, 0)

        def attend(b, carry):
            i = h * nc + b
            at = pl.ds(pl.multiple_of(b * rows, rows), rows)
            scores = nt(kcat[...], q_ref[h, at])
            segment = jnp.abs(codef_ref[b])
            allowed = jnp.concatenate([segcol[...]] * (rows // 128), axis=1) == segment
            scores = jnp.where(allowed, scores, MASKED)
            top = jnp.max(scores, axis=0, keepdims=True)
            top = jnp.where(top == MASKED, 0.0, top)
            exponent = jnp.exp(scores - top)
            inverse = 1.0 / jnp.maximum(jnp.sum(exponent, axis=0, keepdims=True), 1.0)
            exponent = exponent.astype(BF)

            @pl.when(i >= 2)
            def _():
                e_out(i - 2).wait()

            ebuf[lax.rem(i, 2)] = exponent
            e_out(i).start()
            inv_ref[i] = inverse
            lanes = pl.ds(pl.multiple_of(h * 128, 128), 128)
            ctx_ref[at, lanes] = (nn(vt[...], exponent) * inverse).T.astype(BF)
            return carry

        lax.fori_loop(0, nc, attend, 0)
        return carry

    lax.fori_loop(0, heads, head_step, 0)
    for i in range(heads * nc - 2, heads * nc):
        e_out(i).wait()
    for r in range(ns - 1):
        landed = wuf_ref.at[lax.rem(p.s + ns - 1 - r, ns)]
        remote(landed, landed, us.at[r], ur.at[r], p.xpeers[r]).wait_recv()
    weight_landed(heads)
    for h in range(heads + 1):
        for r in range(ns - 1):
            weight(h, r).wait_send()
    for r in range(ns - 1):
        up_send(r).wait_send()
    for k in range(nc - 1):
        x_send(k).wait_send()
        code_send(k).wait_send()
    gather.drain(p.c, 0, own)
    for k in range(1, nc):
        gather.drain(blocks[k], k)


def spread(values):
    average = jnp.mean(values, axis=-1, keepdims=True)
    centred = values - average
    inverse = lax.rsqrt(jnp.mean(centred * centred, axis=-1, keepdims=True) + EPS)
    return centred * inverse, inverse


def unspread(upstream, normed, inverse, gain):
    scaled = upstream * gain
    first = jnp.mean(scaled, axis=-1, keepdims=True)
    second = jnp.mean(scaled * normed, axis=-1, keepdims=True)
    return inverse * (scaled - first - normed * second)


def total(values):
    return jnp.sum(values, axis=0, keepdims=True)


SKEWS_C = (0, 1, 3, 4, 5, 6, 8, 9, 10, 11, 13, 14, 15)
FF_CHUNKS = 12
OUT_CHUNKS = 2
HEAD_CHUNKS = 3
FIRST_SUM, CHUNK, HOP = -30.0, 2.1, 5.5
STEP_ENDS = (-29.0, -25.0, -22.0, -20.0)
BACK_START, BACK_STEP = -17.0, 1.42


def layer_kernel(
    ns, nc, ctx_ref, wo_ref, xf_ref, wuf, og_ref, wd_ref, *rest,
):
    vecs, rest = rest[:7], rest[7:]
    (
        wf_ref, code_ref, inv_ref, q_ref, kv_ref, e_ref,
        ing_ref, hidf_ref, dw_ref, sm_ref,
        ga, hid, gfi, small,
        wdf, ogo, hsend,
        t0, m0, s0, y0, t1, m1, s1, y1, t2, m2, s2, y2,
        low, gf, active, slope, gup, fo, fh, fi, gs,
        dctx, kcat, dkey, dval, dqkv, qb, ebuf, dqo,
        ig, zo, zr, zq, xr, smt, smz, smx,
        local, ws, wr, os, orr, hs, hr,
        es, xs, xrs, z1s, z1r, z2s, z2r, z3s, z3r, z4s, z4r, igs, igr,
        ss, sr, szs, szr, sxs, sxr, *tp_sems,
    ) = rest
    p = Place(ns, nc)
    piece, width = xf_ref.shape[2:]
    rows = 4 * piece
    length = nc * rows
    heads = q_ref.shape[0]
    steps = heads * nc
    chunks = dw_ref.shape[0]
    back = slope

    def fetch(i):
        return pltpu.make_async_copy(e_ref.at[i], ebuf.at[lax.rem(i, 2)], es.at[lax.rem(i, 2)])

    fetch(0).start()
    greet([p.mate, p.ymate] + p.zpeers + p.xpeers)

    def down_send(r):
        return remote(wd_ref, wdf.at[p.s], ws.at[r], wr.at[r], p.xpeers[r])

    for r in range(ns - 1):
        down_send(r).start()
    mine = pl.ds(p.t * piece, piece)

    def og_send(k):
        peer = p.zpeers[k]
        return remote(og_ref.at[peer["ctx"], mine], ogo.at[p.c], os.at[k], orr.at[k], peer)

    for k in range(nc - 1):
        og_send(k).start()
    copies = [
        pltpu.make_async_copy(og_ref.at[p.c, mine], ogo.at[p.c], local.at[0]),
        pltpu.make_async_copy(wd_ref, wdf.at[p.s], local.at[1]),
    ]
    for copy in copies:
        copy.start()
    small[...] = jnp.zeros_like(small)

    sums = [
        TpReduce(p, *bufs, [tp_sems[j].at[i] for j in range(4)])
        for i, bufs in enumerate(
            ((t0, m0, s0, y0), (t1, m1, s1, y1), (t2, m2, s2, y2), (t0, m0, s0, y0))
        )
    ]
    shares = [
        TpGather(p, buf, [tp_sems[4 + j].at[i] for j in range(6)])
        for i, buf in enumerate((low, gf, ga, hidf_ref, ing_ref))
    ]
    back_sum, share_h, share_g = sums[3], shares[3], shares[4]
    out_bias, gain1, bias1, up_bias, down_bias, gain2, bias2 = (
        ref[...].reshape(1, -1) for ref in vecs
    )


    def x_send(k, r):
        peer = p.xpeers[r]
        return remote(dqo.at[k, peer["shard"]], xr.at[r, k], xs.at[k, r], xrs.at[k, r], peer)

    outer = (p.c == 0) | (p.c == nc - 1)
    inner = (p.c > 0) & (p.c < nc - 1)
    inward = {"ctx": 1 + p.c // 3}
    outward = {"ctx": lax.rem(3 * (p.c + nc - 1), 6)}
    across = {"ctx": lax.rem(2 * nc - 1 - p.c, nc)}

    def to_inner(k):
        return remote(zo.at[k], zr.at[k], z1s.at[k], z1r.at[k], inward)

    def to_owner(k):
        return remote(zq.at[k], zq.at[k], z2s.at[k], z2r.at[k], across)

    def to_other(k):
        return remote(dw_ref.at[k], dw_ref.at[k], z3s.at[k], z3r.at[k], across)

    def to_outer(k):
        return remote(dw_ref.at[k], dw_ref.at[k], z4s.at[k], z4r.at[k], outward)

    def owns(k):
        return lax.rem(k + p.c, 2) == 1

    def line_start(k):
        grad = dqo[k, p.s].astype(F32)
        for r in range(ns - 1):
            x_send(k, r).wait_recv()
            grad = grad + xr[r, k].astype(F32)
        zo[k] = grad.astype(BF)

        @pl.when(outer)
        def _():
            to_inner(k).start()

    def line_in(k):
        @pl.when(inner)
        def _():
            to_inner(k).wait_recv()

        @pl.when(inner & jnp.logical_not(owns(k)))
        def _():
            zq[k] = (zo[k].astype(F32) + zr[k].astype(F32)).astype(BF)
            to_owner(k).start()

    def line_own(k):
        @pl.when(inner & owns(k))
        def _():
            to_owner(k).wait_recv()
            dw_ref[k] = (zo[k].astype(F32) + zr[k].astype(F32) + zq[k].astype(F32)).astype(BF)
            to_other(k).start()
            to_outer(k).start()

    def line_pass(k):
        @pl.when(inner & jnp.logical_not(owns(k)))
        def _():
            to_other(k).wait_recv()
            to_outer(k).start()

    plan = []
    for k in range(chunks):
        for hop, action in enumerate((line_start, line_in, line_own, line_pass)):
            plan.append((FIRST_SUM + CHUNK * k + HOP * hop, functools.partial(action, k)))

    def due(after, until):
        stretch = [entry for entry in plan if after < entry[0] <= until]
        return [action for _, action in sorted(stretch, key=lambda entry: entry[0])]

    def run(actions):
        for action in actions:
            action()

    def line_end(k):
        @pl.when(outer)
        def _():
            to_outer(k).wait_recv()
            to_inner(k).wait_send()

        @pl.when(inner)
        def _():
            @pl.when(owns(k))
            def _():
                to_other(k).wait_send()

            @pl.when(jnp.logical_not(owns(k)))
            def _():
                to_owner(k).wait_send()

            to_outer(k).wait_send()

    sizes = [HEAD_CHUNKS] * 4 + [OUT_CHUNKS] + [HEAD_CHUNKS] * heads
    groups = [(sum(sizes[:g]), n) for g, n in enumerate(sizes)]

    def put_grad(lo, n, value):
        for j in range(n):
            dqo[lo + j] = value[:, j * 128 : (j + 1) * 128].reshape(dqo.shape[1:])
            for r in range(ns - 1):
                x_send(lo + j, r).start()


    def put(terms, b, values):
        terms[b] = values.astype(BF).reshape(2, 2, piece, width)

    def add_small(row, values):
        small[row : row + 1] += total(values)

    def block_rows(b):
        return pl.ds(pl.multiple_of(b * rows, rows), rows)

    def out_project(b):
        put(t0, b, nt(ctx_ref[block_rows(b)], wo_ref[...].reshape(width, -1)))
        sums[0].send(b)

    def norm_one(b):
        h = xf_ref[b, p.t].astype(F32) + (sums[0].result(b) + out_bias)
        normed, inverse = spread(h)
        first = normed * gain1 + bias1
        fo[b] = first
        fh[b] = normed
        fi[b] = inverse
        low[b, p.t] = first.astype(BF)
        shares[0].send(b, b)

    def feed_forward(b):
        shares[0].arrive(b, b)
        up = nn(low[b].reshape(rows, width), wuf[...].reshape(width, -1)) + up_bias
        cdf = 0.5 * (1.0 + lax.erf(up * ROOT_HALF))
        act = (up * cdf).astype(BF)
        active[b] = act
        slope[b] = cdf + up * (jnp.exp(-0.5 * up * up) * INV_ROOT_TWO_PI)

        @pl.when(b == 0)
        def _():
            for r in range(ns - 1):
                landed = wdf.at[lax.rem(p.s + ns - 1 - r, ns)]
                remote(landed, landed, ws.at[r], wr.at[r], p.xpeers[r]).wait_recv()
            copies[1].wait()

        put(t1, b, nt(active[b], wdf[...].reshape(width, -1)))
        sums[1].send(b)

    def hid_send(b):
        return remote(hsend.at[b], hid.at[p.c], hs.at[b], hr.at[p.c], {"ctx": b})

    def norm_two(b):
        @pl.when(b == 0)
        def _():
            for k in range(nc - 1):
                landed = ogo.at[lax.rem(p.c + nc - 1 - k, nc)]
                remote(landed, landed, os.at[k], orr.at[k], p.zpeers[k]).wait_recv()
            copies[0].wait()

        normed, inverse = spread(fo[b] + (sums[1].result(b) + down_bias))
        hsend[b] = (normed * gain2 + bias2).astype(BF)

        upstream = ogo[b].astype(F32)
        add_small(2, upstream * normed)
        add_small(3, upstream)
        grad = unspread(upstream, normed, inverse, gain2)
        gs[b] = grad
        grad = grad.astype(BF)
        gf[b, p.t] = grad
        add_small(5, grad.astype(F32))
        shares[1].send(b, b)

        @pl.when(b != p.c)
        def _():
            hid_send(b).start()

        @pl.when(b == p.c)
        def _():
            pltpu.make_async_copy(hsend.at[b], hid.at[p.c], local.at[3]).start()

    def feed_back(b):
        shares[1].arrive(b, b)
        grad = nn(gf[b].reshape(rows, width), wdf[...].reshape(width, -1))
        grad = (grad.astype(BF).astype(F32) * slope[b]).astype(BF)
        gup[b] = grad
        add_small(6, grad.astype(F32))
        put(t2, b, nt(grad, wuf[...].reshape(width, -1)))
        sums[2].send(b)

    def norm_back(b):
        grad = gs[b] + sums[2].result(b)
        add_small(0, grad * fh[b])
        add_small(1, grad)
        grad = unspread(grad, fh[b], fi[b], gain1)
        gfi[b] = grad
        grad = grad.astype(BF)
        ga[b, p.t] = grad
        add_small(4, grad.astype(F32))
        shares[2].send(b, b)

    stages = (
        out_project,
        sums[0].across,
        norm_one,
        lambda b: shares[0].forward(b, b),
        feed_forward,
        sums[1].across,
        norm_two,
        lambda b: shares[1].forward(b, b),
        feed_back,
        sums[2].across,
        norm_back,
        lambda b: shares[2].forward(b, b),
        lambda b: shares[2].arrive(b, b),
    )

    half = HEAD_CHUNKS * 128

    def weight_grad(g):
        left = (gf, low)[g // 2][...].reshape(length, width)
        right = (active, gup)[g // 2][:, :, half * (g % 2) : half * (g % 2 + 1)]
        put_grad(*groups[g], tn(left, right.reshape(length, half)).astype(BF))

    def run_at(step, events):
        for when, action in events.items():

            @pl.when(step == when)
            def _(action=action):
                action()

    full = SKEWS_C[8] + nc - 1
    ends = (-100.0,) + STEP_ENDS
    feed_events = {
        full + 2 + j: functools.partial(run, due(ends[j], ends[j + 1])) for j in range(4)
    }
    feed_events[full] = lambda: (weight_grad(0), weight_grad(1))
    feed_events[full + 1] = lambda: (weight_grad(2), weight_grad(3))

    def feed_slot(step, carry):
        for skew, stage in zip(SKEWS_C, stages):
            b = step - skew

            @pl.when((b >= 0) & (b < nc))
            def _(stage=stage, b=b):
                stage(b)

        run_at(step, feed_events)
        return carry

    lax.fori_loop(0, SKEWS_C[-1] + nc, feed_slot, 0)


    def small_tp(i, peer):
        return remote(smt.at[2 * i], smt.at[2 * i + 1], ss.at[i], sr.at[i], peer)

    shared = lax.broadcasted_iota(jnp.int32, smt.shape[1:], 0) < 6

    def small_fold(i):
        return smt[2 * i] + jnp.where(shared, smt[2 * i + 1], 0.0)

    def small_z(k):
        return remote(smz.at[p.c], smz.at[p.c], szs.at[k], szr.at[k], p.zpeers[k])

    def small_x(r):
        return remote(smx.at[p.s], smx.at[p.s], sxs.at[r], sxr.at[r], p.xpeers[r])

    def small_zero():
        smt[0] = jnp.zeros_like(smt[0])
        smt[0, :, 0:width] = small[...]
        for h in range(heads):
            smt[0, 7:8, h * 384 : (h + 1) * 384] = qb[h]
        small_tp(0, p.mate).start()

    def small_one():
        small_tp(0, p.mate).wait_recv()
        smt[2] = small_fold(0)
        small_tp(1, p.ymate).start()

    def small_two():
        small_tp(1, p.ymate).wait_recv()
        smz[p.c] = small_fold(1)
        for k in range(nc - 1):
            small_z(k).start()

    def small_three():
        for k in range(nc - 1):
            landed = smz.at[lax.rem(p.c + nc - 1 - k, nc)]
            remote(landed, landed, szs.at[k], szr.at[k], p.zpeers[k]).wait_recv()
        value = smz[0]
        for k in range(1, nc):
            value = value + smz[k]
        smx[p.s] = value
        for r in range(ns - 1):
            small_x(r).start()

    def small_four():
        for r in range(ns - 1):
            landed = smx.at[lax.rem(p.s + ns - 1 - r, ns)]
            remote(landed, landed, sxs.at[r], sxr.at[r], p.xpeers[r]).wait_recv()
        value = smx[0]
        for r in range(1, ns):
            value = value + smx[r]
        sm_ref[...] = value


    def grad_send(b):
        return remote(ig.at[b], ing_ref.at[p.c, p.t], igs.at[b], igr.at[p.c], {"ctx": b})

    def grad_own(b):
        ig[b] = (gfi[b] + back_sum.result(b)).astype(BF)

        @pl.when(b != p.c)
        def _():
            grad_send(b).start()

        @pl.when(b == p.c)
        def _():
            pltpu.make_async_copy(ig.at[b], ing_ref.at[p.c, p.t], local.at[4]).start()

    order = [lax.rem(p.c + k, nc) for k in range(nc)]

    def grad_share(k):
        q = order[k]
        if k > 0:
            landed = ing_ref.at[q, p.t]
            remote(landed, landed, igs.at[q], igr.at[q], {"ctx": q}).wait_recv()
        else:
            pltpu.make_async_copy(ig.at[p.c], ing_ref.at[p.c, p.t], local.at[4]).wait()
        share_g.send(q, k)


    for k in range(1, nc):
        src = lax.rem(p.c + k, nc)
        landed = hid.at[src]
        remote(landed, landed, hs.at[src], hr.at[src], p.zpeers[k - 1]).wait_recv()
        hid_send(src).wait_send()
    pltpu.make_async_copy(hsend.at[p.c], hid.at[p.c], local.at[3]).wait()
    for b in range(nc):
        share_h.send(b, b, hid.at[b])
    keep = pltpu.make_async_copy(hid, hidf_ref.at[:, p.t], local.at[5])
    keep.start()
    for b in range(nc):
        sums[0].drain(b)
    grad_attn = ga[...].reshape(length, width)
    out = wo_ref[...].reshape(width, heads * 128)
    for i in range(heads):
        dctx[i] = nn(grad_attn, out[:, i * 128 : (i + 1) * 128]).astype(BF)
    value = tn(grad_attn, ctx_ref[...]).astype(BF)
    value = [value[:, i * 128 + HEAD : (i + 1) * 128] for i in range(heads)]
    put_grad(*groups[4], jnp.concatenate(value + [jnp.zeros_like(value[0])], axis=1))
    back[...] = jnp.zeros_like(back)
    low_half = lax.broadcasted_iota(jnp.int32, (rows, 128), 1) < HEAD

    def attend_step(i):
        h, b = i // nc, lax.rem(i, nc)
        fetch(i).wait()

        @pl.when(i + 1 < steps)
        def _():
            fetch(i + 1).start()

        @pl.when(b == 0)
        def _():
            for j in range(nc):
                at = slice(j * rows, (j + 1) * rows)
                entity = column(code_ref[j]) < 0.0
                kv = kv_ref[h, at].astype(F32)
                kept = jnp.where(low_half, kv, pltpu.roll(kv, HEAD, 1))
                kcat[at] = jnp.where(low_half == entity, 0.0, kept).astype(BF)
            dkey[...] = jnp.zeros_like(dkey)
            dval[...] = jnp.zeros_like(dval)

        at = block_rows(b)
        lanes = pl.ds(pl.multiple_of(h * 128, 128), 128)
        grad_ctx = dctx[h, at].astype(F32).T * inv_ref[i]
        row_dot = jnp.sum(grad_ctx * ctx_ref[at, lanes].astype(F32).T, axis=0, keepdims=True)
        grad_ctx = grad_ctx.astype(BF)
        weight = ebuf[lax.rem(i, 2)]
        grad = nn(kv_ref[h], grad_ctx)
        grad = (weight.astype(F32) * (grad - row_dot)).astype(BF)
        dval[...] += nt(weight, grad_ctx)
        dkey[...] += nn(grad, q_ref[h, at])
        grad_q = tn(kcat[...], grad).T * HEAD ** (-0.5)
        entity = column(code_ref[b]) < 0.0
        dqkv[at, 0:128] = jnp.where(entity, 0.0, grad_q).astype(BF)
        dqkv[at, 128:256] = jnp.where(entity, grad_q, 0.0).astype(BF)

        @pl.when(b == nc - 1)
        def _():
            for j in range(nc):
                part = slice(j * rows, (j + 1) * rows)
                entity = column(code_ref[j]) < 0.0
                grad_k = dkey[part]
                grad_k = jnp.where(entity, pltpu.roll(grad_k, HEAD, 1), grad_k)
                dqkv[part, 256:384] = jnp.where(low_half, grad_k, dval[part]).astype(BF)
            w = wf_ref[h].reshape(width, 384)

            @pl.when(h < heads - 1)
            def _():
                for j in range(nc):
                    back[j] += nt(dqkv[j * rows : (j + 1) * rows], w)

            @pl.when(h == heads - 1)
            def _():
                for j in range(nc):
                    put(t0, j, back[j] + nt(dqkv[j * rows : (j + 1) * rows], w))
                    back_sum.send(j)

            grads = dqkv[...]
            value = tn(xf_ref[...].reshape(length, width), grads).astype(BF)
            put_grad(FF_CHUNKS + OUT_CHUNKS + HEAD_CHUNKS * h, HEAD_CHUNKS, value)
            qb[h] = total(grads.astype(F32))

    def forward_hidden():
        for b in range(nc):
            share_h.forward(b, b)

    def hand(k):
        share_g.forward(order[k], k)

    run(due(STEP_ENDS[-1], BACK_START))
    ends = [BACK_START + BACK_STEP * i for i in range(steps + 1)]
    events = {i: functools.partial(run, due(ends[i], ends[i + 1])) for i in range(steps)}
    events[3] = lambda: (forward_hidden(), run(due(ends[3], ends[4])))

    def slot(i, carry):
        attend_step(i)
        run_at(i, events)
        return carry

    lax.fori_loop(0, steps, slot, 0)
    for b in range(nc):
        plan += [
            (2.0 + 0.5 * b, functools.partial(back_sum.across, b)),
            (6.5 + 2.0 * b, functools.partial(grad_own, b)),
            (13.0 + 1.0 * b, functools.partial(grad_share, b)),
            (18.0 + 2.0 * b, functools.partial(hand, b)),
        ]
    plan += [(3.8, small_zero), (7.0, small_one), (14.5, small_two), (19.5, small_three)]
    plan += [(25.0, small_four)]
    run(due(ends[-1], 1000.0))
    for b in range(nc):
        share_h.arrive(b, b)
        share_g.arrive(order[b], b)
    for k in range(chunks):
        line_end(k)
    keep.wait()
    for k in range(chunks):
        for r in range(ns - 1):
            x_send(k, r).wait_send()
    for b in range(nc):
        for i in range(1, 4):
            sums[i].drain(b)
        for i in range(3):
            shares[i].drain(b, b)
        share_h.drain(b, b, hid.at[b])
        share_g.drain(order[b], b)

        @pl.when(b != p.c)
        def _(b=b):
            grad_send(b).wait_send()

    for r in range(ns - 1):
        down_send(r).wait_send()
    for k in range(nc - 1):
        og_send(k).wait_send()
    small_tp(0, p.mate).wait_send()
    small_tp(1, p.ymate).wait_send()
    for k in range(nc - 1):
        small_z(k).wait_send()
    for r in range(ns - 1):
        small_x(r).wait_send()


def deliver_kernel(
    ing_ref, hid_ref, dw_ref, sm_ref,
    hidden_ref, grad_ref, qw_ref, kvw_ref, qb_ref, vb_ref, ow_ref, uw_ref, dn_ref, *vec_refs,
):
    hidden_ref[...] = hid_ref[...]
    grad_ref[...] = ing_ref[...].astype(F32)

    @pl.when(pl.program_id(0) == 0)
    def _():
        def wide(lo, n):
            return jnp.concatenate([dw_ref[lo + j].astype(F32) for j in range(n)], axis=1)

        uw_ref[...] = wide(6, 6)
        dn_ref[...] = wide(0, 6).T
        heads = qb_ref.shape[1] // HEAD
        ow_ref[...] = wide(FF_CHUNKS, OUT_CHUNKS)[:, : heads * HEAD].T
        first = FF_CHUNKS + OUT_CHUNKS
        grads = [wide(first + HEAD_CHUNKS * h, HEAD_CHUNKS).T for h in range(heads)]
        small = sm_ref[...]
        for k in range(6):
            cols = slice(k * HEAD, (k + 1) * HEAD)
            part = jnp.concatenate([grad[cols] for grad in grads], axis=0)
            vec = jnp.concatenate(
                [
                    small[7:8, h * 384 + k * HEAD : h * 384 + (k + 1) * HEAD]
                    for h in range(heads)
                ],
                axis=1,
            )
            if k < 4:
                qw_ref[k] = part
                qb_ref[k : k + 1] = vec
            else:
                kvw_ref[k - 4] = part
            if k == 5:
                vb_ref[...] = vec.reshape(-1)
        width = uw_ref.shape[1]
        for i, ref in enumerate(vec_refs):
            ref[...] = small[i : i + 1, :width].reshape(-1)


def vmem(count):
    return [pl.BlockSpec(memory_space=pltpu.VMEM)] * count


def struct(shape, dtype):
    return jax.ShapeDtypeStruct(shape, dtype)


def params(collective_id):
    return pltpu.CompilerParams(
        vmem_limit_bytes=VMEM_LIMIT, collective_id=collective_id, has_side_effects=True
    )


TP_GATHER = 6
TP_REDUCE = 4


def per_device(
    hidden_in,
    token_type,
    segment,
    query_weight,
    key_value_weight,
    query_bias,
    value_bias,
    out_weight,
    out_bias,
    norm1_gain,
    norm1_bias,
    up_weight,
    up_bias,
    down_weight,
    down_bias,
    norm2_gain,
    norm2_bias,
    out_grad,
):
    ns, nc = lax.axis_size("shard"), lax.axis_size("ctx")
    seqs, local_len, width = hidden_in.shape
    part = query_weight.shape[2]
    heads = part // HEAD
    shard_rows = query_weight.shape[1]
    ff = up_weight.shape[1]
    piece = local_len // 4
    length = nc * local_len
    assert seqs == nc == 4 and heads == 3 and ff == width
    wide = ns - 1

    mixed = OUT_CHUNKS + HEAD_CHUNKS * heads
    line = (FF_CHUNKS + mixed, shard_rows, 128)
    hbm = [pl.BlockSpec(memory_space=pl.ANY)]
    xf, q, kv, code, wf, wo, down_t, wuf, ctx, inv, e = pl.pallas_call(
        functools.partial(project_kernel, ns, nc),
        out_shape=(
            struct((nc, 4, piece, width), BF),
            struct((heads, length, 128), BF),
            struct((heads, length, 128), BF),
            struct((nc, 1, local_len), F32),
            struct((heads, ns, shard_rows, 384), BF),
            struct((ns, shard_rows, 384), BF),
            struct((shard_rows, ff), BF),
            struct((ns, shard_rows, ff), BF),
            struct((length, heads * 128), BF),
            struct((heads * nc, 1, local_len), F32),
            struct((heads * nc, length, local_len), BF),
        ),
        in_specs=vmem(9) + hbm,
        out_specs=vmem(10) + hbm,
        scratch_shapes=[
            pltpu.VMEM((heads + 1, shard_rows, 384), BF),
            pltpu.VMEM((nc, 1, local_len), F32),
            pltpu.VMEM((heads, 1, 384), F32),
            pltpu.VMEM((length, 128), BF),
            pltpu.VMEM((128, length), BF),
            pltpu.VMEM((length, 128), F32),
            pltpu.VMEM((2, length, local_len), BF),
            DMA((5,)),
        ]
        + [DMA((nc - 1,))] * 4
        + [DMA((heads + 1, wide))] * 2
        + [DMA((wide,))] * 2
        + [DMA((2,))]
        + [DMA((nc,))] * TP_GATHER,
        compiler_params=params(0),
        name="project",
    )(
        hidden_in,
        token_type,
        segment,
        query_weight.swapaxes(1, 2),
        key_value_weight.swapaxes(1, 2),
        out_weight,
        down_weight,
        query_bias,
        value_bias,
        up_weight,
    )

    full = pltpu.VMEM((nc, 4, piece, width), BF)
    own = pltpu.VMEM((nc, piece, width), BF)
    own32 = pltpu.VMEM((nc, piece, width), F32)
    reduce_bufs = [
        pltpu.VMEM((nc, 2, 2, piece, width), BF),
        pltpu.VMEM((nc, 2, piece, width), BF),
        own,
        own,
    ]
    rows_ff = pltpu.VMEM((nc, local_len, ff), BF)
    total_chunks = line[0]
    chunks = pltpu.VMEM(line, BF)
    wide_small = heads * 384
    ing, hid, dw, small = pl.pallas_call(
        functools.partial(layer_kernel, ns, nc),
        out_shape=(
            struct((nc, 4, piece, width), BF),
            struct((nc, 4, piece, width), BF),
            struct(line, BF),
            struct((8, wide_small), F32),
        ),
        in_specs=vmem(4) + hbm * 2 + vmem(12) + hbm,
        out_specs=vmem(4),
        scratch_shapes=[
            full,
            own,
            own32,
            pltpu.VMEM((8, width), F32),
            pltpu.VMEM((ns, shard_rows, ff), BF),
            own,
            own,
        ]
        + reduce_bufs * 3
        + [
            full,
            full,
            rows_ff,
            pltpu.VMEM((nc, local_len, ff), F32),
            rows_ff,
            own32,
            own32,
            pltpu.VMEM((nc, piece, 1), F32),
            own32,
            pltpu.VMEM((heads, length, 128), BF),
            pltpu.VMEM((length, 128), BF),
            pltpu.VMEM((length, 128), F32),
            pltpu.VMEM((length, 128), F32),
            pltpu.VMEM((length, 384), BF),
            pltpu.VMEM((heads, 1, 384), F32),
            pltpu.VMEM((2, length, local_len), BF),
            pltpu.VMEM((total_chunks, ns, shard_rows, 128), BF),
            own,
        ]
        + [chunks] * 3
        + [
            pltpu.VMEM((wide, total_chunks, shard_rows, 128), BF),
            pltpu.VMEM((4, 8, wide_small), F32),
            pltpu.VMEM((nc, 8, wide_small), F32),
            pltpu.VMEM((ns, 8, wide_small), F32),
            DMA((6,)),
        ]
        + [DMA((wide,))] * 2
        + [DMA((nc - 1,))] * 2
        + [DMA((nc,))] * 2
        + [DMA((2,))]
        + [DMA((total_chunks, wide))] * 2
        + [DMA((total_chunks,))] * 8
        + [DMA((nc,))] * 2
        + [DMA((2,))] * 2
        + [DMA((nc - 1,))] * 2
        + [DMA((wide,))] * 2
        + [DMA((4, nc))] * TP_REDUCE
        + [DMA((5, nc))] * TP_GATHER,
        compiler_params=params(1),
        name="layer",
    )(
        ctx,
        wo,
        xf,
        wuf,
        out_grad,
        down_t,
        out_bias,
        norm1_gain,
        norm1_bias,
        up_bias,
        down_bias,
        norm2_gain,
        norm2_bias,
        wf,
        code,
        inv,
        q,
        kv,
        e,
    )

    def block(*shape):
        return pl.BlockSpec(shape, lambda i: (i,) + (0,) * (len(shape) - 1))

    def fixed(*shape):
        return pl.BlockSpec(shape, lambda i: (0,) * len(shape))

    def vector(size):
        return pl.BlockSpec((size,), lambda i: (0,))

    (
        hidden_out,
        in_grad,
        qw,
        kvw,
        qb,
        vb,
        ow,
        uw,
        dn,
        gain1,
        bias1,
        gain2,
        bias2,
        ob,
        db,
        ub,
    ) = pl.pallas_call(
        deliver_kernel,
        grid=(nc,),
        out_shape=(
            struct((nc, local_len, width), BF),
            struct((nc, local_len, width), F32),
            struct((4, part, shard_rows), F32),
            struct((2, part, shard_rows), F32),
            struct((4, part), F32),
            struct((part,), F32),
            struct((part, shard_rows), F32),
            struct((shard_rows, ff), F32),
            struct((ff, shard_rows), F32),
        )
        + (struct((width,), F32),) * 7,
        in_specs=[
            block(1, local_len, width),
            block(1, local_len, width),
            fixed(*line),
            fixed(8, wide_small),
        ],
        out_specs=[
            block(1, local_len, width),
            block(1, local_len, width),
            fixed(4, part, shard_rows),
            fixed(2, part, shard_rows),
            fixed(4, part),
            vector(part),
            fixed(part, shard_rows),
            fixed(shard_rows, ff),
            fixed(ff, shard_rows),
        ]
        + [vector(width)] * 7,
        compiler_params=pltpu.CompilerParams(
            vmem_limit_bytes=VMEM_LIMIT, dimension_semantics=("arbitrary",)
        ),
        name="deliver",
    )(ing.reshape(nc, local_len, width), hid.reshape(nc, local_len, width), dw, small)
    return (
        hidden_out,
        in_grad,
        qw.swapaxes(1, 2),
        kvw.swapaxes(1, 2),
        qb,
        vb,
        ow,
        ob,
        gain1,
        bias1,
        uw,
        ub,
        dn,
        db,
        gain2,
        bias2,
    )


def solution(mesh):
    in_specs = (
        P("shard", "ctx", None),
        P("shard", "ctx"),
        P("shard", "ctx"),
        P(None, "shard", "tp"),
        P(None, "shard", "tp"),
        P(None, "tp"),
        P("tp"),
        P("tp", "shard"),
        P(),
        P(),
        P(),
        P("shard", "tp"),
        P("tp"),
        P("tp", "shard"),
        P(),
        P(),
        P(),
        P("shard", "ctx", None),
    )
    out_specs = (
        P("shard", "ctx", None),
        P("shard", "ctx", None),
        P(None, "shard", "tp"),
        P(None, "shard", "tp"),
        P(None, "tp"),
        P("tp"),
        P("tp", "shard"),
        P(),
        P(),
        P(),
        P("shard", "tp"),
        P("tp"),
        P("tp", "shard"),
        P(),
        P(),
        P(),
    )
    return jax.shard_map(
        per_device, mesh=mesh, in_specs=in_specs, out_specs=out_specs, check_vma=False
    )
```

```python
import functools

import jax
import jax.numpy as jnp
from jax import lax
from jax.experimental import pallas as pl
from jax.experimental.pallas import tpu as pltpu
from jax.sharding import PartitionSpec as P

BF = jnp.bfloat16
F32 = jnp.float32
HEAD = 64
EPS = 1e-05
MASKED = -1e30
ROOT_HALF = 0.7071067811865476
INV_ROOT_TWO_PI = 0.3989422804014327
VMEM_LIMIT = 66 * 1024 * 1000
MESH = pl.DeviceIdType.MESH
DMA = pltpu.SemaphoreType.DMA


def nn(left, right):
    return lax.dot_general(left, right, (((1,), (0,)), ((), ())), preferred_element_type=F32)


def nt(left, right):
    return lax.dot_general(left, right, (((1,), (1,)), ((), ())), preferred_element_type=F32)


def tn(left, right):
    return lax.dot_general(left, right, (((0,), (0,)), ((), ())), preferred_element_type=F32)


def remote(src, dst, send_sem, recv_sem, peer):
    return pltpu.make_async_remote_copy(
        src_ref=src,
        dst_ref=dst,
        send_sem=send_sem,
        recv_sem=recv_sem,
        device_id=peer,
        device_id_type=MESH,
    )


def greet(peers):
    barrier = pltpu.get_barrier_semaphore()
    for peer in peers:
        pl.semaphore_signal(barrier, inc=1, device_id=peer, device_id_type=MESH)
    pl.semaphore_wait(barrier, len(peers))


class Place:
    def __init__(self, ns, nc):
        self.s = lax.axis_index("shard")
        self.c = lax.axis_index("ctx")
        self.t = lax.axis_index("tp")
        self.core = lax.rem(self.t, 2)
        self.y = self.t // 2
        self.mate_t = self.t + 1 - 2 * self.core
        self.ymate_t = lax.rem(self.t + 2, 4)
        self.mate = {"tp": self.mate_t}
        self.ymate = {"tp": self.ymate_t}
        self.zpeers = [{"ctx": lax.rem(self.c + k, nc)} for k in range(1, nc)]
        self.xpeers = [{"shard": lax.rem(self.s + r, ns)} for r in range(1, ns)]


class TpGather:
    def __init__(self, place, buf, sems):
        self.p, self.buf = place, buf
        self.ys, self.yr, self.ks, self.kr, self.fs, self.fr = sems

    def _y(self, b, i, src):
        p = self.p
        return remote(src, self.buf.at[b, p.t], self.ys.at[i], self.yr.at[i], p.ymate)

    def _k(self, b, i, src):
        p = self.p
        return remote(src, self.buf.at[b, p.t], self.ks.at[i], self.kr.at[i], p.mate)

    def _f(self, b, i):
        p = self.p
        piece = self.buf.at[b, p.ymate_t]
        return remote(piece, piece, self.fs.at[i], self.fr.at[i], p.mate)

    def send(self, b, i, src=None):
        src = self.buf.at[b, self.p.t] if src is None else src
        self._y(b, i, src).start()
        self._k(b, i, src).start()

    def forward(self, b, i):
        p = self.p
        piece = self.buf.at[b, p.ymate_t]
        remote(piece, piece, self.ys.at[i], self.yr.at[i], p.ymate).wait_recv()
        self._f(b, i).start()

    def arrive(self, b, i):
        p = self.p
        piece = self.buf.at[b, p.mate_t]
        remote(piece, piece, self.ks.at[i], self.kr.at[i], p.mate).wait_recv()
        piece = self.buf.at[b, lax.rem(p.mate_t + 2, 4)]
        remote(piece, piece, self.fs.at[i], self.fr.at[i], p.mate).wait_recv()

    def drain(self, b, i, src=None):
        src = self.buf.at[b, self.p.t] if src is None else src
        self._y(b, i, src).wait_send()
        self._k(b, i, src).wait_send()
        self._f(b, i).wait_send()


class TpReduce:
    def __init__(self, place, terms, from_mate, staged, from_y, sems):
        self.p, self.terms, self.from_mate, self.staged, self.from_y = (
            place,
            terms,
            from_mate,
            staged,
            from_y,
        )
        self.ks, self.kr, self.ys, self.yr = sems

    def _k(self, b):
        p = self.p
        return remote(
            self.terms.at[b, :, 1 - p.core],
            self.from_mate.at[b],
            self.ks.at[b],
            self.kr.at[b],
            p.mate,
        )

    def _y(self, b):
        return remote(
            self.staged.at[b], self.from_y.at[b], self.ys.at[b], self.yr.at[b], self.p.ymate
        )

    def send(self, b):
        self._k(b).start()

    def across(self, b):
        p = self.p
        self._k(b).wait_recv()
        other = 1 - p.y
        self.staged[b] = (
            self.terms[b, other, p.core].astype(F32) + self.from_mate[b, other].astype(F32)
        ).astype(BF)
        self._y(b).start()

    def result(self, b):
        p = self.p
        self._y(b).wait_recv()
        return (
            self.terms[b, p.y, p.core].astype(F32)
            + self.from_mate[b, p.y].astype(F32)
            + self.from_y[b].astype(F32)
        )

    def drain(self, b):
        self._k(b).wait_send()
        self._y(b).wait_send()


def column(row, width=128):
    return jnp.broadcast_to(row, (width, row.shape[-1])).T


def project_kernel(
    ns, nc, x_ref, type_ref, seg_ref, qw_ref, kvw_ref, ow_ref, dn_ref, qb_ref, vb_ref, wu_ref,
    xf_ref, q_ref, kv_ref, codef_ref, wf_ref, wo_ref, dnt_ref, wuf_ref, ctx_ref, inv_ref, e_ref,
    wst, code, bias, kcat, vt, segcol, ebuf,
    local, zs, zr, ds, dr, ws, wr, us, ur, es, *tp_sems,
):
    p = Place(ns, nc)
    piece = x_ref.shape[1] // 4
    heads = wst.shape[0] - 1
    for j in range(nc):
        label = seg_ref[j : j + 1]
        code[j] = jnp.where(type_ref[j : j + 1] == 0, label, -label).astype(F32)
    greet([p.mate, p.ymate] + p.zpeers + p.xpeers)
    mine = pl.ds(p.t * piece, piece)

    def x_send(k):
        peer = p.zpeers[k]
        return remote(
            x_ref.at[peer["ctx"], mine], xf_ref.at[p.c, p.t], zs.at[k], zr.at[k], peer
        )

    def code_send(k):
        peer = p.zpeers[k]
        return remote(code.at[peer["ctx"]], codef_ref.at[p.c], ds.at[k], dr.at[k], peer)

    def gathered(h, src):
        return wo_ref.at[src] if isinstance(h, int) and h == heads else wf_ref.at[h, src]

    def weight(h, r):
        return remote(wst.at[h], gathered(h, p.s), ws.at[h, r], wr.at[h, r], p.xpeers[r])

    def weight_landed(h):
        for r in range(ns - 1):
            landed = gathered(h, lax.rem(p.s + ns - 1 - r, ns))
            remote(landed, landed, ws.at[h, r], wr.at[h, r], p.xpeers[r]).wait_recv()

    for k in range(nc - 1):
        x_send(k).start()
    own = x_ref.at[p.c, mine]
    gather = TpGather(p, xf_ref, tp_sems)
    gather.send(p.c, 0, own)
    for h in range(heads):
        cols = slice(h * HEAD, (h + 1) * HEAD)
        parts = [qw_ref[k, cols] for k in range(4)] + [kvw_ref[k, cols] for k in range(2)]
        wst[h] = jnp.concatenate(parts, axis=0).T
        for r in range(ns - 1):
            weight(h, r).start()
    turned = ow_ref[...].T
    blank = jnp.zeros((turned.shape[0], HEAD), BF)
    parts = []
    for h in range(heads):
        parts += [blank, turned[:, h * HEAD : (h + 1) * HEAD]]
    wst[heads] = jnp.concatenate(parts, axis=1)
    for r in range(ns - 1):
        weight(heads, r).start()

    def up_send(r):
        return remote(wu_ref, wuf_ref.at[p.s], us.at[r], ur.at[r], p.xpeers[r])

    for r in range(ns - 1):
        up_send(r).start()
    for k in range(nc - 1):
        code_send(k).start()
    copies = [
        pltpu.make_async_copy(own, xf_ref.at[p.c, p.t], local.at[0]),
        pltpu.make_async_copy(code.at[p.c], codef_ref.at[p.c], local.at[1]),
        pltpu.make_async_copy(wst.at[pl.ds(0, heads)], wf_ref.at[:, p.s], local.at[2]),
        pltpu.make_async_copy(wst.at[heads], wo_ref.at[p.s], local.at[3]),
        pltpu.make_async_copy(wu_ref, wuf_ref.at[p.s], local.at[4]),
    ]
    for copy in copies:
        copy.start()
    vb = vb_ref[...].reshape(1, -1)
    for h in range(heads):
        cols = slice(h * HEAD, (h + 1) * HEAD)
        parts = [qb_ref[k : k + 1, cols] for k in range(4)]
        bias[h] = jnp.concatenate(parts + [jnp.zeros((1, HEAD), F32), vb[:, cols]], axis=1)
    dnt_ref[...] = dn_ref[...].T
    blocks = [lax.rem(p.c + nc - k, nc) for k in range(nc)]
    for k in range(1, nc):
        landed = xf_ref.at[blocks[k], p.t]
        remote(landed, landed, zs.at[k - 1], zr.at[k - 1], p.zpeers[k - 1]).wait_recv()
        gather.send(blocks[k], k)
        gather.forward(blocks[k - 1], k - 1)
    gather.forward(blocks[nc - 1], nc - 1)
    for k in range(nc):
        gather.arrive(blocks[k], k)
    for k in range(nc - 1):
        landed = codef_ref.at[blocks[k + 1]]
        remote(landed, landed, ds.at[k], dr.at[k], p.zpeers[k]).wait_recv()
    for copy in copies:
        copy.wait()
    width = xf_ref.shape[-1]
    rows = 4 * piece
    length = nc * rows
    for j in range(nc):
        col = jnp.abs(column(codef_ref[j]))
        segcol[j * rows : (j + 1) * rows] = jnp.where(col == 0.0, -1.0, col)
    low_half = lax.broadcasted_iota(jnp.int32, (rows, 128), 1) < HEAD

    def e_out(i):
        slot = lax.rem(i, 2)
        return pltpu.make_async_copy(ebuf.at[slot], e_ref.at[i], es.at[slot])

    def head_step(h, carry):
        weight_landed(h)

        def project(b, carry):
            x = xf_ref[b].reshape(rows, width)
            out = nn(x, wf_ref[h].reshape(width, 384)) + bias[h]
            entity = column(codef_ref[b]) < 0.0
            at = pl.ds(pl.multiple_of(b * rows, rows), rows)
            chosen = jnp.where(entity, out[:, 128:256], out[:, 0:128])
            q_ref[h, at] = (chosen * HEAD ** (-0.5)).astype(BF)
            kv = out[:, 256:384].astype(BF)
            kv_ref[h, at] = kv
            kv = kv.astype(F32)
            turned = pltpu.roll(kv, HEAD, 1)
            keep = jnp.where(low_half, kv, turned)
            kcat[at] = jnp.where(low_half == entity, 0.0, keep).astype(BF)
            vt[:, at] = jnp.where(low_half, 0.0, kv).T.astype(BF)
            return carry

        lax.fori_loop(0, nc, project, 0)

        def attend(b, carry):
            i = h * nc + b
            at = pl.ds(pl.multiple_of(b * rows, rows), rows)
            scores = nt(kcat[...], q_ref[h, at])
            segment = jnp.abs(codef_ref[b])
            allowed = jnp.concatenate([segcol[...]] * (rows // 128), axis=1) == segment
            scores = jnp.where(allowed, scores, MASKED)
            top = jnp.max(scores, axis=0, keepdims=True)
            top = jnp.where(top == MASKED, 0.0, top)
            exponent = jnp.exp(scores - top)
            inverse = 1.0 / jnp.maximum(jnp.sum(exponent, axis=0, keepdims=True), 1.0)
            exponent = exponent.astype(BF)

            @pl.when(i >= 2)
            def _():
                e_out(i - 2).wait()

            ebuf[lax.rem(i, 2)] = exponent
            e_out(i).start()
            inv_ref[i] = inverse
            lanes = pl.ds(pl.multiple_of(h * 128, 128), 128)
            ctx_ref[at, lanes] = (nn(vt[...], exponent) * inverse).T.astype(BF)
            return carry

        lax.fori_loop(0, nc, attend, 0)
        return carry

    lax.fori_loop(0, heads, head_step, 0)
    for i in range(heads * nc - 2, heads * nc):
        e_out(i).wait()
    for r in range(ns - 1):
        landed = wuf_ref.at[lax.rem(p.s + ns - 1 - r, ns)]
        remote(landed, landed, us.at[r], ur.at[r], p.xpeers[r]).wait_recv()
    weight_landed(heads)
    for h in range(heads + 1):
        for r in range(ns - 1):
            weight(h, r).wait_send()
    for r in range(ns - 1):
        up_send(r).wait_send()
    for k in range(nc - 1):
        x_send(k).wait_send()
        code_send(k).wait_send()
    gather.drain(p.c, 0, own)
    for k in range(1, nc):
        gather.drain(blocks[k], k)


def spread(values):
    average = jnp.mean(values, axis=-1, keepdims=True)
    centred = values - average
    inverse = lax.rsqrt(jnp.mean(centred * centred, axis=-1, keepdims=True) + EPS)
    return centred * inverse, inverse


def unspread(upstream, normed, inverse, gain):
    scaled = upstream * gain
    first = jnp.mean(scaled, axis=-1, keepdims=True)
    second = jnp.mean(scaled * normed, axis=-1, keepdims=True)
    return inverse * (scaled - first - normed * second)


def total(values):
    return jnp.sum(values, axis=0, keepdims=True)


SKEWS_C = (0, 1, 2, 3, 4, 5, 6, 7, 8, 9, 11, 12, 13)
FF_CHUNKS = 12
OUT_CHUNKS = 2
HEAD_CHUNKS = 3
FIRST_SUM, CHUNK, HOP = -30.0, 2.1, 5.5
STEP_ENDS = (-29.0, -25.0, -22.0, -20.0)
BACK_START, BACK_STEP = -17.0, 1.42


def layer_kernel(
    ns, nc, ctx_ref, wo_ref, xf_ref, wuf, og_ref, wd_ref, *rest,
):
    vecs, rest = rest[:7], rest[7:]
    (
        wf_ref, code_ref, inv_ref, q_ref, kv_ref, e_ref,
        ing_ref, hidf_ref, dw_ref, sm_ref,
        ga, hid, gfi, small,
        wdf, ogo, hsend,
        t0, m0, s0, y0, t1, m1, s1, y1, t2, m2, s2, y2,
        low, gf, active, slope, gup, fo, fh, fi, gs,
        dctx, kcat, dkey, dval, dqkv, qb, ebuf, dqo,
        ig, zo, zr, zq, xr, smt, smz, smx,
        local, ws, wr, os, orr, hs, hr,
        es, xs, xrs, z1s, z1r, z2s, z2r, z3s, z3r, z4s, z4r, igs, igr,
        ss, sr, szs, szr, sxs, sxr, *tp_sems,
    ) = rest
    p = Place(ns, nc)
    piece, width = xf_ref.shape[2:]
    rows = 4 * piece
    length = nc * rows
    heads = q_ref.shape[0]
    steps = heads * nc
    chunks = dw_ref.shape[0]
    back = slope

    def fetch(i):
        return pltpu.make_async_copy(e_ref.at[i], ebuf.at[lax.rem(i, 2)], es.at[lax.rem(i, 2)])

    fetch(0).start()
    greet([p.mate, p.ymate] + p.zpeers + p.xpeers)

    def down_send(r):
        return remote(wd_ref, wdf.at[p.s], ws.at[r], wr.at[r], p.xpeers[r])

    for r in range(ns - 1):
        down_send(r).start()
    mine = pl.ds(p.t * piece, piece)

    def og_send(k):
        peer = p.zpeers[k]
        return remote(og_ref.at[peer["ctx"], mine], ogo.at[p.c], os.at[k], orr.at[k], peer)

    for k in range(nc - 1):
        og_send(k).start()
    copies = [
        pltpu.make_async_copy(og_ref.at[p.c, mine], ogo.at[p.c], local.at[0]),
        pltpu.make_async_copy(wd_ref, wdf.at[p.s], local.at[1]),
    ]
    for copy in copies:
        copy.start()
    small[...] = jnp.zeros_like(small)

    sums = [
        TpReduce(p, *bufs, [tp_sems[j].at[i] for j in range(4)])
        for i, bufs in enumerate(
            ((t0, m0, s0, y0), (t1, m1, s1, y1), (t2, m2, s2, y2), (t0, m0, s0, y0))
        )
    ]
    shares = [
        TpGather(p, buf, [tp_sems[4 + j].at[i] for j in range(6)])
        for i, buf in enumerate((low, gf, ga, hidf_ref, ing_ref))
    ]
    back_sum, share_h, share_g = sums[3], shares[3], shares[4]
    out_bias, gain1, bias1, up_bias, down_bias, gain2, bias2 = (
        ref[...].reshape(1, -1) for ref in vecs
    )


    def x_send(k, r):
        peer = p.xpeers[r]
        return remote(dqo.at[k, peer["shard"]], xr.at[r, k], xs.at[k, r], xrs.at[k, r], peer)

    outer = (p.c == 0) | (p.c == nc - 1)
    inner = (p.c > 0) & (p.c < nc - 1)
    inward = {"ctx": 1 + p.c // 3}
    outward = {"ctx": lax.rem(3 * (p.c + nc - 1), 6)}
    across = {"ctx": lax.rem(2 * nc - 1 - p.c, nc)}

    def to_inner(k):
        return remote(zo.at[k], zr.at[k], z1s.at[k], z1r.at[k], inward)

    def to_owner(k):
        return remote(zq.at[k], zq.at[k], z2s.at[k], z2r.at[k], across)

    def to_other(k):
        return remote(dw_ref.at[k], dw_ref.at[k], z3s.at[k], z3r.at[k], across)

    def to_outer(k):
        return remote(dw_ref.at[k], dw_ref.at[k], z4s.at[k], z4r.at[k], outward)

    def owns(k):
        return lax.rem(k + p.c, 2) == 1

    def line_start(k):
        grad = dqo[k, p.s].astype(F32)
        for r in range(ns - 1):
            x_send(k, r).wait_recv()
            grad = grad + xr[r, k].astype(F32)
        zo[k] = grad.astype(BF)

        @pl.when(outer)
        def _():
            to_inner(k).start()

    def line_in(k):
        @pl.when(inner)
        def _():
            to_inner(k).wait_recv()

        @pl.when(inner & jnp.logical_not(owns(k)))
        def _():
            zq[k] = (zo[k].astype(F32) + zr[k].astype(F32)).astype(BF)
            to_owner(k).start()

    def line_own(k):
        @pl.when(inner & owns(k))
        def _():
            to_owner(k).wait_recv()
            dw_ref[k] = (zo[k].astype(F32) + zr[k].astype(F32) + zq[k].astype(F32)).astype(BF)
            to_other(k).start()
            to_outer(k).start()

    def line_pass(k):
        @pl.when(inner & jnp.logical_not(owns(k)))
        def _():
            to_other(k).wait_recv()
            to_outer(k).start()

    plan = []
    for k in range(chunks):
        for hop, action in enumerate((line_start, line_in, line_own, line_pass)):
            plan.append((FIRST_SUM + CHUNK * k + HOP * hop, functools.partial(action, k)))

    def due(after, until):
        stretch = [entry for entry in plan if after < entry[0] <= until]
        return [action for _, action in sorted(stretch, key=lambda entry: entry[0])]

    def run(actions):
        for action in actions:
            action()

    def line_end(k):
        @pl.when(outer)
        def _():
            to_outer(k).wait_recv()
            to_inner(k).wait_send()

        @pl.when(inner)
        def _():
            @pl.when(owns(k))
            def _():
                to_other(k).wait_send()

            @pl.when(jnp.logical_not(owns(k)))
            def _():
                to_owner(k).wait_send()

            to_outer(k).wait_send()

    sizes = [HEAD_CHUNKS] * 4 + [OUT_CHUNKS] + [HEAD_CHUNKS] * heads
    groups = [(sum(sizes[:g]), n) for g, n in enumerate(sizes)]

    def put_grad(lo, n, value):
        for j in range(n):
            dqo[lo + j] = value[:, j * 128 : (j + 1) * 128].reshape(dqo.shape[1:])
            for r in range(ns - 1):
                x_send(lo + j, r).start()


    def put(terms, b, values):
        terms[b] = values.astype(BF).reshape(2, 2, piece, width)

    def add_small(row, values):
        small[row : row + 1] += total(values)

    def block_rows(b):
        return pl.ds(pl.multiple_of(b * rows, rows), rows)

    def out_project(b):
        put(t0, b, nt(ctx_ref[block_rows(b)], wo_ref[...].reshape(width, -1)))
        sums[0].send(b)

    def norm_one(b):
        h = xf_ref[b, p.t].astype(F32) + (sums[0].result(b) + out_bias)
        normed, inverse = spread(h)
        first = normed * gain1 + bias1
        fo[b] = first
        fh[b] = normed
        fi[b] = inverse
        low[b, p.t] = first.astype(BF)
        shares[0].send(b, b)

    def feed_forward(b):
        shares[0].arrive(b, b)
        up = nn(low[b].reshape(rows, width), wuf[...].reshape(width, -1)) + up_bias
        cdf = 0.5 * (1.0 + lax.erf(up * ROOT_HALF))
        act = (up * cdf).astype(BF)
        active[b] = act
        slope[b] = cdf + up * (jnp.exp(-0.5 * up * up) * INV_ROOT_TWO_PI)

        @pl.when(b == 0)
        def _():
            for r in range(ns - 1):
                landed = wdf.at[lax.rem(p.s + ns - 1 - r, ns)]
                remote(landed, landed, ws.at[r], wr.at[r], p.xpeers[r]).wait_recv()
            copies[1].wait()

        put(t1, b, nt(active[b], wdf[...].reshape(width, -1)))
        sums[1].send(b)

    def hid_send(b):
        return remote(hsend.at[b], hid.at[p.c], hs.at[b], hr.at[p.c], {"ctx": b})

    def norm_two(b):
        @pl.when(b == 0)
        def _():
            for k in range(nc - 1):
                landed = ogo.at[lax.rem(p.c + nc - 1 - k, nc)]
                remote(landed, landed, os.at[k], orr.at[k], p.zpeers[k]).wait_recv()
            copies[0].wait()

        normed, inverse = spread(fo[b] + (sums[1].result(b) + down_bias))
        hsend[b] = (normed * gain2 + bias2).astype(BF)

        upstream = ogo[b].astype(F32)
        add_small(2, upstream * normed)
        add_small(3, upstream)
        grad = unspread(upstream, normed, inverse, gain2)
        gs[b] = grad
        grad = grad.astype(BF)
        gf[b, p.t] = grad
        add_small(5, grad.astype(F32))
        shares[1].send(b, b)

        @pl.when(b != p.c)
        def _():
            hid_send(b).start()

        @pl.when(b == p.c)
        def _():
            pltpu.make_async_copy(hsend.at[b], hid.at[p.c], local.at[3]).start()

    def feed_back(b):
        shares[1].arrive(b, b)
        grad = nn(gf[b].reshape(rows, width), wdf[...].reshape(width, -1))
        grad = (grad.astype(BF).astype(F32) * slope[b]).astype(BF)
        gup[b] = grad
        add_small(6, grad.astype(F32))
        put(t2, b, nt(grad, wuf[...].reshape(width, -1)))
        sums[2].send(b)

    def norm_back(b):
        grad = gs[b] + sums[2].result(b)
        add_small(0, grad * fh[b])
        add_small(1, grad)
        grad = unspread(grad, fh[b], fi[b], gain1)
        gfi[b] = grad
        grad = grad.astype(BF)
        ga[b, p.t] = grad
        add_small(4, grad.astype(F32))
        shares[2].send(b, b)

    stages = (
        out_project,
        sums[0].across,
        norm_one,
        lambda b: shares[0].forward(b, b),
        feed_forward,
        sums[1].across,
        norm_two,
        lambda b: shares[1].forward(b, b),
        feed_back,
        sums[2].across,
        norm_back,
        lambda b: shares[2].forward(b, b),
        lambda b: shares[2].arrive(b, b),
    )

    half = HEAD_CHUNKS * 128

    def weight_grad(g):
        left = (gf, low)[g // 2][...].reshape(length, width)
        right = (active, gup)[g // 2][:, :, half * (g % 2) : half * (g % 2 + 1)]
        put_grad(*groups[g], tn(left, right.reshape(length, half)).astype(BF))

    def run_at(step, events):
        for when, action in events.items():

            @pl.when(step == when)
            def _(action=action):
                action()

    full = SKEWS_C[8] + nc - 1
    ends = (-100.0,) + STEP_ENDS
    feed_events = {
        full + 2 + j: functools.partial(run, due(ends[j], ends[j + 1])) for j in range(4)
    }
    feed_events[full] = lambda: (weight_grad(0), weight_grad(1))
    feed_events[full + 1] = lambda: (weight_grad(2), weight_grad(3))

    def feed_slot(step, carry):
        for skew, stage in zip(SKEWS_C, stages):
            b = step - skew

            @pl.when((b >= 0) & (b < nc))
            def _(stage=stage, b=b):
                stage(b)

        run_at(step, feed_events)
        return carry

    lax.fori_loop(0, SKEWS_C[-1] + nc, feed_slot, 0)


    def small_tp(i, peer):
        return remote(smt.at[2 * i], smt.at[2 * i + 1], ss.at[i], sr.at[i], peer)

    shared = lax.broadcasted_iota(jnp.int32, smt.shape[1:], 0) < 6

    def small_fold(i):
        return smt[2 * i] + jnp.where(shared, smt[2 * i + 1], 0.0)

    def small_z(k):
        return remote(smz.at[p.c], smz.at[p.c], szs.at[k], szr.at[k], p.zpeers[k])

    def small_x(r):
        return remote(smx.at[p.s], smx.at[p.s], sxs.at[r], sxr.at[r], p.xpeers[r])

    def small_zero():
        smt[0] = jnp.zeros_like(smt[0])
        smt[0, :, 0:width] = small[...]
        for h in range(heads):
            smt[0, 7:8, h * 384 : (h + 1) * 384] = qb[h]
        small_tp(0, p.mate).start()

    def small_one():
        small_tp(0, p.mate).wait_recv()
        smt[2] = small_fold(0)
        small_tp(1, p.ymate).start()

    def small_two():
        small_tp(1, p.ymate).wait_recv()
        smz[p.c] = small_fold(1)
        for k in range(nc - 1):
            small_z(k).start()

    def small_three():
        for k in range(nc - 1):
            landed = smz.at[lax.rem(p.c + nc - 1 - k, nc)]
            remote(landed, landed, szs.at[k], szr.at[k], p.zpeers[k]).wait_recv()
        value = smz[0]
        for k in range(1, nc):
            value = value + smz[k]
        smx[p.s] = value
        for r in range(ns - 1):
            small_x(r).start()

    def small_four():
        for r in range(ns - 1):
            landed = smx.at[lax.rem(p.s + ns - 1 - r, ns)]
            remote(landed, landed, sxs.at[r], sxr.at[r], p.xpeers[r]).wait_recv()
        value = smx[0]
        for r in range(1, ns):
            value = value + smx[r]
        sm_ref[...] = value


    def grad_send(b):
        return remote(ig.at[b], ing_ref.at[p.c, p.t], igs.at[b], igr.at[p.c], {"ctx": b})

    def grad_own(b):
        ig[b] = (gfi[b] + back_sum.result(b)).astype(BF)

        @pl.when(b != p.c)
        def _():
            grad_send(b).start()

        @pl.when(b == p.c)
        def _():
            pltpu.make_async_copy(ig.at[b], ing_ref.at[p.c, p.t], local.at[4]).start()

    order = [lax.rem(p.c + k, nc) for k in range(nc)]

    def grad_share(k):
        q = order[k]
        if k > 0:
            landed = ing_ref.at[q, p.t]
            remote(landed, landed, igs.at[q], igr.at[q], {"ctx": q}).wait_recv()
        else:
            pltpu.make_async_copy(ig.at[p.c], ing_ref.at[p.c, p.t], local.at[4]).wait()
        share_g.send(q, k)


    for k in range(1, nc):
        src = lax.rem(p.c + k, nc)
        landed = hid.at[src]
        remote(landed, landed, hs.at[src], hr.at[src], p.zpeers[k - 1]).wait_recv()
        hid_send(src).wait_send()
    pltpu.make_async_copy(hsend.at[p.c], hid.at[p.c], local.at[3]).wait()
    for b in range(nc):
        share_h.send(b, b, hid.at[b])
    keep = pltpu.make_async_copy(hid, hidf_ref.at[:, p.t], local.at[5])
    keep.start()
    for b in range(nc):
        sums[0].drain(b)
    grad_attn = ga[...].reshape(length, width)
    out = wo_ref[...].reshape(width, heads * 128)
    for i in range(heads):
        dctx[i] = nn(grad_attn, out[:, i * 128 : (i + 1) * 128]).astype(BF)
    value = tn(grad_attn, ctx_ref[...]).astype(BF)
    value = [value[:, i * 128 + HEAD : (i + 1) * 128] for i in range(heads)]
    put_grad(*groups[4], jnp.concatenate(value + [jnp.zeros_like(value[0])], axis=1))
    back[...] = jnp.zeros_like(back)
    low_half = lax.broadcasted_iota(jnp.int32, (rows, 128), 1) < HEAD

    def attend_step(i):
        h, b = i // nc, lax.rem(i, nc)
        fetch(i).wait()

        @pl.when(i + 1 < steps)
        def _():
            fetch(i + 1).start()

        @pl.when(b == 0)
        def _():
            for j in range(nc):
                at = slice(j * rows, (j + 1) * rows)
                entity = column(code_ref[j]) < 0.0
                kv = kv_ref[h, at].astype(F32)
                kept = jnp.where(low_half, kv, pltpu.roll(kv, HEAD, 1))
                kcat[at] = jnp.where(low_half == entity, 0.0, kept).astype(BF)
            dkey[...] = jnp.zeros_like(dkey)
            dval[...] = jnp.zeros_like(dval)

        at = block_rows(b)
        lanes = pl.ds(pl.multiple_of(h * 128, 128), 128)
        grad_ctx = dctx[h, at].astype(F32).T * inv_ref[i]
        row_dot = jnp.sum(grad_ctx * ctx_ref[at, lanes].astype(F32).T, axis=0, keepdims=True)
        grad_ctx = grad_ctx.astype(BF)
        weight = ebuf[lax.rem(i, 2)]
        grad = nn(kv_ref[h], grad_ctx)
        grad = (weight.astype(F32) * (grad - row_dot)).astype(BF)
        dval[...] += nt(weight, grad_ctx)
        dkey[...] += nn(grad, q_ref[h, at])
        grad_q = tn(kcat[...], grad).T * HEAD ** (-0.5)
        entity = column(code_ref[b]) < 0.0
        dqkv[at, 0:128] = jnp.where(entity, 0.0, grad_q).astype(BF)
        dqkv[at, 128:256] = jnp.where(entity, grad_q, 0.0).astype(BF)

        @pl.when(b == nc - 1)
        def _():
            for j in range(nc):
                part = slice(j * rows, (j + 1) * rows)
                entity = column(code_ref[j]) < 0.0
                grad_k = dkey[part]
                grad_k = jnp.where(entity, pltpu.roll(grad_k, HEAD, 1), grad_k)
                dqkv[part, 256:384] = jnp.where(low_half, grad_k, dval[part]).astype(BF)
            w = wf_ref[h].reshape(width, 384)

            @pl.when(h < heads - 1)
            def _():
                for j in range(nc):
                    back[j] += nt(dqkv[j * rows : (j + 1) * rows], w)

            @pl.when(h == heads - 1)
            def _():
                for j in range(nc):
                    put(t0, j, back[j] + nt(dqkv[j * rows : (j + 1) * rows], w))
                    back_sum.send(j)

            grads = dqkv[...]
            value = tn(xf_ref[...].reshape(length, width), grads).astype(BF)
            put_grad(FF_CHUNKS + OUT_CHUNKS + HEAD_CHUNKS * h, HEAD_CHUNKS, value)
            qb[h] = total(grads.astype(F32))

    def forward_hidden():
        for b in range(nc):
            share_h.forward(b, b)

    def hand(k):
        share_g.forward(order[k], k)

    run(due(STEP_ENDS[-1], BACK_START))
    ends = [BACK_START + BACK_STEP * i for i in range(steps + 1)]
    events = {i: functools.partial(run, due(ends[i], ends[i + 1])) for i in range(steps)}
    events[3] = lambda: (forward_hidden(), run(due(ends[3], ends[4])))

    def slot(i, carry):
        attend_step(i)
        run_at(i, events)
        return carry

    lax.fori_loop(0, steps, slot, 0)
    for b in range(nc):
        plan += [
            (2.0 + 0.5 * b, functools.partial(back_sum.across, b)),
            (6.5 + 2.0 * b, functools.partial(grad_own, b)),
            (13.0 + 1.0 * b, functools.partial(grad_share, b)),
            (18.0 + 2.0 * b, functools.partial(hand, b)),
        ]
    plan += [(3.8, small_zero), (7.0, small_one), (14.5, small_two), (19.5, small_three)]
    plan += [(25.0, small_four)]
    run(due(ends[-1], 1000.0))
    for b in range(nc):
        share_h.arrive(b, b)
        share_g.arrive(order[b], b)
    for k in range(chunks):
        line_end(k)
    keep.wait()
    for k in range(chunks):
        for r in range(ns - 1):
            x_send(k, r).wait_send()
    for b in range(nc):
        for i in range(1, 4):
            sums[i].drain(b)
        for i in range(3):
            shares[i].drain(b, b)
        share_h.drain(b, b, hid.at[b])
        share_g.drain(order[b], b)

        @pl.when(b != p.c)
        def _(b=b):
            grad_send(b).wait_send()

    for r in range(ns - 1):
        down_send(r).wait_send()
    for k in range(nc - 1):
        og_send(k).wait_send()
    small_tp(0, p.mate).wait_send()
    small_tp(1, p.ymate).wait_send()
    for k in range(nc - 1):
        small_z(k).wait_send()
    for r in range(ns - 1):
        small_x(r).wait_send()


def deliver_kernel(
    ing_ref, hid_ref, dw_ref, sm_ref,
    hidden_ref, grad_ref, qw_ref, kvw_ref, qb_ref, vb_ref, ow_ref, uw_ref, dn_ref, *vec_refs,
):
    hidden_ref[...] = hid_ref[...]
    grad_ref[...] = ing_ref[...].astype(F32)

    @pl.when(pl.program_id(0) == 0)
    def _():
        def wide(lo, n):
            return jnp.concatenate([dw_ref[lo + j].astype(F32) for j in range(n)], axis=1)

        uw_ref[...] = wide(6, 6)
        dn_ref[...] = wide(0, 6).T
        heads = qb_ref.shape[1] // HEAD
        ow_ref[...] = wide(FF_CHUNKS, OUT_CHUNKS)[:, : heads * HEAD].T
        first = FF_CHUNKS + OUT_CHUNKS
        grads = [wide(first + HEAD_CHUNKS * h, HEAD_CHUNKS).T for h in range(heads)]
        small = sm_ref[...]
        for k in range(6):
            cols = slice(k * HEAD, (k + 1) * HEAD)
            part = jnp.concatenate([grad[cols] for grad in grads], axis=0)
            vec = jnp.concatenate(
                [
                    small[7:8, h * 384 + k * HEAD : h * 384 + (k + 1) * HEAD]
                    for h in range(heads)
                ],
                axis=1,
            )
            if k < 4:
                qw_ref[k] = part
                qb_ref[k : k + 1] = vec
            else:
                kvw_ref[k - 4] = part
            if k == 5:
                vb_ref[...] = vec.reshape(-1)
        width = uw_ref.shape[1]
        for i, ref in enumerate(vec_refs):
            ref[...] = small[i : i + 1, :width].reshape(-1)


def vmem(count):
    return [pl.BlockSpec(memory_space=pltpu.VMEM)] * count


def struct(shape, dtype):
    return jax.ShapeDtypeStruct(shape, dtype)


def params(collective_id):
    return pltpu.CompilerParams(
        vmem_limit_bytes=VMEM_LIMIT, collective_id=collective_id, has_side_effects=True
    )


TP_GATHER = 6
TP_REDUCE = 4


def per_device(
    hidden_in,
    token_type,
    segment,
    query_weight,
    key_value_weight,
    query_bias,
    value_bias,
    out_weight,
    out_bias,
    norm1_gain,
    norm1_bias,
    up_weight,
    up_bias,
    down_weight,
    down_bias,
    norm2_gain,
    norm2_bias,
    out_grad,
):
    ns, nc = lax.axis_size("shard"), lax.axis_size("ctx")
    seqs, local_len, width = hidden_in.shape
    part = query_weight.shape[2]
    heads = part // HEAD
    shard_rows = query_weight.shape[1]
    ff = up_weight.shape[1]
    piece = local_len // 4
    length = nc * local_len
    assert seqs == nc == 4 and heads == 3 and ff == width
    wide = ns - 1

    mixed = OUT_CHUNKS + HEAD_CHUNKS * heads
    line = (FF_CHUNKS + mixed, shard_rows, 128)
    hbm = [pl.BlockSpec(memory_space=pl.ANY)]
    xf, q, kv, code, wf, wo, down_t, wuf, ctx, inv, e = pl.pallas_call(
        functools.partial(project_kernel, ns, nc),
        out_shape=(
            struct((nc, 4, piece, width), BF),
            struct((heads, length, 128), BF),
            struct((heads, length, 128), BF),
            struct((nc, 1, local_len), F32),
            struct((heads, ns, shard_rows, 384), BF),
            struct((ns, shard_rows, 384), BF),
            struct((shard_rows, ff), BF),
            struct((ns, shard_rows, ff), BF),
            struct((length, heads * 128), BF),
            struct((heads * nc, 1, local_len), F32),
            struct((heads * nc, length, local_len), BF),
        ),
        in_specs=vmem(9) + hbm,
        out_specs=vmem(10) + hbm,
        scratch_shapes=[
            pltpu.VMEM((heads + 1, shard_rows, 384), BF),
            pltpu.VMEM((nc, 1, local_len), F32),
            pltpu.VMEM((heads, 1, 384), F32),
            pltpu.VMEM((length, 128), BF),
            pltpu.VMEM((128, length), BF),
            pltpu.VMEM((length, 128), F32),
            pltpu.VMEM((2, length, local_len), BF),
            DMA((5,)),
        ]
        + [DMA((nc - 1,))] * 4
        + [DMA((heads + 1, wide))] * 2
        + [DMA((wide,))] * 2
        + [DMA((2,))]
        + [DMA((nc,))] * TP_GATHER,
        compiler_params=params(0),
        name="project",
    )(
        hidden_in,
        token_type,
        segment,
        query_weight.swapaxes(1, 2),
        key_value_weight.swapaxes(1, 2),
        out_weight,
        down_weight,
        query_bias,
        value_bias,
        up_weight,
    )

    full = pltpu.VMEM((nc, 4, piece, width), BF)
    own = pltpu.VMEM((nc, piece, width), BF)
    own32 = pltpu.VMEM((nc, piece, width), F32)
    reduce_bufs = [
        pltpu.VMEM((nc, 2, 2, piece, width), BF),
        pltpu.VMEM((nc, 2, piece, width), BF),
        own,
        own,
    ]
    rows_ff = pltpu.VMEM((nc, local_len, ff), BF)
    total_chunks = line[0]
    chunks = pltpu.VMEM(line, BF)
    wide_small = heads * 384
    ing, hid, dw, small = pl.pallas_call(
        functools.partial(layer_kernel, ns, nc),
        out_shape=(
            struct((nc, 4, piece, width), BF),
            struct((nc, 4, piece, width), BF),
            struct(line, BF),
            struct((8, wide_small), F32),
        ),
        in_specs=vmem(4) + hbm * 2 + vmem(12) + hbm,
        out_specs=vmem(4),
        scratch_shapes=[
            full,
            own,
            own32,
            pltpu.VMEM((8, width), F32),
            pltpu.VMEM((ns, shard_rows, ff), BF),
            own,
            own,
        ]
        + reduce_bufs * 3
        + [
            full,
            full,
            rows_ff,
            pltpu.VMEM((nc, local_len, ff), F32),
            rows_ff,
            own32,
            own32,
            pltpu.VMEM((nc, piece, 1), F32),
            own32,
            pltpu.VMEM((heads, length, 128), BF),
            pltpu.VMEM((length, 128), BF),
            pltpu.VMEM((length, 128), F32),
            pltpu.VMEM((length, 128), F32),
            pltpu.VMEM((length, 384), BF),
            pltpu.VMEM((heads, 1, 384), F32),
            pltpu.VMEM((2, length, local_len), BF),
            pltpu.VMEM((total_chunks, ns, shard_rows, 128), BF),
            own,
        ]
        + [chunks] * 3
        + [
            pltpu.VMEM((wide, total_chunks, shard_rows, 128), BF),
            pltpu.VMEM((4, 8, wide_small), F32),
            pltpu.VMEM((nc, 8, wide_small), F32),
            pltpu.VMEM((ns, 8, wide_small), F32),
            DMA((6,)),
        ]
        + [DMA((wide,))] * 2
        + [DMA((nc - 1,))] * 2
        + [DMA((nc,))] * 2
        + [DMA((2,))]
        + [DMA((total_chunks, wide))] * 2
        + [DMA((total_chunks,))] * 8
        + [DMA((nc,))] * 2
        + [DMA((2,))] * 2
        + [DMA((nc - 1,))] * 2
        + [DMA((wide,))] * 2
        + [DMA((4, nc))] * TP_REDUCE
        + [DMA((5, nc))] * TP_GATHER,
        compiler_params=params(1),
        name="layer",
    )(
        ctx,
        wo,
        xf,
        wuf,
        out_grad,
        down_t,
        out_bias,
        norm1_gain,
        norm1_bias,
        up_bias,
        down_bias,
        norm2_gain,
        norm2_bias,
        wf,
        code,
        inv,
        q,
        kv,
        e,
    )

    def block(*shape):
        return pl.BlockSpec(shape, lambda i: (i,) + (0,) * (len(shape) - 1))

    def fixed(*shape):
        return pl.BlockSpec(shape, lambda i: (0,) * len(shape))

    def vector(size):
        return pl.BlockSpec((size,), lambda i: (0,))

    (
        hidden_out,
        in_grad,
        qw,
        kvw,
        qb,
        vb,
        ow,
        uw,
        dn,
        gain1,
        bias1,
        gain2,
        bias2,
        ob,
        db,
        ub,
    ) = pl.pallas_call(
        deliver_kernel,
        grid=(nc,),
        out_shape=(
            struct((nc, local_len, width), BF),
            struct((nc, local_len, width), F32),
            struct((4, part, shard_rows), F32),
            struct((2, part, shard_rows), F32),
            struct((4, part), F32),
            struct((part,), F32),
            struct((part, shard_rows), F32),
            struct((shard_rows, ff), F32),
            struct((ff, shard_rows), F32),
        )
        + (struct((width,), F32),) * 7,
        in_specs=[
            block(1, local_len, width),
            block(1, local_len, width),
            fixed(*line),
            fixed(8, wide_small),
        ],
        out_specs=[
            block(1, local_len, width),
            block(1, local_len, width),
            fixed(4, part, shard_rows),
            fixed(2, part, shard_rows),
            fixed(4, part),
            vector(part),
            fixed(part, shard_rows),
            fixed(shard_rows, ff),
            fixed(ff, shard_rows),
        ]
        + [vector(width)] * 7,
        compiler_params=pltpu.CompilerParams(
            vmem_limit_bytes=VMEM_LIMIT, dimension_semantics=("arbitrary",)
        ),
        name="deliver",
    )(ing.reshape(nc, local_len, width), hid.reshape(nc, local_len, width), dw, small)
    return (
        hidden_out,
        in_grad,
        qw.swapaxes(1, 2),
        kvw.swapaxes(1, 2),
        qb,
        vb,
        ow,
        ob,
        gain1,
        bias1,
        uw,
        ub,
        dn,
        db,
        gain2,
        bias2,
    )


def solution(mesh):
    in_specs = (
        P("shard", "ctx", None),
        P("shard", "ctx"),
        P("shard", "ctx"),
        P(None, "shard", "tp"),
        P(None, "shard", "tp"),
        P(None, "tp"),
        P("tp"),
        P("tp", "shard"),
        P(),
        P(),
        P(),
        P("shard", "tp"),
        P("tp"),
        P("tp", "shard"),
        P(),
        P(),
        P(),
        P("shard", "ctx", None),
    )
    out_specs = (
        P("shard", "ctx", None),
        P("shard", "ctx", None),
        P(None, "shard", "tp"),
        P(None, "shard", "tp"),
        P(None, "tp"),
        P("tp"),
        P("tp", "shard"),
        P(),
        P(),
        P(),
        P("shard", "tp"),
        P("tp"),
        P("tp", "shard"),
        P(),
        P(),
        P(),
    )
    return jax.shard_map(
        per_device, mesh=mesh, in_specs=in_specs, out_specs=out_specs, check_vma=False
    )
```
